256 devices in a mesh: px: 32 (over z, y), py: 8 (over x, core).
Axes of the slice: x: 4, y: 4, z: 8, core: 2. Of those that a mesh axis runs over, the one named last changes fastest.
Arguments:
- residual: float32 [32, 512, 1024], P(None, 'px', 'py'), may hold values from -6 to 6
- factor_fine: bfloat16 [256, 8, 520, 256], P('px', 'py'), may hold values from -0.25 to 0.25
- factor_one: bfloat16 [128, 4, 520, 256], P('px'), may hold values from -0.25 to 0.25
- factor_two: bfloat16 [64, 2, 520, 256], P('px'), may hold values from -0.25 to 0.25
- factor_three: bfloat16 [32, 1, 520, 256], P('px'), may hold values from -0.25 to 0.25
- factor_four: bfloat16 [16, 1, 264, 128], replicated, may hold values from -0.375 to 0.375
- coarse_inverse: bfloat16 [512, 512], replicated, may hold values from -0.25 to 0.25
Outputs:
- preconditioned: float32 [32, 512, 1024], P(None, 'px', 'py')
The draws below stay inside these ranges and needn't reach their ends.
All inputs are finite; a program needn't handle non-finite values.
Results may differ from the reference program's by a relative error of at most 0.0029.
Values sent between devices are 32-bit elements; how exact they have to be, the bound alone decides.
A program may use at most 128 MiB of HBM per device.

```python
import math
import jax
import jax.numpy as jnp
from jax import lax

RHS = 32
CY = 128
NX = 512
NY = 1024
NX1 = 256
NY1 = 512
NX2 = 128
NY2 = 256
NX3 = 64
NY3 = 128
NX4 = 32
NY4 = 64
NX5 = 16
NY5 = 32
TW1 = 128
TW2 = 128
TW3 = 128
TW4 = 64
N_PY = 8


def steps_of(own_key, dims, split, low, top_value):
    level, own = 1.0, jax.random.fold_in(own_key, 6)
    for axis_at, blocks in split:
        steps = jnp.exp(jax.random.uniform(jax.random.fold_in(own, axis_at), (blocks,), jnp.float32, low / len(split), top_value / len(split)))
        level = level * jnp.repeat(steps, dims[axis_at] // blocks).reshape([-1 if axis == axis_at else 1 for axis in range(len(dims))])
    return level


def centred(key, dims, scale, most, pieces=(), kind=jnp.bfloat16):
    drawn = jax.random.normal(key, dims, jnp.float32) * scale
    if len(pieces) > 0:
        drawn = steps_of(key, dims, pieces, -0.22, 0.18) * drawn
    return jnp.clip(drawn, min=-most, max=most).astype(kind)


def setup_inputs(seed: int = 0) -> dict:
    arg_keys = jax.random.split(jax.random.key(seed), 8)
    return {
        "residual": centred(arg_keys[0], (RHS, NX, NY), 1.0, 6.0, ((1, 32), (2, 8)), jnp.float32),
        "factor_fine": centred(arg_keys[1], (NX // 2, N_PY, 4 * (CY + 2), 2 * CY), (4 * (CY + 2)) ** -0.5, 0.25, ((0, 32), (1, 8))),
        "factor_one": centred(arg_keys[2], (NX1 // 2, NY1 // TW1, 4 * (TW1 + 2), 2 * TW1), (4 * (TW1 + 2)) ** -0.5, 0.25, ((0, 32),)),
        "factor_two": centred(arg_keys[3], (NX2 // 2, NY2 // TW2, 4 * (TW2 + 2), 2 * TW2), (4 * (TW2 + 2)) ** -0.5, 0.25, ((0, 32),)),
        "factor_three": centred(arg_keys[4], (NX3 // 2, NY3 // TW3, 4 * (TW3 + 2), 2 * TW3), (4 * (TW3 + 2)) ** -0.5, 0.25, ((0, 32),)),
        "factor_four": centred(arg_keys[5], (NX4 // 2, NY4 // TW4, 4 * (TW4 + 2), 2 * TW4), (4 * (TW4 + 2)) ** -0.5, 0.375),
        "coarse_inverse": centred(arg_keys[6], (NX5 * NY5, NX5 * NY5), (NX5 * NY5) ** -0.5, 0.25),
    }


tap_scale = 1.0 / math.sqrt(20.0)

def shrink(padded, dimension):
    length = padded.shape[dimension] - 2
    before = padded.shape[:dimension]
    after = padded.shape[dimension + 1:]
    lower = lax.slice_in_dim(padded, 0, length, axis=dimension).reshape(before + (length // 2, 2) + after)
    upper = lax.slice_in_dim(padded, 2, length + 2, axis=dimension).reshape(before + (length // 2, 2) + after)
    outer_low = lax.index_in_dim(lower, 0, dimension + 1, keepdims=False)
    inner_low = lax.index_in_dim(lower, 1, dimension + 1, keepdims=False)
    inner_high = lax.index_in_dim(upper, 0, dimension + 1, keepdims=False)
    outer_high = lax.index_in_dim(upper, 1, dimension + 1, keepdims=False)
    return tap_scale * (outer_low + 3.0 * inner_low + 3.0 * inner_high + outer_high)

def prolong(padded, dimension):
    length = padded.shape[dimension] - 2
    left = lax.slice_in_dim(padded, 0, length, axis=dimension)
    centre = lax.slice_in_dim(padded, 1, length + 1, axis=dimension)
    right = lax.slice_in_dim(padded, 2, length + 2, axis=dimension)
    even_cells = tap_scale * (3.0 * centre + left)
    odd_cells = tap_scale * (3.0 * centre + right)
    stacked = jnp.stack([even_cells, odd_cells], axis=dimension + 1)
    target = list(centre.shape)
    target[dimension] = 2 * length
    return stacked.reshape(tuple(target))

def pad_both(field):
    return jnp.pad(field, ((0, 0), (1, 1), (1, 1)))

def restrict_both(padded):
    return shrink(shrink(padded, 1), 2)

def prolong_both(padded):
    return prolong(prolong(padded, 1), 2)

def make_windows(padded, width):
    systems, height, breadth = padded.shape
    inner_rows = height - 2
    inner_cols = breadth - 2
    tiles = inner_cols // width
    pairs = inner_rows // 2
    top = padded[:, :inner_rows].reshape(systems, pairs, 2, breadth)
    bottom = padded[:, 2:].reshape(systems, pairs, 2, breadth)
    strips = jnp.concatenate([top, bottom], axis=2)
    main = strips[..., :inner_cols].reshape(systems, pairs, 4, tiles, width)
    extra = jnp.pad(strips[..., width:], ((0, 0), (0, 0), (0, 0), (0, width - 2)))
    extra = extra.reshape(systems, pairs, 4, tiles, width)[..., :2]
    windows = jnp.concatenate([main, extra], axis=4).transpose(0, 1, 3, 2, 4)
    return windows.reshape(systems, pairs, tiles, 4 * (width + 2)).astype(jnp.bfloat16)

def solve_blocks(padded, factor):
    width = factor.shape[3] // 2
    systems, height, breadth = padded.shape
    windows = make_windows(padded, width)
    pairs = windows.shape[1]
    tiles = windows.shape[2]
    solved = jnp.einsum('rbqe,bqeo->rbqo', windows.astype(jnp.float32), factor.astype(jnp.float32), precision=lax.Precision.HIGHEST)
    solved = solved.reshape(systems, pairs, tiles, 2, width).transpose(0, 1, 3, 2, 4)
    return solved.reshape(systems, height - 2, breadth - 2)

def reference(residual, factor_fine, factor_one, factor_two, factor_three, factor_four, coarse_inverse):
    factors = [factor_fine, factor_one, factor_two, factor_three, factor_four]
    parts = []
    level_now = residual
    for level in range(5):
        padded = pad_both(level_now)
        parts.append(solve_blocks(padded, factors[level]))
        level_now = restrict_both(padded)
    systems, rows_five, cols_five = level_now.shape
    flat = level_now.reshape(systems, rows_five * cols_five).astype(jnp.bfloat16)
    correction = jnp.dot(flat, coarse_inverse, preferred_element_type=jnp.float32).reshape(systems, rows_five, cols_five)
    for level in range(4, 0, -1):
        correction = parts[level] + prolong_both(pad_both(correction))
    return parts[0] + prolong_both(pad_both(correction))
```

```python
import functools

import jax
import jax.numpy as jnp
import numpy as np
from jax import lax
from jax.experimental import pallas as pl
from jax.experimental.pallas import tpu as pltpu
from jax.sharding import PartitionSpec as P

F32 = jnp.float32
BF = jnp.bfloat16
MESH = pl.DeviceIdType.MESH
LANES_FOUR = (6, 16, 38)
ROWS_TWO = ((0, 1, 2), (4, 5, 3))
GROUP_OF = (0, 1, 2, 2, 3, 3, 3, 3, 3)


def composites(count):
    found, now = [], np.eye(count)
    for _ in range(5):
        fine = now.shape[0]
        step = np.zeros((fine // 2, fine))
        for i in range(fine // 2):
            for shift, tap in ((-1, 1), (0, 3), (1, 3), (2, 1)):
                if 0 <= 2 * i + shift < fine:
                    step[i, 2 * i + shift] = tap
        now = step @ now
        found.append(now)
    return found


def pick(matrix, row, low, count):
    if 0 <= row < matrix.shape[0]:
        return matrix[row, low : low + count]
    return np.zeros(count)


def edge_lanes(row):
    slot, first, count = ((0, 0, 2), (1, 2, 3), (3, 5, 3), (2, 8, 2))[(row >= 2) + (row >= 5) + (row >= 8)]
    base = 32 * slot + 18 + 2 * (row - first)
    return base, base + 2 * count


def down_rows(rows, px):
    z, low = px // 4, 16 * px
    a1, a2, a3, a4, a5 = (m / 20.0 ** (i + 1) for i, m in enumerate(rows))
    w = np.zeros((9, 16, 128))
    for s in range(4):
        w[0, :, 32 * s : 32 * s + 6] = pick(a5, 2 * z - 1 + s, low, 16)[:, None]
        w[1, :, 32 * s : 32 * s + 18] = pick(a3, 2 * px - 1 + s, low, 16)[:, None]
    for m, at in enumerate(LANES_FOUR):
        for h in range(2):
            w[0, :, at + 64 * h : at + 64 * h + 10] = pick(a4, 4 * z - 1 + 2 * m + h, low, 16)[:, None]
    for e in range(16):
        w[0, e // 2, 48 + e] = 1.0
        w[0, 8 + e // 2, 112 + e] = 1.0
    for r in range(10):
        for at in edge_lanes(r):
            w[1, :, at : at + 2] = pick(a1, 8 * px - 1 + r, low, 16)[:, None]
    for half in range(2):
        for u in range(3):
            w[2 + half, :, 42 * u : 42 * u + 34] = pick(a2, 4 * px - 1 + ROWS_TWO[half][u], low, 16)[:, None]
    for m in range(5):
        for h in range(2):
            w[4 + m, :, 64 * h : 64 * h + 64] = pick(a1, 8 * px - 1 + 2 * m + h, low, 16)[:, None]
    return w


def down_columns(columns, py):
    b1, b2, b3, b4, b5 = columns
    low = 128 * py
    b = np.zeros((128, 512))
    for s in range(4):
        for c in range(6):
            b[:, 32 * s + c] = pick(b5, 4 * py - 1 + c, low, 128)
        for c in range(18):
            b[:, 128 + 32 * s + c] = pick(b3, 16 * py - 1 + c, low, 128)
    for at in LANES_FOUR:
        for c in range(10):
            b[:, at + c] = b[:, at + 64 + c] = pick(b4, 8 * py - 1 + c, low, 128)
    for e in range(16):
        b[0 if e % 2 else 127, 48 + e] = 1.0
        b[0 if e % 2 else 127, 112 + e] = 1.0
    for r in range(10):
        p, q = edge_lanes(r)
        for at, col in ((p, -1), (p + 1, 0), (q, 63), (q + 1, 64)):
            b[:, 128 + at] = pick(b1, 64 * py + col, low, 128)
    for u in range(3):
        for c in range(34):
            b[:, 256 + 42 * u + c] = pick(b2, 32 * py - 1 + c, low, 128)
    for c in range(64):
        b[:, 384 + c] = b[:, 448 + c] = pick(b1, 64 * py + c, low, 128)
    return b


def up_columns(columns, py):
    b1, b2, b3, b4, b5 = columns
    low, tile, core = 128 * py, 128 * (py // 2), py % 2
    one = np.stack([pick(b1, tile + c, low, 128) for c in range(128)])
    if core == 0:
        one[127] = pick(b1, tile - 1, low, 128)
    else:
        one[0] = pick(b1, tile + 128, low, 128)
    two = np.stack([pick(b2, c, low, 128) for c in range(256)])
    three = np.stack([pick(b3, c, low, 128) for c in range(128)])
    four = np.stack([pick(b4, c % 64, low, 128) for c in range(128)])
    five = np.stack([pick(b5, c % 32, low, 128) for c in range(128)])
    return one, two, three, four, five


def up_rows(rows, px):
    z, low = px // 4, 16 * px
    w = np.zeros((32, 16))
    firsts = ((0, 10, 8 * px - 1), (10, 6, 4 * px - 1), (16, 4, 2 * px - 1), (20, 8, 4 * z - 2), (28, 4, 2 * z - 1))
    for level, (at, count, first) in enumerate(firsts):
        for i in range(count):
            w[at + i] = pick(rows[level], first + i, low, 16) / 20.0 ** (level + 1)
    return w


def split(matrix):
    high = matrix.astype(BF)
    return high, (matrix - high.astype(np.float64)).astype(BF)


@functools.cache
def tables():
    rows, columns = composites(512), composites(1024)
    some = (12, 13, 14, 15, 0, 31)
    down_w = np.stack([down_rows(rows, px) for px in some])
    up_w = np.stack([up_rows(rows, px) for px in some])
    down_b, down_b5 = [], []
    for py in (0, 3, 7):
        high, low = split(down_columns(columns, py))
        down_b.append(high)
        down_b5.append(low[:, :128])
    up = []
    for py in range(8):
        one, two, three, four, five = up_columns(columns, py)
        high, low = split(five)
        up.append(np.concatenate([m.astype(BF) for m in (one, two, three, four)] + [high, low]))
    return (
        down_w.astype(np.float32),
        np.pad(up_w.reshape(6, 4, 128), ((0, 0), (0, 4), (0, 0))).astype(np.float32),
        np.stack(down_b),
        np.stack(down_b5),
        np.stack(up),
    )


def kernel(
    down_used, up_used,
    res_hbm, ff_hbm, f1_hbm, f2_hbm, f3_hbm, f4_hbm, ci_hbm, dw_hbm, uw_hbm, db_hbm, db5_hbm, up_hbm,
    out_ref,
    res, ff, f1, f2, f3, f4, ci, dw, uw, db, db5, up,
    xt, yy, own, sb, pb, xa, xb, xm, yb5, yb4, zb5, f4own, zb4, hs, hb, cs, cb, p0, p5, acc,
    lsem, asend, arecv, bsend, brecv, csend, crecv, msend, mrecv, y5send, y5recv, y4send, y4recv,
    z5send, z5recv, z4send, z4recv, hsend, hrecv, esend, erecv,
):
    px, py = lax.axis_index("px"), lax.axis_index("py")
    z, y = px // 4, px % 4
    x, core = py // 2, py % 2
    has_left, has_right = px > 0, px < 31
    beside = jnp.where(core == 0, py - 1, py + 1)
    has_beside = jnp.logical_and(beside >= 0, beside < 8)
    beside = jnp.clip(beside, 0, 7)
    variant = jnp.where(px == 0, 4, jnp.where(px == 31, 5, y))
    place = jnp.where(py == 0, 0, jnp.where(py == 7, 2, 1))
    lane = lax.broadcasted_iota(jnp.int32, (32, 128), 1)

    def roll(tile, shift):
        if isinstance(shift, int):
            shift %= 128
            return tile if shift == 0 else pltpu.roll(tile, shift, 1)
        return pltpu.roll(tile, shift, 1)

    def only(mask, tile):
        return jnp.where(mask, tile, 0.0)

    local = [
        (res_hbm, res),
        (db_hbm.at[place], db.at[pl.ds(0, 128)]),
        (db_hbm.at[place], db.at[pl.ds(128, 128)]),
        (db5_hbm.at[place], db5),
        (dw_hbm.at[variant], dw),
        (uw_hbm.at[variant], uw),
        (up_hbm.at[py], up),
        (f3_hbm.at[0, 0], f3),
        (f2_hbm, f2),
        (ci_hbm, ci),
        (ff_hbm, ff),
    ]
    local += [(f1_hbm.at[b, x], f1.at[b]) for b in range(4)]
    local += [(f4_hbm.at[jnp.clip(2 * z - 1 + b, 0, 15), 0], f4.at[b]) for b in range(4)]
    local = [pltpu.make_async_copy(s, d, lsem.at[i]) for i, (s, d) in enumerate(local)]
    for copy in local:
        copy.start()

    barrier = pltpu.get_barrier_semaphore()

    def greet(**where):
        pl.semaphore_signal(barrier, inc=1, device_id=where, device_id_type=MESH)

    for d in range(1, 8):
        greet(px=px, py=(py + d) % 8)
        greet(px=((z + d) % 8) * 4 + y, py=py)
    for d in range(1, 4):
        greet(px=z * 4 + (y + d) % 4, py=py)

    @pl.when(has_left)
    def _():
        greet(px=px - 1, py=py)

    @pl.when(has_right)
    def _():
        greet(px=px + 1, py=py)

    @pl.when(jnp.logical_and(has_left, has_beside))
    def _():
        greet(px=px - 1, py=beside)

    @pl.when(jnp.logical_and(has_right, has_beside))
    def _():
        greet(px=px + 1, py=beside)

    def send(src, dst, ssem, rsem, **where):
        return pltpu.make_async_remote_copy(
            src_ref=src, dst_ref=dst, send_sem=ssem, recv_sem=rsem, device_id=where, device_id_type=MESH
        )

    nothing = jnp.zeros((32, 128), F32)

    def clear(ref, *lead):
        ref[lead] = nothing

    for end in (0, 9):
        clear(xa, end)
        clear(zb5, end)
        for i in range(3):
            clear(xb, end, i)

    @pl.when(px == 0)
    def _():
        for i in range(4):
            clear(pb, 0, i)
        for i in range(3):
            clear(hb, 0, i)

    @pl.when(px == 31)
    def _():
        for i in range(4):
            clear(pb, 1, i)
        for i in range(3):
            clear(hb, 1, i)

    @pl.when(z == 0)
    def _():
        for i in range(3):
            clear(zb4, 0, i)

    @pl.when(z == 7)
    def _():
        for i in range(3):
            clear(zb4, 1, i)

    diag = (
        jnp.logical_and(has_beside, has_left),
        has_beside,
        jnp.logical_and(has_beside, has_right),
    )
    for i in range(3):

        @pl.when(jnp.logical_not(diag[i]))
        def _(i=i):
            clear(cb, i)

    local[0].wait()
    for f in range(16):
        xt[f] = res[pl.ds(f, 32, stride=16), :]
    rows = xt[...].reshape(512, 128)
    high = rows.astype(BF)
    low = (rows - high.astype(F32)).astype(BF)
    both = jnp.concatenate([high, low], axis=1)
    for i in range(1, 5):
        local[i].wait()
    yy[:, :256] = jnp.dot(both, db[:, :256], preferred_element_type=F32)
    yy[:, :128] += jnp.dot(high, db5[...], preferred_element_type=F32)

    def packed(t):
        at = 128 * GROUP_OF[t]
        total = None
        for f in range(16):
            if down_used[t][f]:
                term = yy[32 * f : 32 * f + 32, at : at + 128] * dw[t, f : f + 1, :]
                total = term if total is None else total + term
        return total

    xa[py + 1] = packed(0)
    pl.semaphore_wait(
        barrier,
        17 + jnp.where(has_left, 1, 0) + jnp.where(has_right, 1, 0) + jnp.where(diag[0], 1, 0) + jnp.where(diag[2], 1, 0),
    )

    def to_py(buffer, ssem, rsem, d, slot):
        return send(buffer.at[slot + 1], buffer.at[slot + 1], ssem.at[d - 1], rsem.at[slot], px=px, py=(py + d) % 8)

    sent = []
    for d in (4, 3, 5, 2, 6, 1, 7):
        copy = to_py(xa, asend, arecv, d, py)
        copy.start()
        sent.append(copy)

    yy[:, 256:] = jnp.dot(both, db[:, 256:], preferred_element_type=F32)
    for t in range(1, 9):
        own[t - 1] = packed(t)
    sb[0, 0] = own[0]
    sb[1, 0] = own[0]
    sb[0, 1] = own[1]
    sb[1, 1] = own[2]
    sb[0, 2] = own[3]
    sb[1, 2] = own[7]
    sb[0, 3] = xt[0]
    sb[1, 3] = xt[15]

    def to_left(src, dst, ssem, rsem):
        return send(src.at[0], dst.at[1], ssem.at[0], rsem.at[1], px=px - 1, py=py)

    def to_right(src, dst, ssem, rsem):
        return send(src.at[1], dst.at[0], ssem.at[1], rsem.at[0], px=px + 1, py=py)

    def start_rows(*refs):
        @pl.when(has_left)
        def _():
            to_left(*refs).start()

        @pl.when(has_right)
        def _():
            to_right(*refs).start()

    def got_rows(src, dst, ssem, rsem):
        @pl.when(has_left)
        def _():
            send(src.at[1], dst.at[0], ssem.at[1], rsem.at[0], px=px - 1, py=py).wait_recv()

        @pl.when(has_right)
        def _():
            send(src.at[0], dst.at[1], ssem.at[0], rsem.at[1], px=px + 1, py=py).wait_recv()

    def sent_rows(*refs):
        @pl.when(has_left)
        def _():
            to_left(*refs).wait_send()

        @pl.when(has_right)
        def _():
            to_right(*refs).wait_send()

    start_rows(sb, pb, bsend, brecv)

    for d in range(1, 8):
        to_py(xa, asend, arecv, d, (py + 8 - d) % 8).wait_recv()
    five = None
    fours = [None] * 3
    for p in range(8):
        tile = xa[p + 1]
        term = only(((lane - 4 * p + 1) & 31) < 6, roll(tile, 4 * p - 1))
        five = term if five is None else five + term
        near = ((lane - 8 * p + 1) & 63) < 10
        for m in range(3):
            term = only(near, roll(tile, 8 * p - 1 - LANES_FOUR[m]))
            fours[m] = term if fours[m] is None else fours[m] + term
    yb5[y] = five
    for m in range(3):
        yb4[y, m] = fours[m]

    def to_y(buffer, ssem, rsem, d, slot):
        return send(buffer.at[slot], buffer.at[slot], ssem.at[d - 1], rsem.at[slot], px=z * 4 + (y + d) % 4, py=py)

    for d in (2, 1, 3):
        copy = to_y(yb5, y5send, y5recv, d, y)
        copy.start()
        sent.append(copy)
    for d in (2, 1, 3):
        copy = to_y(yb4, y4send, y4recv, d, y)
        copy.start()
        sent.append(copy)

    got_rows(sb, pb, bsend, brecv)
    mine = own[0]
    across = jnp.where(lane < 64, roll(pb[0, 0], 64), roll(pb[1, 0], 64))
    inside = jnp.logical_or((lane & 63) < 50, (lane & 63) > 61)
    mine = mine + only(inside, across)
    corner = jnp.where(lane < 28, roll(pb[0, 3], 27), roll(pb[1, 3], 29))
    mine = jnp.where(jnp.logical_and(lane >= 26, lane < 30), corner, mine)
    xb[py + 1, 0] = mine
    xb[py + 1, 1] = own[1] + only(lane < 84, pb[0, 1])
    xb[py + 1, 2] = own[2] + only(lane < 84, pb[1, 1])
    xm[core, 0] = own[3] + pb[0, 2]
    for m in range(1, 4):
        xm[core, m] = own[3 + m]
    xm[core, 4] = own[7] + pb[1, 2]

    def to_partner(slot):
        return send(xm.at[slot], xm.at[slot], msend, mrecv, px=px, py=2 * x + 1 - core)

    to_partner(core).start()
    sent.append(to_partner(core))
    for d in (4, 3, 5, 2, 6, 1, 7):
        copy = to_py(xb, csend, crecv, d, py)
        copy.start()
        sent.append(copy)

    for d in range(1, 4):
        to_y(yb5, y5send, y5recv, d, (y + 4 - d) % 4).wait_recv()
    zb5[z + 1] = (yb5[0] + yb5[1]) + (yb5[2] + yb5[3])

    def to_z(d, slot):
        return send(zb5.at[slot + 1], zb5.at[slot + 1], z5send.at[d - 1], z5recv.at[slot], px=((z + d) % 8) * 4 + y, py=py)

    for d in (4, 3, 5, 2, 6, 1, 7):
        copy = to_z(d, z)
        copy.start()
        sent.append(copy)
    for d in range(1, 4):
        to_y(yb4, y4send, y4recv, d, (y + 4 - d) % 4).wait_recv()
    for m in range(3):
        f4own[m] = (yb4[0, m] + yb4[1, m]) + (yb4[2, m] + yb4[3, m])

    def z4_down():
        return send(f4own, zb4.at[1], z4send.at[0], z4recv.at[1], px=px - 4, py=py)

    def z4_up():
        return send(f4own, zb4.at[0], z4send.at[1], z4recv.at[0], px=px + 4, py=py)

    @pl.when(z > 0)
    def _():
        z4_down().start()

    @pl.when(z < 7)
    def _():
        z4_up().start()

    def solve(windows, factor):
        return jnp.dot(windows.astype(BF), factor, preferred_element_type=F32)

    def window(shifted, halo):
        parts = [jnp.where(lane == 0, halo(0), shifted[0])]
        for j in range(1, 4):
            parts.append(jnp.where(lane <= 2 * j - 2, shifted[j - 1], jnp.where(lane <= 2 * j, halo(j), shifted[j])))
        last = jnp.where(lane <= 6, shifted[3], halo(4))
        return jnp.concatenate(parts + [last[:, :8]], axis=1)

    def lifted(tiles, table):
        count = 32 * len(tiles)
        fine = jnp.concatenate(tiles, axis=0)
        top = fine.astype(BF)
        rest = (fine - top.astype(F32)).astype(BF)
        product = jnp.dot(jnp.concatenate([top, rest], axis=0), table, preferred_element_type=F32)
        product = product[:count] + product[count:]
        return [product[32 * i : 32 * i + 32] for i in range(len(tiles))]

    for d in range(1, 8):
        to_py(xb, csend, crecv, d, (py + 8 - d) % 8).wait_recv()
    local[6].wait()
    local[7].wait()
    rows_three = []
    for s in range(4):
        total = None
        for p in range(8):
            near = jnp.logical_and(lane >= 16 * p - 1, lane <= 16 * p + 16)
            term = only(near, roll(xb[p + 1, 0], 16 * p - 1 - 32 * s))
            total = term if total is None else total + term
        rows_three.append(total)
    shifted = [roll(rows_three[k], 2 * k + 1) for k in range(4)]
    solved = solve(window(shifted, lambda j: nothing), f3[...])
    three = lifted([solved[:, :128], solved[:, 128:]], up[384:512, :])
    hs[0, 2] = three[0]
    hs[1, 2] = three[1]

    rows_two = []
    for r in range(6):
        half, u = next((h, ROWS_TWO[h].index(r)) for h in range(2) if r in ROWS_TWO[h])
        pair = [None, None]
        for p in range(8):
            turned = roll(xb[p + 1, 1 + half], 32 * p - 1 - 42 * u)
            first = 32 * (p % 4) - 1
            near = jnp.logical_and(lane >= first, lane <= first + 33)
            term = only(near, turned)
            pair[p // 4] = term if pair[p // 4] is None else pair[p // 4] + term
            if p == 3:
                pair[1] = only(lane == 0, turned)
            if p == 4:
                pair[0] = pair[0] + only(lane == 127, turned)
        rows_two.append(pair)
    local[8].wait()
    two = []
    for b in range(2):
        turned = [[roll(rows_two[2 * b + k][t], 2 * k + 1) for k in range(4)] for t in range(2)]

        def right_of(j, turned=turned):
            return only(lane == 2 * j - 1, turned[1][j - 1]) if j > 0 else nothing

        def left_of(j, turned=turned):
            return only(lane == 2 * j, turned[0][j]) if j < 4 else nothing

        left_tile = solve(window(turned[0], right_of), f2[b, 0])
        right_tile = solve(window(turned[1], left_of), f2[b, 1])
        for h in range(2):
            at = slice(128 * h, 128 * h + 128)
            two.append((left_tile[:, at], right_tile[:, at]))
    part = lifted([pair[0] for pair in two], up[128:256, :])
    other = lifted([pair[1] for pair in two], up[256:384, :])
    two = [a + b for a, b in zip(part, other)]
    hs[0, 1] = two[0]
    hs[1, 1] = two[3]

    to_partner(1 - core).wait_recv()
    left_edge, first_edge, second_edge, right_edge = (xb[2 * x + i, 0] for i in range(4))
    even = (lane & 1) == 0

    def edges(n):
        mid = jnp.where(even, second_edge, roll(first_edge, -n))
        outer = jnp.where(even, right_edge, roll(left_edge, -n))
        halo = jnp.where(even, first_edge + roll(left_edge, -n), right_edge + roll(second_edge, -n))
        return mid, outer, halo

    edges_of = {2: edges(4), 3: edges(6)}
    rows_one = []
    for r in range(10):
        m, h = divmod(r, 2)
        if h == 0:
            main = jnp.where(lane < 64, xm[0, m], roll(xm[1, m], 64))
        else:
            main = jnp.where(lane < 64, roll(xm[0, m], 64), xm[1, m])
        at, last = edge_lanes(r)
        mid, outer, _ = edges_of[(last - at) // 2]
        main = main + only(jnp.logical_or(lane == 63, lane == 64), roll(mid, 63 - at))
        main = main + only(jnp.logical_or(lane == 127, lane == 0), roll(outer, 127 - at))
        rows_one.append(main)
    halo_two, halo_three = edges_of[2][2], edges_of[3][2]
    halos = jnp.where(
        lane < 4,
        roll(halo_two, -18),
        jnp.where(lane < 10, roll(halo_three, -46), jnp.where(lane < 16, roll(halo_three, -104), roll(halo_two, -66))),
    )
    one = []
    for b in range(4):
        local[11 + b].wait()
        turned = [roll(rows_one[2 * b + k], 2 * k + 1) for k in range(4)]
        side = roll(halos, -4 * b)
        solved = solve(window(turned, lambda j, side=side: side), f1[b])
        one += [solved[:, :128], solved[:, 128:]]
    hs[0, 0] = one[0]
    hs[1, 0] = one[7]
    start_rows(hs, hb, hsend, hrecv)
    column = nothing
    for r in range(8):
        column = jnp.where(lane == r, roll(one[r], r + core), column)
    cs[...] = column

    def to_side(d):
        return send(cs, cb.at[1 - d], esend.at[1 - d], erecv.at[1 - d], px=px + d, py=beside)

    for d in (-1, 1, 0):

        @pl.when(diag[1 + d])
        def _(d=d):
            to_side(d).start()

    before, after = xa[py], xa[py + 2]
    corner_before, corner_after = xb[py, 0], xb[py + 2, 0]
    facing = jnp.where(even, before, after)
    corners = jnp.where(even, corner_before, corner_after)
    halos = jnp.where(
        lane < 2,
        roll(corners, -26),
        jnp.where(lane < 18, roll(facing, -46), jnp.where(lane < 34, roll(facing, -94), roll(corners, 6))),
    )
    local[10].wait()
    for b in range(8):
        tiles = []
        for k in range(4):
            at = 2 * b + k
            tile = pb[0, 3] if at == 0 else pb[1, 3] if at == 17 else xt[at - 1]
            tiles.append(roll(tile, 2 * k + 1))
        side = roll(halos, -4 * b)
        solved = solve(window(tiles, lambda j, side=side: side), ff[b, 0])
        p0[2 * b] = solved[:, :128]
        p0[2 * b + 1] = solved[:, 128:]

    @pl.when(z > 0)
    def _():
        send(f4own, zb4.at[0], z4send.at[1], z4recv.at[0], px=px - 4, py=py).wait_recv()

    @pl.when(z < 7)
    def _():
        send(f4own, zb4.at[1], z4send.at[0], z4recv.at[1], px=px + 4, py=py).wait_recv()

    quads = (zb4[0, 1], zb4[0, 2] + f4own[0], f4own[1], f4own[2] + zb4[1, 0], zb4[1, 1])
    fours = []
    for b in range(4):
        local[15 + b].wait()
        first, second = quads[b], quads[b + 1]
        v0 = jnp.where(
            lane <= 64,
            only(lane >= 1, roll(first, 1)),
            only(lane >= 67, roll(first, 3)),
        )
        v1 = jnp.where(
            lane <= 2,
            roll(first, 3),
            jnp.where(lane <= 68, only(lane >= 5, roll(second, 5)), only(lane >= 71, roll(second, 7))),
        )
        v2 = only(lane <= 6, roll(second, 7))
        solved = solve(jnp.concatenate([v0, v1, v2[:, :8]], axis=1), f4[b])
        fours += [only(lane < 64, solved), only(lane >= 64, solved)]
    four = lifted(fours, up[512:640, :])

    got_rows(hs, hb, hsend, hrecv)
    for d in (-1, 0, 1):

        @pl.when(diag[1 + d])
        def _(d=d):
            send(cs, cb.at[1 + d], esend.at[1 + d], erecv.at[1 + d], px=px + d, py=beside).wait_recv()

    one = [hb[0, 0]] + one + [hb[1, 0]]
    at_lane = 127 * (1 - core)
    for r in range(10):
        source, from_lane = (0, 7) if r == 0 else (2, 0) if r == 9 else (1, r - 1)
        one[r] = jnp.where(lane == at_lane, roll(cb[source], (at_lane - from_lane + 128) % 128), one[r])
    one = lifted(one, up[0:128, :])
    two = [hb[0, 1]] + two + [hb[1, 1]]
    three = [hb[0, 2]] + three + [hb[1, 2]]
    local[5].wait()
    terms = one + two + three + four
    for f in range(16):
        total = p0[f]
        for r in range(28):
            if up_used[r][f]:
                total = total + uw[r // 8, 16 * (r % 8) + f] * terms[r]
        acc[f] = total

    for d in range(1, 8):
        to_z(d, (z + 8 - d) % 8).wait_recv()
    local[9].wait()
    down = [roll(zb5[i + 1], -32) if i < 8 else nothing for i in range(0, 10, 2)]
    rise = [nothing] + [roll(zb5[i + 1], 32) for i in range(1, 8, 2)]
    flat = [
        jnp.where(lane < 96, down[j], down[j + 1]) + jnp.where(lane >= 32, rise[j + 1], rise[j]) for j in range(4)
    ]
    solved = solve(jnp.concatenate(flat, axis=1), ci[...])
    clear(p5, 0)
    clear(p5, 5)
    for j in range(4):
        p5[j + 1] = solved[:, 128 * j : 128 * j + 128]
    odd = z % 2
    lead = (z + odd) // 2
    edge = 32 + 64 * odd
    five = jnp.where(lane < edge, roll(p5[lead], edge), roll(p5[lead + 1], edge))
    fives = [only((lane // 32) == s, five) for s in range(4)]
    full = jnp.concatenate(fives, axis=0)
    top = full.astype(BF)
    rest = (full - top.astype(F32)).astype(BF)
    product = jnp.dot(jnp.concatenate([top, rest], axis=0), up[640:768, :], preferred_element_type=F32)
    product = product[:128] + product[128:] + jnp.dot(top, up[768:896, :], preferred_element_type=F32)
    for f in range(16):
        total = acc[f]
        for s in range(4):
            if up_used[28 + s][f]:
                total = total + uw[3, 16 * (4 + s) + f] * product[32 * s : 32 * s + 32]
        out_ref[pl.ds(f, 32, stride=16), :] = total

    for copy in sent:
        copy.wait_send()
    sent_rows(sb, pb, bsend, brecv)
    sent_rows(hs, hb, hsend, hrecv)

    @pl.when(z > 0)
    def _():
        z4_down().wait_send()

    @pl.when(z < 7)
    def _():
        z4_up().wait_send()

    for d in (-1, 0, 1):

        @pl.when(diag[1 + d])
        def _(d=d):
            to_side(d).wait_send()


def per_device(residual, fine, one, two, three, four, inverse):
    down_w, up_w, down_b, down_b5, up = tables()
    down_used = (down_w != 0).any(axis=(0, 3)).tolist()
    up_used = (up_w[:, :4] != 0).any(axis=0).reshape(32, 16).tolist()
    tile = (32, 128)

    def tiles(*lead):
        return pltpu.VMEM(lead + tile, F32)

    dma = pltpu.SemaphoreType.DMA
    out = pl.pallas_call(
        functools.partial(kernel, down_used, up_used),
        out_shape=jax.ShapeDtypeStruct((512, 128), F32),
        in_specs=[pl.BlockSpec(memory_space=pltpu.HBM)] * 12,
        out_specs=pl.BlockSpec(memory_space=pltpu.VMEM),
        scratch_shapes=[
            pltpu.VMEM((512, 128), F32),
            pltpu.VMEM((8, 1, 520, 256), BF),
            pltpu.VMEM((4, 520, 256), BF),
            pltpu.VMEM((2, 2, 520, 256), BF),
            pltpu.VMEM((520, 256), BF),
            pltpu.VMEM((4, 264, 128), BF),
            pltpu.VMEM((512, 512), BF),
            pltpu.VMEM((9, 16, 128), F32),
            pltpu.SMEM((8, 128), F32),
            pltpu.VMEM((256, 512), BF),
            pltpu.VMEM((128, 128), BF),
            pltpu.VMEM((896, 128), BF),
            tiles(16),
            pltpu.VMEM((512, 512), F32),
            tiles(8),
            tiles(2, 4),
            tiles(2, 4),
            tiles(10),
            tiles(10, 3),
            tiles(2, 5),
            tiles(4),
            tiles(4, 3),
            tiles(10),
            tiles(3),
            tiles(2, 3),
            tiles(2, 3),
            tiles(2, 3),
            tiles(),
            tiles(3),
            tiles(16),
            tiles(6),
            tiles(16),
            dma((19,)),
            dma((7,)),
            dma((8,)),
            dma((2,)),
            dma((2,)),
            dma((7,)),
            dma((8,)),
            dma,
            dma,
            dma((3,)),
            dma((4,)),
            dma((3,)),
            dma((4,)),
            dma((7,)),
            dma((8,)),
            dma((2,)),
            dma((2,)),
            dma((2,)),
            dma((2,)),
            dma((3,)),
            dma((3,)),
        ],
        compiler_params=pltpu.CompilerParams(collective_id=0, has_side_effects=True, vmem_limit_bytes=48 << 20),
    )(
        residual.reshape(512, 128), fine, one, two, three, four, inverse,
        jnp.asarray(down_w), jnp.asarray(up_w), jnp.asarray(down_b), jnp.asarray(down_b5), jnp.asarray(up),
    )
    return out.reshape(32, 16, 128)


def solution(mesh):
    placed = (
        P(None, "px", "py"),
        P("px", "py", None, None),
        P("px", None, None, None),
        P("px", None, None, None),
        P("px", None, None, None),
        P(),
        P(),
    )
    return jax.shard_map(
        per_device, mesh=mesh, in_specs=placed, out_specs=P(None, "px", "py"), check_vma=False
    )
```

```python
import functools

import jax
import jax.numpy as jnp
import numpy as np
from jax import lax
from jax.experimental import pallas as pl
from jax.experimental.pallas import tpu as pltpu
from jax.sharding import PartitionSpec as P

F32 = jnp.float32
BF = jnp.bfloat16
MESH = pl.DeviceIdType.MESH
LANES_FOUR = (6, 16, 38)
ROWS_TWO = ((0, 1, 2), (4, 5, 3))
GROUP_OF = (0, 1, 2, 2, 3, 3, 3, 3, 3)


def composites(count):
    found, now = [], np.eye(count)
    for _ in range(5):
        fine = now.shape[0]
        step = np.zeros((fine // 2, fine))
        for i in range(fine // 2):
            for shift, tap in ((-1, 1), (0, 3), (1, 3), (2, 1)):
                if 0 <= 2 * i + shift < fine:
                    step[i, 2 * i + shift] = tap
        now = step @ now
        found.append(now)
    return found


def pick(matrix, row, low, count):
    if 0 <= row < matrix.shape[0]:
        return matrix[row, low : low + count]
    return np.zeros(count)


def edge_lanes(row):
    slot, first, count = ((0, 0, 2), (1, 2, 3), (3, 5, 3), (2, 8, 2))[(row >= 2) + (row >= 5) + (row >= 8)]
    base = 32 * slot + 18 + 2 * (row - first)
    return base, base + 2 * count


def down_rows(rows, px):
    z, low = px // 4, 16 * px
    a1, a2, a3, a4, a5 = (m / 20.0 ** (i + 1) for i, m in enumerate(rows))
    w = np.zeros((9, 16, 128))
    for s in range(4):
        w[0, :, 32 * s : 32 * s + 6] = pick(a5, 2 * z - 1 + s, low, 16)[:, None]
        w[1, :, 32 * s : 32 * s + 18] = pick(a3, 2 * px - 1 + s, low, 16)[:, None]
    for m, at in enumerate(LANES_FOUR):
        for h in range(2):
            w[0, :, at + 64 * h : at + 64 * h + 10] = pick(a4, 4 * z - 1 + 2 * m + h, low, 16)[:, None]
    for e in range(16):
        w[0, e // 2, 48 + e] = 1.0
        w[0, 8 + e // 2, 112 + e] = 1.0
    for r in range(10):
        for at in edge_lanes(r):
            w[1, :, at : at + 2] = pick(a1, 8 * px - 1 + r, low, 16)[:, None]
    for half in range(2):
        for u in range(3):
            w[2 + half, :, 42 * u : 42 * u + 34] = pick(a2, 4 * px - 1 + ROWS_TWO[half][u], low, 16)[:, None]
    for m in range(5):
        for h in range(2):
            w[4 + m, :, 64 * h : 64 * h + 64] = pick(a1, 8 * px - 1 + 2 * m + h, low, 16)[:, None]
    return w


def down_columns(columns, py):
    b1, b2, b3, b4, b5 = columns
    low = 128 * py
    b = np.zeros((128, 512))
    for s in range(4):
        for c in range(6):
            b[:, 32 * s + c] = pick(b5, 4 * py - 1 + c, low, 128)
        for c in range(18):
            b[:, 128 + 32 * s + c] = pick(b3, 16 * py - 1 + c, low, 128)
    for at in LANES_FOUR:
        for c in range(10):
            b[:, at + c] = b[:, at + 64 + c] = pick(b4, 8 * py - 1 + c, low, 128)
    for e in range(16):
        b[0 if e % 2 else 127, 48 + e] = 1.0
        b[0 if e % 2 else 127, 112 + e] = 1.0
    for r in range(10):
        p, q = edge_lanes(r)
        for at, col in ((p, -1), (p + 1, 0), (q, 63), (q + 1, 64)):
            b[:, 128 + at] = pick(b1, 64 * py + col, low, 128)
    for u in range(3):
        for c in range(34):
            b[:, 256 + 42 * u + c] = pick(b2, 32 * py - 1 + c, low, 128)
    for c in range(64):
        b[:, 384 + c] = b[:, 448 + c] = pick(b1, 64 * py + c, low, 128)
    return b


def up_columns(columns, py):
    b1, b2, b3, b4, b5 = columns
    low, tile, core = 128 * py, 128 * (py // 2), py % 2
    one = np.stack([pick(b1, tile + c, low, 128) for c in range(128)])
    if core == 0:
        one[127] = pick(b1, tile - 1, low, 128)
    else:
        one[0] = pick(b1, tile + 128, low, 128)
    two = np.stack([pick(b2, c, low, 128) for c in range(256)])
    three = np.stack([pick(b3, c, low, 128) for c in range(128)])
    four = np.stack([pick(b4, c % 64, low, 128) for c in range(128)])
    five = np.stack([pick(b5, c % 32, low, 128) for c in range(128)])
    return one, two, three, four, five


def up_rows(rows, px):
    z, low = px // 4, 16 * px
    w = np.zeros((32, 16))
    firsts = ((0, 10, 8 * px - 1), (10, 6, 4 * px - 1), (16, 4, 2 * px - 1), (20, 8, 4 * z - 2), (28, 4, 2 * z - 1))
    for level, (at, count, first) in enumerate(firsts):
        for i in range(count):
            w[at + i] = pick(rows[level], first + i, low, 16) / 20.0 ** (level + 1)
    return w


def split(matrix):
    high = matrix.astype(BF)
    return high, (matrix - high.astype(np.float64)).astype(BF)


@functools.cache
def tables():
    rows, columns = composites(512), composites(1024)
    some = (12, 13, 14, 15, 0, 31)
    down_w = np.stack([down_rows(rows, px) for px in some])
    up_w = np.stack([up_rows(rows, px) for px in some])
    down_b, down_b5 = [], []
    for py in (0, 3, 7):
        high, low = split(down_columns(columns, py))
        down_b.append(high)
        down_b5.append(low[:, :128])
    up = []
    for py in range(8):
        one, two, three, four, five = up_columns(columns, py)
        high, low = split(five)
        up.append(np.concatenate([m.astype(BF) for m in (one, two, three, four)] + [high, low]))
    return (
        down_w.astype(np.float32),
        np.pad(up_w.reshape(6, 4, 128), ((0, 0), (0, 4), (0, 0))).astype(np.float32),
        np.stack(down_b),
        np.stack(down_b5),
        np.stack(up),
    )


def kernel(
    down_used, up_used,
    res_hbm, ff_hbm, f1_hbm, f2_hbm, f3_hbm, f4_hbm, ci_hbm, dw_hbm, uw_hbm, db_hbm, db5_hbm, up_hbm,
    out_ref,
    res, ff, f1, f2, f3, f4, ci, dw, uw, db, db5, up,
    xt, yy, own, sb, pb, xa, xb, xm, yb5, yb4, zb5, f4own, zb4, hs, hb, cs, cb, p0, p5, acc,
    lsem, asend, arecv, bsend, brecv, csend, crecv, msend, mrecv, y5send, y5recv, y4send, y4recv,
    z5send, z5recv, z4send, z4recv, hsend, hrecv, esend, erecv,
):
    px, py = lax.axis_index("px"), lax.axis_index("py")
    z, y = px // 4, px % 4
    x, core = py // 2, py % 2
    has_left, has_right = px > 0, px < 31
    beside = jnp.where(core == 0, py - 1, py + 1)
    has_beside = jnp.logical_and(beside >= 0, beside < 8)
    beside = jnp.clip(beside, 0, 7)
    variant = jnp.where(px == 0, 4, jnp.where(px == 31, 5, y))
    place = jnp.where(py == 0, 0, jnp.where(py == 7, 2, 1))
    lane = lax.broadcasted_iota(jnp.int32, (32, 128), 1)

    def roll(tile, shift):
        if isinstance(shift, int):
            shift %= 128
            return tile if shift == 0 else pltpu.roll(tile, shift, 1)
        return pltpu.roll(tile, shift, 1)

    def only(mask, tile):
        return jnp.where(mask, tile, 0.0)

    local = [
        (res_hbm, res),
        (db_hbm.at[place], db.at[pl.ds(0, 128)]),
        (db_hbm.at[place], db.at[pl.ds(128, 128)]),
        (db5_hbm.at[place], db5),
        (dw_hbm.at[variant], dw),
        (uw_hbm.at[variant], uw),
        (up_hbm.at[py], up),
        (f3_hbm.at[0, 0], f3),
        (f2_hbm, f2),
        (ci_hbm, ci),
        (ff_hbm, ff),
    ]
    local += [(f1_hbm.at[b, x], f1.at[b]) for b in range(4)]
    local += [(f4_hbm.at[jnp.clip(2 * z - 1 + b, 0, 15), 0], f4.at[b]) for b in range(4)]
    local = [pltpu.make_async_copy(s, d, lsem.at[i]) for i, (s, d) in enumerate(local)]
    for copy in local:
        copy.start()

    barrier = pltpu.get_barrier_semaphore()

    def greet(**where):
        pl.semaphore_signal(barrier, inc=1, device_id=where, device_id_type=MESH)

    for d in range(1, 8):
        greet(px=px, py=(py + d) % 8)
        greet(px=((z + d) % 8) * 4 + y, py=py)
    for d in range(1, 4):
        greet(px=z * 4 + (y + d) % 4, py=py)

    @pl.when(has_left)
    def _():
        greet(px=px - 1, py=py)

    @pl.when(has_right)
    def _():
        greet(px=px + 1, py=py)

    @pl.when(jnp.logical_and(has_left, has_beside))
    def _():
        greet(px=px - 1, py=beside)

    @pl.when(jnp.logical_and(has_right, has_beside))
    def _():
        greet(px=px + 1, py=beside)

    def send(src, dst, ssem, rsem, **where):
        return pltpu.make_async_remote_copy(
            src_ref=src, dst_ref=dst, send_sem=ssem, recv_sem=rsem, device_id=where, device_id_type=MESH
        )

    nothing = jnp.zeros((32, 128), F32)

    def clear(ref, *lead):
        ref[lead] = nothing

    for end in (0, 9):
        clear(xa, end)
        clear(zb5, end)
        for i in range(3):
            clear(xb, end, i)

    @pl.when(px == 0)
    def _():
        for i in range(4):
            clear(pb, 0, i)
        for i in range(3):
            clear(hb, 0, i)

    @pl.when(px == 31)
    def _():
        for i in range(4):
            clear(pb, 1, i)
        for i in range(3):
            clear(hb, 1, i)

    @pl.when(z == 0)
    def _():
        for i in range(3):
            clear(zb4, 0, i)

    @pl.when(z == 7)
    def _():
        for i in range(3):
            clear(zb4, 1, i)

    diag = (
        jnp.logical_and(has_beside, has_left),
        has_beside,
        jnp.logical_and(has_beside, has_right),
    )
    for i in range(3):

        @pl.when(jnp.logical_not(diag[i]))
        def _(i=i):
            clear(cb, i)

    local[0].wait()
    for f in range(16):
        xt[f] = res[pl.ds(f, 32, stride=16), :]
    rows = xt[...].reshape(512, 128)
    high = rows.astype(BF)
    low = (rows - high.astype(F32)).astype(BF)
    both = jnp.concatenate([high, low], axis=1)
    for i in range(1, 5):
        local[i].wait()
    yy[:, :256] = jnp.dot(both, db[:, :256], preferred_element_type=F32)
    yy[:, :128] += jnp.dot(high, db5[...], preferred_element_type=F32)

    def packed(t):
        at = 128 * GROUP_OF[t]
        total = None
        for f in range(16):
            if down_used[t][f]:
                term = yy[32 * f : 32 * f + 32, at : at + 128] * dw[t, f : f + 1, :]
                total = term if total is None else total + term
        return total

    xa[py + 1] = packed(0)
    pl.semaphore_wait(
        barrier,
        17 + jnp.where(has_left, 1, 0) + jnp.where(has_right, 1, 0) + jnp.where(diag[0], 1, 0) + jnp.where(diag[2], 1, 0),
    )

    def to_py(buffer, ssem, rsem, d, slot):
        return send(buffer.at[slot + 1], buffer.at[slot + 1], ssem.at[d - 1], rsem.at[slot], px=px, py=(py + d) % 8)

    sent = []
    for d in (4, 3, 5, 2, 6, 1, 7):
        copy = to_py(xa, asend, arecv, d, py)
        copy.start()
        sent.append(copy)

    yy[:, 256:] = jnp.dot(both, db[:, 256:], preferred_element_type=F32)
    for t in range(1, 9):
        own[t - 1] = packed(t)
    sb[0, 0] = own[0]
    sb[1, 0] = own[0]
    sb[0, 1] = own[1]
    sb[1, 1] = own[2]
    sb[0, 2] = own[3]
    sb[1, 2] = own[7]
    sb[0, 3] = xt[0]
    sb[1, 3] = xt[15]

    def to_left(src, dst, ssem, rsem):
        return send(src.at[0], dst.at[1], ssem.at[0], rsem.at[1], px=px - 1, py=py)

    def to_right(src, dst, ssem, rsem):
        return send(src.at[1], dst.at[0], ssem.at[1], rsem.at[0], px=px + 1, py=py)

    def start_rows(*refs):
        @pl.when(has_left)
        def _():
            to_left(*refs).start()

        @pl.when(has_right)
        def _():
            to_right(*refs).start()

    def got_rows(src, dst, ssem, rsem):
        @pl.when(has_left)
        def _():
            send(src.at[1], dst.at[0], ssem.at[1], rsem.at[0], px=px - 1, py=py).wait_recv()

        @pl.when(has_right)
        def _():
            send(src.at[0], dst.at[1], ssem.at[0], rsem.at[1], px=px + 1, py=py).wait_recv()

    def sent_rows(*refs):
        @pl.when(has_left)
        def _():
            to_left(*refs).wait_send()

        @pl.when(has_right)
        def _():
            to_right(*refs).wait_send()

    start_rows(sb, pb, bsend, brecv)

    for d in range(1, 8):
        to_py(xa, asend, arecv, d, (py + 8 - d) % 8).wait_recv()
    five = None
    fours = [None] * 3
    for p in range(8):
        tile = xa[p + 1]
        term = only(((lane - 4 * p + 1) & 31) < 6, roll(tile, 4 * p - 1))
        five = term if five is None else five + term
        near = ((lane - 8 * p + 1) & 63) < 10
        for m in range(3):
            term = only(near, roll(tile, 8 * p - 1 - LANES_FOUR[m]))
            fours[m] = term if fours[m] is None else fours[m] + term
    yb5[y] = five
    for m in range(3):
        yb4[y, m] = fours[m]

    def to_y(buffer, ssem, rsem, d, slot):
        return send(buffer.at[slot], buffer.at[slot], ssem.at[d - 1], rsem.at[slot], px=z * 4 + (y + d) % 4, py=py)

    for d in (2, 1, 3):
        copy = to_y(yb5, y5send, y5recv, d, y)
        copy.start()
        sent.append(copy)
    for d in (2, 1, 3):
        copy = to_y(yb4, y4send, y4recv, d, y)
        copy.start()
        sent.append(copy)

    got_rows(sb, pb, bsend, brecv)
    mine = own[0]
    across = jnp.where(lane < 64, roll(pb[0, 0], 64), roll(pb[1, 0], 64))
    inside = jnp.logical_or((lane & 63) < 50, (lane & 63) > 61)
    mine = mine + only(inside, across)
    corner = jnp.where(lane < 28, roll(pb[0, 3], 27), roll(pb[1, 3], 29))
    mine = jnp.where(jnp.logical_and(lane >= 26, lane < 30), corner, mine)
    xb[py + 1, 0] = mine
    xb[py + 1, 1] = own[1] + only(lane < 84, pb[0, 1])
    xb[py + 1, 2] = own[2] + only(lane < 84, pb[1, 1])
    xm[core, 0] = own[3] + pb[0, 2]
    for m in range(1, 4):
        xm[core, m] = own[3 + m]
    xm[core, 4] = own[7] + pb[1, 2]

    def to_partner(slot):
        return send(xm.at[slot], xm.at[slot], msend, mrecv, px=px, py=2 * x + 1 - core)

    to_partner(core).start()
    sent.append(to_partner(core))
    for d in (4, 3, 5, 2, 6, 1, 7):
        copy = to_py(xb, csend, crecv, d, py)
        copy.start()
        sent.append(copy)

    for d in range(1, 4):
        to_y(yb5, y5send, y5recv, d, (y + 4 - d) % 4).wait_recv()
    zb5[z + 1] = (yb5[0] + yb5[1]) + (yb5[2] + yb5[3])

    def to_z(d, slot):
        return send(zb5.at[slot + 1], zb5.at[slot + 1], z5send.at[d - 1], z5recv.at[slot], px=((z + d) % 8) * 4 + y, py=py)

    for d in (4, 3, 5, 2, 6, 1, 7):
        copy = to_z(d, z)
        copy.start()
        sent.append(copy)
    for d in range(1, 4):
        to_y(yb4, y4send, y4recv, d, (y + 4 - d) % 4).wait_recv()
    for m in range(3):
        f4own[m] = (yb4[0, m] + yb4[1, m]) + (yb4[2, m] + yb4[3, m])

    def z4_down():
        return send(f4own, zb4.at[1], z4send.at[0], z4recv.at[1], px=px - 4, py=py)

    def z4_up():
        return send(f4own, zb4.at[0], z4send.at[1], z4recv.at[0], px=px + 4, py=py)

    @pl.when(z > 0)
    def _():
        z4_down().start()

    @pl.when(z < 7)
    def _():
        z4_up().start()

    def solve(windows, factor):
        return jnp.dot(windows.astype(BF), factor, preferred_element_type=F32)

    def window(shifted, halo):
        parts = [jnp.where(lane == 0, halo(0), shifted[0])]
        for j in range(1, 4):
            parts.append(jnp.where(lane <= 2 * j - 2, shifted[j - 1], jnp.where(lane <= 2 * j, halo(j), shifted[j])))
        last = jnp.where(lane <= 6, shifted[3], halo(4))
        return jnp.concatenate(parts + [last[:, :8]], axis=1)

    def lifted(tiles, table):
        count = 32 * len(tiles)
        fine = jnp.concatenate(tiles, axis=0)
        top = fine.astype(BF)
        rest = (fine - top.astype(F32)).astype(BF)
        product = jnp.dot(jnp.concatenate([top, rest], axis=0), table, preferred_element_type=F32)
        product = product[:count] + product[count:]
        return [product[32 * i : 32 * i + 32] for i in range(len(tiles))]

    for d in range(1, 8):
        to_py(xb, csend, crecv, d, (py + 8 - d) % 8).wait_recv()
    local[6].wait()
    local[7].wait()
    rows_three = []
    for s in range(4):
        total = None
        for p in range(8):
            near = jnp.logical_and(lane >= 16 * p - 1, lane <= 16 * p + 16)
            term = only(near, roll(xb[p + 1, 0], 16 * p - 1 - 32 * s))
            total = term if total is None else total + term
        rows_three.append(total)
    shifted = [roll(rows_three[k], 2 * k + 1) for k in range(4)]
    solved = solve(window(shifted, lambda j: nothing), f3[...])
    three = lifted([solved[:, :128], solved[:, 128:]], up[384:512, :])
    hs[0, 2] = three[0]
    hs[1, 2] = three[1]

    rows_two = []
    for r in range(6):
        half, u = next((h, ROWS_TWO[h].index(r)) for h in range(2) if r in ROWS_TWO[h])
        pair = [None, None]
        for p in range(8):
            turned = roll(xb[p + 1, 1 + half], 32 * p - 1 - 42 * u)
            first = 32 * (p % 4) - 1
            near = jnp.logical_and(lane >= first, lane <= first + 33)
            term = only(near, turned)
            pair[p // 4] = term if pair[p // 4] is None else pair[p // 4] + term
            if p == 3:
                pair[1] = only(lane == 0, turned)
            if p == 4:
                pair[0] = pair[0] + only(lane == 127, turned)
        rows_two.append(pair)
    local[8].wait()
    two = []
    for b in range(2):
        turned = [[roll(rows_two[2 * b + k][t], 2 * k + 1) for k in range(4)] for t in range(2)]

        def right_of(j, turned=turned):
            return only(lane == 2 * j - 1, turned[1][j - 1]) if j > 0 else nothing

        def left_of(j, turned=turned):
            return only(lane == 2 * j, turned[0][j]) if j < 4 else nothing

        left_tile = solve(window(turned[0], right_of), f2[b, 0])
        right_tile = solve(window(turned[1], left_of), f2[b, 1])
        for h in range(2):
            at = slice(128 * h, 128 * h + 128)
            two.append((left_tile[:, at], right_tile[:, at]))
    part = lifted([pair[0] for pair in two], up[128:256, :])
    other = lifted([pair[1] for pair in two], up[256:384, :])
    two = [a + b for a, b in zip(part, other)]
    hs[0, 1] = two[0]
    hs[1, 1] = two[3]

    to_partner(1 - core).wait_recv()
    left_edge, first_edge, second_edge, right_edge = (xb[2 * x + i, 0] for i in range(4))
    even = (lane & 1) == 0

    def edges(n):
        mid = jnp.where(even, second_edge, roll(first_edge, -n))
        outer = jnp.where(even, right_edge, roll(left_edge, -n))
        halo = jnp.where(even, first_edge + roll(left_edge, -n), right_edge + roll(second_edge, -n))
        return mid, outer, halo

    edges_of = {2: edges(4), 3: edges(6)}
    rows_one = []
    for r in range(10):
        m, h = divmod(r, 2)
        if h == 0:
            main = jnp.where(lane < 64, xm[0, m], roll(xm[1, m], 64))
        else:
            main = jnp.where(lane < 64, roll(xm[0, m], 64), xm[1, m])
        at, last = edge_lanes(r)
        mid, outer, _ = edges_of[(last - at) // 2]
        main = main + only(jnp.logical_or(lane == 63, lane == 64), roll(mid, 63 - at))
        main = main + only(jnp.logical_or(lane == 127, lane == 0), roll(outer, 127 - at))
        rows_one.append(main)
    halo_two, halo_three = edges_of[2][2], edges_of[3][2]
    halos = jnp.where(
        lane < 4,
        roll(halo_two, -18),
        jnp.where(lane < 10, roll(halo_three, -46), jnp.where(lane < 16, roll(halo_three, -104), roll(halo_two, -66))),
    )
    one = []
    for b in range(4):
        local[11 + b].wait()
        turned = [roll(rows_one[2 * b + k], 2 * k + 1) for k in range(4)]
        side = roll(halos, -4 * b)
        solved = solve(window(turned, lambda j, side=side: side), f1[b])
        one += [solved[:, :128], solved[:, 128:]]
    hs[0, 0] = one[0]
    hs[1, 0] = one[7]
    start_rows(hs, hb, hsend, hrecv)
    column = nothing
    for r in range(8):
        column = jnp.where(lane == r, roll(one[r], r + core), column)
    cs[...] = column

    def to_side(d):
        return send(cs, cb.at[1 - d], esend.at[1 - d], erecv.at[1 - d], px=px + d, py=beside)

    for d in (-1, 1, 0):

        @pl.when(diag[1 + d])
        def _(d=d):
            to_side(d).start()

    before, after = xa[py], xa[py + 2]
    corner_before, corner_after = xb[py, 0], xb[py + 2, 0]
    facing = jnp.where(even, before, after)
    corners = jnp.where(even, corner_before, corner_after)
    halos = jnp.where(
        lane < 2,
        roll(corners, -26),
        jnp.where(lane < 18, roll(facing, -46), jnp.where(lane < 34, roll(facing, -94), roll(corners, 6))),
    )
    local[10].wait()
    for b in range(8):
        tiles = []
        for k in range(4):
            at = 2 * b + k
            tile = pb[0, 3] if at == 0 else pb[1, 3] if at == 17 else xt[at - 1]
            tiles.append(roll(tile, 2 * k + 1))
        side = roll(halos, -4 * b)
        solved = solve(window(tiles, lambda j, side=side: side), ff[b, 0])
        p0[2 * b] = solved[:, :128]
        p0[2 * b + 1] = solved[:, 128:]

    @pl.when(z > 0)
    def _():
        send(f4own, zb4.at[0], z4send.at[1], z4recv.at[0], px=px - 4, py=py).wait_recv()

    @pl.when(z < 7)
    def _():
        send(f4own, zb4.at[1], z4send.at[0], z4recv.at[1], px=px + 4, py=py).wait_recv()

    quads = (zb4[0, 1], zb4[0, 2] + f4own[0], f4own[1], f4own[2] + zb4[1, 0], zb4[1, 1])
    fours = []
    for b in range(4):
        local[15 + b].wait()
        first, second = quads[b], quads[b + 1]
        v0 = jnp.where(
            lane <= 64,
            only(lane >= 1, roll(first, 1)),
            only(lane >= 67, roll(first, 3)),
        )
        v1 = jnp.where(
            lane <= 2,
            roll(first, 3),
            jnp.where(lane <= 68, only(lane >= 5, roll(second, 5)), only(lane >= 71, roll(second, 7))),
        )
        v2 = only(lane <= 6, roll(second, 7))
        solved = solve(jnp.concatenate([v0, v1, v2[:, :8]], axis=1), f4[b])
        fours += [only(lane < 64, solved), only(lane >= 64, solved)]
    four = lifted(fours, up[512:640, :])

    got_rows(hs, hb, hsend, hrecv)
    for d in (-1, 0, 1):

        @pl.when(diag[1 + d])
        def _(d=d):
            send(cs, cb.at[1 + d], esend.at[1 + d], erecv.at[1 + d], px=px + d, py=beside).wait_recv()

    one = [hb[0, 0]] + one + [hb[1, 0]]
    at_lane = 127 * (1 - core)
    for r in range(10):
        source, from_lane = (0, 7) if r == 0 else (2, 0) if r == 9 else (1, r - 1)
        one[r] = jnp.where(lane == at_lane, roll(cb[source], (at_lane - from_lane + 128) % 128), one[r])
    one = lifted(one, up[0:128, :])
    two = [hb[0, 1]] + two + [hb[1, 1]]
    three = [hb[0, 2]] + three + [hb[1, 2]]
    local[5].wait()
    terms = one + two + three + four
    for f in range(16):
        total = p0[f]
        for r in range(28):
            if up_used[r][f]:
                total = total + uw[r // 8, 16 * (r % 8) + f] * terms[r]
        acc[f] = total

    for d in range(1, 8):
        to_z(d, (z + 8 - d) % 8).wait_recv()
    local[9].wait()
    down = [roll(zb5[i + 1], -32) if i < 8 else nothing for i in range(0, 10, 2)]
    rise = [nothing] + [roll(zb5[i + 1], 32) for i in range(1, 8, 2)]
    flat = [
        jnp.where(lane < 96, down[j], down[j + 1]) + jnp.where(lane >= 32, rise[j + 1], rise[j]) for j in range(4)
    ]
    solved = solve(jnp.concatenate(flat, axis=1), ci[...])
    clear(p5, 0)
    clear(p5, 5)
    for j in range(4):
        p5[j + 1] = solved[:, 128 * j : 128 * j + 128]
    odd = z % 2
    lead = (z + odd) // 2
    edge = 32 + 64 * odd
    five = jnp.where(lane < edge, roll(p5[lead], edge), roll(p5[lead + 1], edge))
    fives = [only((lane // 32) == s, five) for s in range(4)]
    full = jnp.concatenate(fives, axis=0)
    top = full.astype(BF)
    rest = (full - top.astype(F32)).astype(BF)
    product = jnp.dot(jnp.concatenate([top, rest], axis=0), up[640:768, :], preferred_element_type=F32)
    product = product[:128] + product[128:] + jnp.dot(top, up[768:896, :], preferred_element_type=F32)
    for f in range(16):
        total = acc[f]
        for s in range(4):
            if up_used[28 + s][f]:
                total = total + uw[3, 16 * (4 + s) + f] * product[32 * s : 32 * s + 32]
        out_ref[pl.ds(f, 32, stride=16), :] = total

    for copy in sent:
        copy.wait_send()
    sent_rows(sb, pb, bsend, brecv)
    sent_rows(hs, hb, hsend, hrecv)

    @pl.when(z > 0)
    def _():
        z4_down().wait_send()

    @pl.when(z < 7)
    def _():
        z4_up().wait_send()

    for d in (-1, 0, 1):

        @pl.when(diag[1 + d])
        def _(d=d):
            to_side(d).wait_send()


def per_device(residual, fine, one, two, three, four, inverse):
    down_w, up_w, down_b, down_b5, up = tables()
    down_used = (down_w != 0).any(axis=(0, 3)).tolist()
    up_used = (up_w[:, :4] != 0).any(axis=0).reshape(32, 16).tolist()
    tile = (32, 128)

    def tiles(*lead):
        return pltpu.VMEM(lead + tile, F32)

    dma = pltpu.SemaphoreType.DMA
    out = pl.pallas_call(
        functools.partial(kernel, down_used, up_used),
        out_shape=jax.ShapeDtypeStruct((512, 128), F32),
        in_specs=[pl.BlockSpec(memory_space=pltpu.HBM)] * 12,
        out_specs=pl.BlockSpec(memory_space=pltpu.VMEM),
        scratch_shapes=[
            pltpu.VMEM((512, 128), F32),
            pltpu.VMEM((8, 1, 520, 256), BF),
            pltpu.VMEM((4, 520, 256), BF),
            pltpu.VMEM((2, 2, 520, 256), BF),
            pltpu.VMEM((520, 256), BF),
            pltpu.VMEM((4, 264, 128), BF),
            pltpu.VMEM((512, 512), BF),
            pltpu.VMEM((9, 16, 128), F32),
            pltpu.SMEM((8, 128), F32),
            pltpu.VMEM((256, 512), BF),
            pltpu.VMEM((128, 128), BF),
            pltpu.VMEM((896, 128), BF),
            tiles(16),
            pltpu.VMEM((512, 512), F32),
            tiles(8),
            tiles(2, 4),
            tiles(2, 4),
            tiles(10),
            tiles(10, 3),
            tiles(2, 5),
            tiles(4),
            tiles(4, 3),
            tiles(10),
            tiles(3),
            tiles(2, 3),
            tiles(2, 3),
            tiles(2, 3),
            tiles(),
            tiles(3),
            tiles(16),
            tiles(6),
            tiles(16),
            dma((19,)),
            dma((7,)),
            dma((8,)),
            dma((2,)),
            dma((2,)),
            dma((7,)),
            dma((8,)),
            dma,
            dma,
            dma((3,)),
            dma((4,)),
            dma((3,)),
            dma((4,)),
            dma((7,)),
            dma((8,)),
            dma((2,)),
            dma((2,)),
            dma((2,)),
            dma((2,)),
            dma((3,)),
            dma((3,)),
        ],
        compiler_params=pltpu.CompilerParams(collective_id=0, has_side_effects=True, vmem_limit_bytes=67043328),
    )(
        residual.reshape(512, 128), fine, one, two, three, four, inverse,
        jnp.asarray(down_w), jnp.asarray(up_w), jnp.asarray(down_b), jnp.asarray(down_b5), jnp.asarray(up),
    )
    return out.reshape(32, 16, 128)


def solution(mesh):
    placed = (
        P(None, "px", "py"),
        P("px", "py", None, None),
        P("px", None, None, None),
        P("px", None, None, None),
        P("px", None, None, None),
        P(),
        P(),
    )
    return jax.shard_map(
        per_device, mesh=mesh, in_specs=placed, out_specs=P(None, "px", "py"), check_vma=False
    )
```

```python
import functools

import jax
import jax.numpy as jnp
import numpy as np
from jax import lax
from jax.experimental import pallas as pl
from jax.experimental.pallas import tpu as pltpu
from jax.sharding import PartitionSpec as P

F32 = jnp.float32
BF = jnp.bfloat16
MESH = pl.DeviceIdType.MESH
LANES_FOUR = (6, 16, 38)
ROWS_TWO = ((0, 1, 2), (4, 5, 3))
GROUP_OF = (0, 1, 2, 2, 3, 3, 3, 3, 3)


def composites(count):
    found, now = [], np.eye(count)
    for _ in range(5):
        fine = now.shape[0]
        step = np.zeros((fine // 2, fine))
        for i in range(fine // 2):
            for shift, tap in ((-1, 1), (0, 3), (1, 3), (2, 1)):
                if 0 <= 2 * i + shift < fine:
                    step[i, 2 * i + shift] = tap
        now = step @ now
        found.append(now)
    return found


def pick(matrix, row, low, count):
    if 0 <= row < matrix.shape[0]:
        return matrix[row, low : low + count]
    return np.zeros(count)


def edge_lanes(row):
    slot, first, count = ((0, 0, 2), (1, 2, 3), (3, 5, 3), (2, 8, 2))[(row >= 2) + (row >= 5) + (row >= 8)]
    base = 32 * slot + 18 + 2 * (row - first)
    return base, base + 2 * count


def down_rows(rows, px):
    z, low = px // 4, 16 * px
    a1, a2, a3, a4, a5 = (m / 20.0 ** (i + 1) for i, m in enumerate(rows))
    w = np.zeros((9, 16, 128))
    for s in range(4):
        w[0, :, 32 * s : 32 * s + 6] = pick(a5, 2 * z - 1 + s, low, 16)[:, None]
        w[1, :, 32 * s : 32 * s + 18] = pick(a3, 2 * px - 1 + s, low, 16)[:, None]
    for m, at in enumerate(LANES_FOUR):
        for h in range(2):
            w[0, :, at + 64 * h : at + 64 * h + 10] = pick(a4, 4 * z - 1 + 2 * m + h, low, 16)[:, None]
    for e in range(16):
        w[0, e // 2, 48 + e] = 1.0
        w[0, 8 + e // 2, 112 + e] = 1.0
    for r in range(10):
        for at in edge_lanes(r):
            w[1, :, at : at + 2] = pick(a1, 8 * px - 1 + r, low, 16)[:, None]
    for half in range(2):
        for u in range(3):
            w[2 + half, :, 42 * u : 42 * u + 34] = pick(a2, 4 * px - 1 + ROWS_TWO[half][u], low, 16)[:, None]
    for m in range(5):
        for h in range(2):
            w[4 + m, :, 64 * h : 64 * h + 64] = pick(a1, 8 * px - 1 + 2 * m + h, low, 16)[:, None]
    return w


def down_columns(columns, py):
    b1, b2, b3, b4, b5 = columns
    low = 128 * py
    b = np.zeros((128, 512))
    for s in range(4):
        for c in range(6):
            b[:, 32 * s + c] = pick(b5, 4 * py - 1 + c, low, 128)
        for c in range(18):
            b[:, 128 + 32 * s + c] = pick(b3, 16 * py - 1 + c, low, 128)
    for at in LANES_FOUR:
        for c in range(10):
            b[:, at + c] = b[:, at + 64 + c] = pick(b4, 8 * py - 1 + c, low, 128)
    for e in range(16):
        b[0 if e % 2 else 127, 48 + e] = 1.0
        b[0 if e % 2 else 127, 112 + e] = 1.0
    for r in range(10):
        p, q = edge_lanes(r)
        for at, col in ((p, -1), (p + 1, 0), (q, 63), (q + 1, 64)):
            b[:, 128 + at] = pick(b1, 64 * py + col, low, 128)
    for u in range(3):
        for c in range(34):
            b[:, 256 + 42 * u + c] = pick(b2, 32 * py - 1 + c, low, 128)
    for c in range(64):
        b[:, 384 + c] = b[:, 448 + c] = pick(b1, 64 * py + c, low, 128)
    return b


def up_one(columns, py):
    low, tile = 128 * py, 128 * (py // 2)
    one = np.stack([pick(columns[0], tile + c, low, 128) for c in range(128)])
    if py % 2 == 0:
        one[127] = pick(columns[0], tile - 1, low, 128)
    else:
        one[0] = pick(columns[0], tile + 128, low, 128)
    return one, np.stack([pick(columns[4], c % 32, low, 128) for c in range(128)])


def up_near(columns, py):
    low = 128 * py
    two, three, four = (np.zeros((128, 128)) for _ in range(3))
    for u in range(3):
        for c in range(34):
            two[42 * u + c] = pick(columns[1], 32 * py - 1 + c, low, 128)
    for s in range(4):
        for c in range(18):
            three[32 * s + c] = pick(columns[2], 16 * py - 1 + c, low, 128)
        for c in range(10):
            four[10 * s + c] = four[64 + 10 * s + c] = pick(columns[3], 8 * py - 1 + c, low, 128)
    return np.concatenate([two, three, four])


def up_rows(rows, px):
    z, low = px // 4, 16 * px
    w = np.zeros((32, 16))
    firsts = ((0, 10, 8 * px - 1), (10, 6, 4 * px - 1), (16, 4, 2 * px - 1), (20, 8, 4 * z - 2), (28, 4, 2 * z - 1))
    for level, (at, count, first) in enumerate(firsts):
        for i in range(count):
            w[at + i] = pick(rows[level], first + i, low, 16) / 20.0 ** (level + 1)
    return w


def split(matrix):
    high = matrix.astype(BF)
    return high, (matrix - high.astype(np.float64)).astype(BF)


@functools.cache
def tables():
    rows, columns = composites(512), composites(1024)
    some = (12, 13, 14, 15, 0, 31)
    down_w = np.stack([down_rows(rows, px) for px in some])
    up_w = np.stack([up_rows(rows, px) for px in some])
    down_b, near = [], []
    for py in (0, 3, 7):
        high, low = split(down_columns(columns, py))
        down_b.append(np.concatenate([high, low[:, :128]], axis=1))
        near.append(up_near(columns, py).astype(BF))
    up = []
    for py in range(8):
        one, five = up_one(columns, py)
        high, low = split(five)
        up.append(np.concatenate([one.astype(BF), high, low]))
    weights = [down_w.reshape(6, 144, 128), np.pad(up_w.reshape(6, 4, 128), ((0, 0), (0, 4), (0, 0)))]
    return (
        np.concatenate(weights, axis=1).astype(np.float32),
        np.stack(down_b),
        np.stack(up),
        np.stack(near),
        (down_w != 0).any(axis=(0, 3)).tolist(),
        (up_w != 0).any(axis=0).tolist(),
    )


def kernel(
    down_used, up_used,
    res_hbm, ff_hbm, f1_hbm, f2_hbm, f3_hbm, f4_hbm, ci_hbm, w_hbm, db_hbm, up_hbm, near_hbm,
    out_ref,
    res, ff, f1, f2, f3, f4, ci, dw, uw, db, db5, up, near,
    xt, yy, own, sb, pb, eb, xm, hs, hb, cs, cb, p0, acc,
    abuf, a5, a3, yb5, yb4, zb5, f4own, zb4, gs, gb, hs2, hb2, rs, rb, rb5, p5,
    lsem, a5send, a5recv, a3send, a3recv, bsend, brecv, dsend, drecv, msend, mrecv, y5send, y5recv, y4send, y4recv,
    z5send, z5recv, z4send, z4recv, hsend, hrecv, esend, erecv, gsend, grecv, h2send, h2recv, rsend, rrecv, r5send, r5recv,
):
    px, py = lax.axis_index("px"), lax.axis_index("py")
    z, y = px // 4, px % 4
    x, core = py // 2, py % 2
    has_left, has_right = px > 0, px < 31
    step = 2 * core - 1
    has_beside = jnp.logical_and(py + step >= 0, py + step < 8)
    beside = jnp.clip(py + step, 0, 7)
    beyond = jnp.clip(py + 2 * step, 0, 7)
    has_behind = jnp.logical_and(py - 2 * step >= 0, py - 2 * step < 8)
    behind = jnp.clip(py - 2 * step, 0, 7)
    partner = py + 1 - 2 * core
    variant = jnp.where(px == 0, 4, jnp.where(px == 31, 5, y))
    place = jnp.where(py == 0, 0, jnp.where(py == 7, 2, 1))
    lane = lax.broadcasted_iota(jnp.int32, (32, 128), 1)
    lane8 = lax.broadcasted_iota(jnp.int32, (8, 128), 1)

    def roll(tile, shift):
        if isinstance(shift, int):
            shift %= 128
            return tile if shift == 0 else pltpu.roll(tile, shift, 1)
        return pltpu.roll(tile, shift, 1)

    def only(mask, tile):
        return jnp.where(mask, tile, 0.0)

    barrier = pltpu.get_barrier_semaphore()

    def greet(**where):
        pl.semaphore_signal(barrier, inc=1, device_id=where, device_id_type=MESH)

    for d in (4, 3, 5, 2, 6, 1, 7):
        greet(px=((z + d) % 8) * 4 + y, py=py)

    local = [
        (res_hbm, res),
        (db_hbm.at[place, :, pl.ds(0, 512)], db.at[pl.ds(0, 128)]),
        (db_hbm.at[place, :, pl.ds(0, 512)], db.at[pl.ds(128, 128)]),
        (db_hbm.at[place, :, pl.ds(512, 128)], db5),
        (w_hbm.at[variant, pl.ds(0, 144)], dw),
        (w_hbm.at[variant, pl.ds(144, 8)], uw),
        (up_hbm.at[py], up),
        (f3_hbm.at[0, 0], f3),
        (f2_hbm, f2),
        (ci_hbm, ci),
        (ff_hbm, ff),
        (near_hbm.at[place], near),
    ]
    local += [(f1_hbm.at[b, x], f1.at[b]) for b in range(4)]
    local += [(f4_hbm.at[jnp.clip(2 * z - 1 + b, 0, 15), 0], f4.at[b]) for b in range(4)]
    local = [pltpu.make_async_copy(s, d, lsem.at[i]) for i, (s, d) in enumerate(local)]
    for copy in local[:5]:
        copy.start()

    for d in (4, 3, 5, 2, 6, 1, 7):
        greet(px=px, py=(py + d) % 8)
    for d in range(1, 4):
        greet(px=z * 4 + (y + d) % 4, py=py)
    left_diagonal = jnp.logical_and(has_left, has_beside)
    right_diagonal = jnp.logical_and(has_right, has_beside)

    @pl.when(has_left)
    def _():
        greet(px=px - 1, py=py)

    @pl.when(has_right)
    def _():
        greet(px=px + 1, py=py)

    @pl.when(left_diagonal)
    def _():
        greet(px=px - 1, py=beside)

    @pl.when(right_diagonal)
    def _():
        greet(px=px + 1, py=beside)

    for copy in local[5:]:
        copy.start()

    def send(src, dst, ssem, rsem, **where):
        return pltpu.make_async_remote_copy(
            src_ref=src, dst_ref=dst, send_sem=ssem, recv_sem=rsem, device_id=where, device_id_type=MESH
        )

    nothing = jnp.zeros((32, 128), F32)
    nothing8 = jnp.zeros((8, 128), F32)
    for end in (0, 9):
        zb5[end] = nothing8
        for i in range(2):
            eb[end, i] = nothing

    for side, missing in ((0, px == 0), (1, px == 31)):

        @pl.when(missing)
        def _(side=side):
            for i in range(3):
                pb[side, i] = nothing
                hb2[side, i] = nothing8
            hb[side] = nothing
            for i in range(6):
                gb[side, i] = nothing8

    for side, missing in ((0, z == 0), (1, z == 7)):

        @pl.when(missing)
        def _(side=side):
            for i in range(3):
                zb4[side, i] = nothing8

    diag = (left_diagonal, has_beside, right_diagonal)
    for i in range(3):

        @pl.when(jnp.logical_not(diag[i]))
        def _(i=i):
            cb[i] = nothing

    local[0].wait()
    for f in range(16):
        xt[f] = res[pl.ds(f, 32, stride=16), :]
    rows = xt[...].reshape(512, 128)
    high = rows.astype(BF)
    low = (rows - high.astype(F32)).astype(BF)
    both = jnp.concatenate([high, low], axis=1)
    for i in range(1, 5):
        local[i].wait()
    yy[:, :256] = jnp.dot(both, db[:, :256], preferred_element_type=F32)
    yy[:, :128] += jnp.dot(high, db5[...], preferred_element_type=F32)

    def packed(t):
        at = 128 * GROUP_OF[t]
        total = None
        for f in range(16):
            if down_used[t][f]:
                term = yy[32 * f : 32 * f + 32, at : at + 128] * dw[16 * t + f : 16 * t + f + 1, :]
                total = term if total is None else total + term
        return total

    eb[py + 1, 0] = packed(0)
    a5[py] = eb[py + 1, 0, pl.ds(pl.multiple_of(8 * x, 8), 8), :]
    pl.semaphore_wait(
        barrier,
        17
        + jnp.where(has_left, 1, 0)
        + jnp.where(has_right, 1, 0)
        + jnp.where(left_diagonal, 1, 0)
        + jnp.where(right_diagonal, 1, 0),
    )

    sent = []

    def begin(copy):
        copy.start()
        sent.append(copy)

    FAR = (4, 3, 5, 2, 6, 1, 7)

    def to_five(d, me):
        peer = (me + d) % 8
        group = pl.multiple_of(8 * (peer // 2), 8)
        return send(eb.at[py + 1, 0, pl.ds(group, 8)], a5.at[me], a5send.at[d - 1], a5recv.at[me], px=px, py=peer)

    def to_three(d, me):
        peer = (me + d) % 8
        return send(abuf.at[peer // 2], a3.at[me], a3send.at[d - 1], a3recv.at[me], px=px, py=peer)

    for d in FAR:
        begin(to_five(d, py))

    yy[:, 256:] = jnp.dot(both, db[:, 256:], preferred_element_type=F32)
    for t in range(1, 4):
        tile = packed(t)
        own[t - 1] = tile
        for c in range(4):
            abuf[c, t - 1] = tile[8 * c : 8 * c + 8]
    a3[py] = abuf[x]
    for d in FAR:
        begin(to_three(d, py))
    for t in range(4, 9):
        own[t - 1] = packed(t)
    sb[0, 0] = own[0]
    sb[1, 0] = own[0]
    sb[0, 1] = own[3]
    sb[1, 1] = own[7]
    sb[0, 2] = xt[0]
    sb[1, 2] = xt[15]

    def left_copy(src, dst, ssem, rsem):
        return send(src.at[0], dst.at[1], ssem.at[0], rsem.at[1], px=px - 1, py=py)

    def right_copy(src, dst, ssem, rsem):
        return send(src.at[1], dst.at[0], ssem.at[1], rsem.at[0], px=px + 1, py=py)

    def start_rows(*refs):
        @pl.when(has_left)
        def _():
            left_copy(*refs).start()

        @pl.when(has_right)
        def _():
            right_copy(*refs).start()

    def got_rows(src, dst, ssem, rsem):
        @pl.when(has_left)
        def _():
            send(src.at[1], dst.at[0], ssem.at[1], rsem.at[0], px=px - 1, py=py).wait_recv()

        @pl.when(has_right)
        def _():
            send(src.at[0], dst.at[1], ssem.at[0], rsem.at[1], px=px + 1, py=py).wait_recv()

    def sent_rows(*refs):
        @pl.when(has_left)
        def _():
            left_copy(*refs).wait_send()

        @pl.when(has_right)
        def _():
            right_copy(*refs).wait_send()

    b_refs = (sb, pb, bsend, brecv)
    start_rows(*b_refs)

    for d in range(1, 8):
        to_five(d, (py + 8 - d) % 8).wait_recv()
    five, fours = None, [None] * 3
    for p in range(8):
        tile = a5[p]
        term = only(((lane8 - 4 * p + 1) & 31) < 6, roll(tile, 4 * p - 1))
        five = term if five is None else five + term
        close = ((lane8 - 8 * p + 1) & 63) < 10
        for m in range(3):
            term = only(close, roll(tile, 8 * p - 1 - LANES_FOUR[m]))
            fours[m] = term if fours[m] is None else fours[m] + term
    yb5[y] = five
    for m in range(3):
        yb4[y, m] = fours[m]

    def to_y(buffer, ssem, rsem, d, slot):
        return send(buffer.at[slot], buffer.at[slot], ssem.at[d - 1], rsem.at[slot], px=z * 4 + (y + d) % 4, py=py)

    for d in (2, 1, 3):
        begin(to_y(yb5, y5send, y5recv, d, y))
    for d in (2, 1, 3):
        begin(to_y(yb4, y4send, y4recv, d, y))

    for d in range(1, 8):
        to_three(d, (py + 8 - d) % 8).wait_recv()
    rows_three = []
    for s in range(4):
        total = None
        for p in range(8):
            close = jnp.logical_and(lane8 >= 16 * p - 1, lane8 <= 16 * p + 16)
            term = only(close, roll(a3[p, 0], 16 * p - 1 - 32 * s))
            total = term if total is None else total + term
        rows_three.append(total)
    rows_two = []
    for r in range(6):
        half, u = next((h, ROWS_TWO[h].index(r)) for h in range(2) if r in ROWS_TWO[h])
        pair = [None, None]
        for p in range(8):
            turned = roll(a3[p, 1 + half], 32 * p - 1 - 42 * u)
            first = 32 * (p % 4) - 1
            close = jnp.logical_and(lane8 >= first, lane8 <= first + 33)
            term = only(close, turned)
            pair[p // 4] = term if pair[p // 4] is None else pair[p // 4] + term
            if p == 3:
                pair[1] = only(lane8 == 0, turned)
            if p == 4:
                pair[0] = pair[0] + only(lane8 == 127, turned)
        rows_two.append(pair)
    for side in range(2):
        for i in range(2):
            gs[side, i] = rows_three[2 * side + i]
            for t in range(2):
                gs[side, 2 + 2 * i + t] = rows_two[4 * side + i][t]
    g_refs = (gs, gb, gsend, grecv)
    start_rows(*g_refs)

    got_rows(*b_refs)
    mine = own[0]
    across = jnp.where(lane < 64, roll(pb[0, 0], 64), roll(pb[1, 0], 64))
    inside = jnp.logical_or((lane & 63) < 50, (lane & 63) > 61)
    mine = mine + only(inside, across)
    corner = jnp.where(lane < 28, roll(pb[0, 2], 27), roll(pb[1, 2], 29))
    eb[py + 1, 1] = jnp.where(jnp.logical_and(lane >= 26, lane < 30), corner, mine)
    xm[core, 0] = own[3] + pb[0, 1]
    for m in range(1, 4):
        xm[core, m] = own[3 + m]
    xm[core, 4] = own[7] + pb[1, 1]

    def to_partner(slot):
        return send(xm.at[slot], xm.at[slot], msend, mrecv, px=px, py=partner)

    def edge_copy(i, slot, peer):
        return send(eb.at[slot + 1], eb.at[slot + 1], dsend.at[i], drecv.at[slot], px=px, py=peer)

    @pl.when(has_beside)
    def _():
        edge_copy(0, py, beside).start()
        edge_copy(1, py, beyond).start()

    begin(edge_copy(2, py, partner))
    begin(to_partner(core))

    for d in range(1, 4):
        to_y(yb5, y5send, y5recv, d, (y + 4 - d) % 4).wait_recv()
    zb5[z + 1] = (yb5[0] + yb5[1]) + (yb5[2] + yb5[3])

    def to_z(d, slot):
        return send(zb5.at[slot + 1], zb5.at[slot + 1], z5send.at[d - 1], z5recv.at[slot], px=((z + d) % 8) * 4 + y, py=py)

    for d in FAR:
        begin(to_z(d, z))
    for d in range(1, 4):
        to_y(yb4, y4send, y4recv, d, (y + 4 - d) % 4).wait_recv()
    for m in range(3):
        f4own[m] = (yb4[0, m] + yb4[1, m]) + (yb4[2, m] + yb4[3, m])

    def z4_down():
        return send(f4own, zb4.at[1], z4send.at[0], z4recv.at[1], px=px - 4, py=py)

    def z4_up():
        return send(f4own, zb4.at[0], z4send.at[1], z4recv.at[0], px=px + 4, py=py)

    @pl.when(z > 0)
    def _():
        z4_down().start()

    @pl.when(z < 7)
    def _():
        z4_up().start()

    def solve(windows, factor):
        return jnp.dot(windows.astype(BF), factor, preferred_element_type=F32)

    def window(at, shifted, halo):
        parts = [jnp.where(at == 0, halo(0), shifted[0])]
        for j in range(1, 4):
            parts.append(jnp.where(at <= 2 * j - 2, shifted[j - 1], jnp.where(at <= 2 * j, halo(j), shifted[j])))
        last = jnp.where(at <= 6, shifted[3], halo(4))
        return jnp.concatenate(parts + [last[:, :8]], axis=1)

    def lifted(tiles, table):
        count = 32 * len(tiles)
        fine = jnp.concatenate(tiles, axis=0)
        top = fine.astype(BF)
        rest = (fine - top.astype(F32)).astype(BF)
        product = jnp.dot(jnp.concatenate([top, rest], axis=0), table, preferred_element_type=F32)
        product = product[:count] + product[count:]
        return [product[32 * i : 32 * i + 32] for i in range(len(tiles))]

    got_rows(*g_refs)
    for side in range(2):
        for i in range(2):
            rows_three[2 * side + i] = rows_three[2 * side + i] + gb[side, i]
            rows_two[4 * side + i] = [rows_two[4 * side + i][t] + gb[side, 2 + 2 * i + t] for t in range(2)]
    local[7].wait()
    shifted = [roll(rows_three[k], 2 * k + 1) for k in range(4)]
    solved = solve(window(lane8, shifted, lambda j: nothing8), f3[...])
    three = [solved[:, :128], solved[:, 128:]]
    local[8].wait()
    two = []
    for b in range(2):
        turned = [[roll(rows_two[2 * b + k][t], 2 * k + 1) for k in range(4)] for t in range(2)]

        def right_of(j, turned=turned):
            return only(lane8 == 2 * j - 1, turned[1][j - 1]) if j > 0 else nothing8

        def left_of(j, turned=turned):
            return only(lane8 == 2 * j, turned[0][j]) if j < 4 else nothing8

        left_tile = solve(window(lane8, turned[0], right_of), f2[b, 0])
        right_tile = solve(window(lane8, turned[1], left_of), f2[b, 1])
        for h in range(2):
            at = slice(128 * h, 128 * h + 128)
            two.append((left_tile[:, at], right_tile[:, at]))
    for side in range(2):
        hs2[side, 0] = three[side]
        for t in range(2):
            hs2[side, 1 + t] = two[3 * side][t]
    h2_refs = (hs2, hb2, h2send, h2recv)
    start_rows(*h2_refs)

    edge_copy(2, partner, partner).wait_recv()

    @pl.when(has_beside)
    def _():
        edge_copy(0, beside, beside).wait_recv()

    @pl.when(has_behind)
    def _():
        edge_copy(1, behind, behind).wait_recv()

    to_partner(1 - core).wait_recv()
    left_edge, first_edge, second_edge, right_edge = (eb[2 * x + i, 1] for i in range(4))
    even = (lane & 1) == 0

    def edges(n):
        mid = jnp.where(even, second_edge, roll(first_edge, -n))
        outer = jnp.where(even, right_edge, roll(left_edge, -n))
        halo = jnp.where(even, first_edge + roll(left_edge, -n), right_edge + roll(second_edge, -n))
        return mid, outer, halo

    edges_of = {2: edges(4), 3: edges(6)}
    rows_one = []
    for r in range(10):
        m, h = divmod(r, 2)
        if h == 0:
            main = jnp.where(lane < 64, xm[0, m], roll(xm[1, m], 64))
        else:
            main = jnp.where(lane < 64, roll(xm[0, m], 64), xm[1, m])
        at, last = edge_lanes(r)
        mid, outer, _ = edges_of[(last - at) // 2]
        main = main + only(jnp.logical_or(lane == 63, lane == 64), roll(mid, 63 - at))
        main = main + only(jnp.logical_or(lane == 127, lane == 0), roll(outer, 127 - at))
        rows_one.append(main)
    halo_two, halo_three = edges_of[2][2], edges_of[3][2]
    halos = jnp.where(
        lane < 4,
        roll(halo_two, -18),
        jnp.where(lane < 10, roll(halo_three, -46), jnp.where(lane < 16, roll(halo_three, -104), roll(halo_two, -66))),
    )
    one = []
    for b in range(4):
        local[12 + b].wait()
        turned = [roll(rows_one[2 * b + k], 2 * k + 1) for k in range(4)]
        side = roll(halos, -4 * b)
        solved = solve(window(lane, turned, lambda j, side=side: side), f1[b])
        one += [solved[:, :128], solved[:, 128:]]
    hs[0] = one[0]
    hs[1] = one[7]
    h_refs = (hs, hb, hsend, hrecv)
    start_rows(*h_refs)
    column = nothing
    for r in range(8):
        column = jnp.where(lane == r, roll(one[r], r + core), column)
    cs[...] = column

    def to_side(d):
        return send(cs, cb.at[1 - d], esend.at[1 - d], erecv.at[1 - d], px=px + d, py=beside)

    for d in (-1, 1, 0):

        @pl.when(diag[1 + d])
        def _(d=d):
            to_side(d).start()

    @pl.when(z > 0)
    def _():
        send(f4own, zb4.at[0], z4send.at[1], z4recv.at[0], px=px - 4, py=py).wait_recv()

    @pl.when(z < 7)
    def _():
        send(f4own, zb4.at[1], z4send.at[0], z4recv.at[1], px=px + 4, py=py).wait_recv()

    quads = (zb4[0, 1], zb4[0, 2] + f4own[0], f4own[1], f4own[2] + zb4[1, 0], zb4[1, 1])
    four = []
    for b in range(4):
        local[16 + b].wait()
        first, second = quads[b], quads[b + 1]
        v0 = jnp.where(
            lane8 <= 64,
            only(lane8 >= 1, roll(first, 1)),
            only(lane8 >= 67, roll(first, 3)),
        )
        v1 = jnp.where(
            lane8 <= 2,
            roll(first, 3),
            jnp.where(lane8 <= 68, only(lane8 >= 5, roll(second, 5)), only(lane8 >= 71, roll(second, 7))),
        )
        v2 = only(lane8 <= 6, roll(second, 7))
        four.append(solve(jnp.concatenate([v0, v1, v2[:, :8]], axis=1), f4[b]))

    got_rows(*h2_refs)
    three = [hb2[0, 0]] + three + [hb2[1, 0]]
    two = [(hb2[0, 1], hb2[0, 2])] + two + [(hb2[1, 1], hb2[1, 2])]
    for c in range(4):

        def moved(tile, shift, width, c=c):
            return roll(tile, (shift + 1 - width * 2 * c + 512 - width * core) % 128)

        for half in range(2):
            pieces = []
            for u in range(3):
                row = two[3 * half + u]
                tile = row[c // 2]
                if c == 1:
                    tile = jnp.where(lane8 == 0, row[1], row[0])
                if c == 2:
                    tile = jnp.where(lane8 == 127, row[0], row[1])
                pieces.append(moved(tile, 42 * u, 32))
            rs[c, half] = jnp.where(lane8 < 42, pieces[0], jnp.where(lane8 < 84, pieces[1], pieces[2]))
        pieces = [moved(three[s], 32 * s, 16) for s in range(4)]
        rs[c, 2] = jnp.where(
            lane8 < 64, jnp.where(lane8 < 32, pieces[0], pieces[1]), jnp.where(lane8 < 96, pieces[2], pieces[3])
        )
        pieces = [moved(four[b], 10 * b, 8) for b in range(4)]
        low_lane = lane8 & 63
        rs[c, 3] = jnp.where(
            low_lane < 20,
            jnp.where(low_lane < 10, pieces[0], pieces[1]),
            jnp.where(low_lane < 30, pieces[2], pieces[3]),
        )
    rb[x] = rs[x]

    def to_chip(d, me):
        peer = (me + d) % 4
        return send(rs.at[peer], rb.at[me], rsend.at[d - 1], rrecv.at[me], px=px, py=2 * peer + core)

    for d in (2, 1, 3):
        begin(to_chip(d, x))

    before, after = eb[py, 0], eb[py + 2, 0]
    corner_before, corner_after = eb[py, 1], eb[py + 2, 1]
    facing = jnp.where(even, before, after)
    corners = jnp.where(even, corner_before, corner_after)
    halos = jnp.where(
        lane < 2,
        roll(corners, -26),
        jnp.where(lane < 18, roll(facing, -46), jnp.where(lane < 34, roll(facing, -94), roll(corners, 6))),
    )
    local[10].wait()
    for b in range(8):
        tiles = []
        for k in range(4):
            at = 2 * b + k
            tile = pb[0, 2] if at == 0 else pb[1, 2] if at == 17 else xt[at - 1]
            tiles.append(roll(tile, 2 * k + 1))
        side = roll(halos, -4 * b)
        solved = solve(window(lane, tiles, lambda j, side=side: side), ff[b, 0])
        p0[2 * b] = solved[:, :128]
        p0[2 * b + 1] = solved[:, 128:]

    for d in range(1, 8):
        to_z(d, (z + 8 - d) % 8).wait_recv()
    local[9].wait()
    down = [roll(zb5[i + 1], -32) if i < 8 else nothing8 for i in range(0, 10, 2)]
    rise = [nothing8] + [roll(zb5[i + 1], 32) for i in range(1, 8, 2)]
    flat = [
        jnp.where(lane8 < 96, down[j], down[j + 1]) + jnp.where(lane8 >= 32, rise[j + 1], rise[j]) for j in range(4)
    ]
    solved = solve(jnp.concatenate(flat, axis=1), ci[...])
    p5[0] = nothing8
    p5[5] = nothing8
    for j in range(4):
        p5[j + 1] = solved[:, 128 * j : 128 * j + 128]
    odd = z % 2
    lead = (z + odd) // 2
    edge = 32 + 64 * odd
    rb5[x] = jnp.where(lane8 < edge, roll(p5[lead], edge), roll(p5[lead + 1], edge))

    def to_chip5(d, me):
        peer = (me + d) % 4
        return send(rb5.at[me], rb5.at[me], r5send.at[d - 1], r5recv.at[me], px=px, py=2 * peer + core)

    for d in (2, 1, 3):
        begin(to_chip5(d, x))

    got_rows(*h_refs)
    for d in (-1, 0, 1):

        @pl.when(diag[1 + d])
        def _(d=d):
            send(cs, cb.at[1 + d], esend.at[1 + d], erecv.at[1 + d], px=px + d, py=beside).wait_recv()

    local[6].wait()
    local[11].wait()
    one = [hb[0]] + one + [hb[1]]
    at_lane = 127 * (1 - core)
    for r in range(10):
        source, from_lane = (0, 7) if r == 0 else (2, 0) if r == 9 else (1, r - 1)
        one[r] = jnp.where(lane == at_lane, roll(cb[source], (at_lane - from_lane + 128) % 128), one[r])
    one = lifted(one, up[0:128, :])
    for d in range(1, 4):
        to_chip(d, (x + 4 - d) % 4).wait_recv()
    back = [rb[:, t].reshape(32, 128) for t in range(4)]
    two = [only(jnp.logical_and(lane >= 42 * u, lane < 42 * u + 34), back[h]) for h in range(2) for u in range(3)]
    three = [only((lane // 32) == s, back[2]) for s in range(4)]
    four = [
        only(jnp.logical_and(lane >= 64 * h + 10 * b, lane < 64 * h + 10 * b + 10), back[3])
        for b in range(4)
        for h in range(2)
    ]
    two = lifted(two, near[0:128, :])
    three = lifted(three, near[128:256, :])
    four = lifted(four, near[256:384, :])
    local[5].wait()
    terms = one + two + three + four
    for f in range(16):
        total = p0[f]
        for r in range(28):
            if up_used[r][f]:
                total = total + uw[r // 8, 16 * (r % 8) + f] * terms[r]
        acc[f] = total

    for d in range(1, 4):
        to_chip5(d, (x + 4 - d) % 4).wait_recv()
    five = rb5[...].reshape(32, 128)
    full = jnp.concatenate([only((lane // 32) == s, five) for s in range(4)], axis=0)
    top = full.astype(BF)
    rest = (full - top.astype(F32)).astype(BF)
    product = jnp.dot(jnp.concatenate([top, rest], axis=0), up[128:256, :], preferred_element_type=F32)
    product = product[:128] + product[128:] + jnp.dot(top, up[256:384, :], preferred_element_type=F32)
    for f in range(16):
        total = acc[f]
        for s in range(4):
            if up_used[28 + s][f]:
                total = total + uw[3, 16 * (4 + s) + f] * product[32 * s : 32 * s + 32]
        out_ref[pl.ds(f, 32, stride=16), :] = total

    for copy in sent:
        copy.wait_send()
    for refs in (b_refs, g_refs, h2_refs, h_refs):
        sent_rows(*refs)

    @pl.when(has_beside)
    def _():
        edge_copy(0, py, beside).wait_send()
        edge_copy(1, py, beyond).wait_send()

    @pl.when(z > 0)
    def _():
        z4_down().wait_send()

    @pl.when(z < 7)
    def _():
        z4_up().wait_send()

    for d in (-1, 0, 1):

        @pl.when(diag[1 + d])
        def _(d=d):
            to_side(d).wait_send()


def per_device(residual, fine, one, two, three, four, inverse):
    weights, down_b, up, near, down_used, up_used = tables()

    def tiles(*lead):
        return pltpu.VMEM(lead + (32, 128), F32)

    def small(*lead):
        return pltpu.VMEM(lead + (8, 128), F32)

    dma = pltpu.SemaphoreType.DMA
    out = pl.pallas_call(
        functools.partial(kernel, down_used, up_used),
        out_shape=jax.ShapeDtypeStruct((512, 128), F32),
        in_specs=[pl.BlockSpec(memory_space=pltpu.HBM)] * 11,
        out_specs=pl.BlockSpec(memory_space=pltpu.VMEM),
        scratch_shapes=[
            pltpu.VMEM((512, 128), F32),
            pltpu.VMEM((8, 1, 520, 256), BF),
            pltpu.VMEM((4, 520, 256), BF),
            pltpu.VMEM((2, 2, 520, 256), BF),
            pltpu.VMEM((520, 256), BF),
            pltpu.VMEM((4, 264, 128), BF),
            pltpu.VMEM((512, 512), BF),
            pltpu.VMEM((144, 128), F32),
            pltpu.SMEM((8, 128), F32),
            pltpu.VMEM((256, 512), BF),
            pltpu.VMEM((128, 128), BF),
            pltpu.VMEM((384, 128), BF),
            pltpu.VMEM((384, 128), BF),
            tiles(16),
            pltpu.VMEM((512, 512), F32),
            tiles(8),
            tiles(2, 3),
            tiles(2, 3),
            tiles(10, 2),
            tiles(2, 5),
            tiles(2),
            tiles(2),
            tiles(),
            tiles(3),
            tiles(16),
            tiles(16),
            small(4, 3),
            small(8),
            small(8, 3),
            small(4),
            small(4, 3),
            small(10),
            small(3),
            small(2, 3),
            small(2, 6),
            small(2, 6),
            small(2, 3),
            small(2, 3),
            small(4, 4),
            small(4, 4),
            small(4),
            small(6),
            dma((20,)),
        ]
        + [
            dma if n == 0 else dma((n,))
            for n in (7, 8, 7, 8, 2, 2, 3, 8, 0, 0, 3, 4, 3, 4, 7, 8, 2, 2, 2, 2, 3, 3, 2, 2, 2, 2, 3, 4, 3, 4)
        ],
        compiler_params=pltpu.CompilerParams(
            collective_id=0, has_side_effects=True, vmem_limit_bytes=56147968
        ),
    )(
        residual.reshape(512, 128), fine, one, two, three, four, inverse,
        jnp.asarray(weights), jnp.asarray(down_b), jnp.asarray(up), jnp.asarray(near),
    )
    return out.reshape(32, 16, 128)


def solution(mesh):
    placed = (
        P(None, "px", "py"),
        P("px", "py", None, None),
        P("px", None, None, None),
        P("px", None, None, None),
        P("px", None, None, None),
        P(),
        P(),
    )
    return jax.shard_map(
        per_device, mesh=mesh, in_specs=placed, out_specs=P(None, "px", "py"), check_vma=False
    )
```

```python
import functools

import jax
import jax.numpy as jnp
import numpy as np
from jax import lax
from jax.experimental import pallas as pl
from jax.experimental.pallas import tpu as pltpu
from jax.sharding import PartitionSpec as P

F32 = jnp.float32
BF = jnp.bfloat16
MESH = pl.DeviceIdType.MESH
LANES_FOUR = (6, 16, 38)
ROWS_TWO = ((0, 1, 2), (4, 5, 3))
GROUP_OF = (0, 1, 2, 2, 3, 3, 3, 3, 3)


def composites(count):
    found, now = [], np.eye(count)
    for _ in range(5):
        fine = now.shape[0]
        step = np.zeros((fine // 2, fine))
        for i in range(fine // 2):
            for shift, tap in ((-1, 1), (0, 3), (1, 3), (2, 1)):
                if 0 <= 2 * i + shift < fine:
                    step[i, 2 * i + shift] = tap
        now = step @ now
        found.append(now)
    return found


def pick(matrix, row, low, count):
    if 0 <= row < matrix.shape[0]:
        return matrix[row, low : low + count]
    return np.zeros(count)


def edge_lanes(row):
    slot, first, count = ((0, 0, 2), (1, 2, 3), (3, 5, 3), (2, 8, 2))[(row >= 2) + (row >= 5) + (row >= 8)]
    base = 32 * slot + 18 + 2 * (row - first)
    return base, base + 2 * count


def down_rows(rows, px):
    z, low = px // 4, 16 * px
    a1, a2, a3, a4, a5 = (m / 20.0 ** (i + 1) for i, m in enumerate(rows))
    w = np.zeros((9, 16, 128))
    for s in range(4):
        w[0, :, 32 * s : 32 * s + 6] = pick(a5, 2 * z - 1 + s, low, 16)[:, None]
        w[1, :, 32 * s : 32 * s + 18] = pick(a3, 2 * px - 1 + s, low, 16)[:, None]
    for m, at in enumerate(LANES_FOUR):
        for h in range(2):
            w[0, :, at + 64 * h : at + 64 * h + 10] = pick(a4, 4 * z - 1 + 2 * m + h, low, 16)[:, None]
    for e in range(16):
        w[0, e // 2, 48 + e] = 1.0
        w[0, 8 + e // 2, 112 + e] = 1.0
    for r in range(10):
        for at in edge_lanes(r):
            w[1, :, at : at + 2] = pick(a1, 8 * px - 1 + r, low, 16)[:, None]
    for half in range(2):
        for u in range(3):
            w[2 + half, :, 42 * u : 42 * u + 34] = pick(a2, 4 * px - 1 + ROWS_TWO[half][u], low, 16)[:, None]
    for m in range(5):
        for h in range(2):
            w[4 + m, :, 64 * h : 64 * h + 64] = pick(a1, 8 * px - 1 + 2 * m + h, low, 16)[:, None]
    return w


def down_columns(columns, py):
    b1, b2, b3, b4, b5 = columns
    low = 128 * py
    b = np.zeros((128, 512))
    for s in range(4):
        for c in range(6):
            b[:, 32 * s + c] = pick(b5, 4 * py - 1 + c, low, 128)
        for c in range(18):
            b[:, 128 + 32 * s + c] = pick(b3, 16 * py - 1 + c, low, 128)
    for at in LANES_FOUR:
        for c in range(10):
            b[:, at + c] = b[:, at + 64 + c] = pick(b4, 8 * py - 1 + c, low, 128)
    for e in range(16):
        b[0 if e % 2 else 127, 48 + e] = 1.0
        b[0 if e % 2 else 127, 112 + e] = 1.0
    for r in range(10):
        p, q = edge_lanes(r)
        for at, col in ((p, -1), (p + 1, 0), (q, 63), (q + 1, 64)):
            b[:, 128 + at] = pick(b1, 64 * py + col, low, 128)
    for u in range(3):
        for c in range(34):
            b[:, 256 + 42 * u + c] = pick(b2, 32 * py - 1 + c, low, 128)
    for c in range(64):
        b[:, 384 + c] = b[:, 448 + c] = pick(b1, 64 * py + c, low, 128)
    return b


def up_one(columns, py):
    low, tile = 128 * py, 128 * (py // 2)
    one = np.stack([pick(columns[0], tile + c, low, 128) for c in range(128)])
    if py % 2 == 0:
        one[127] = pick(columns[0], tile - 1, low, 128)
    else:
        one[0] = pick(columns[0], tile + 128, low, 128)
    return one, np.stack([pick(columns[4], c % 32, low, 128) for c in range(128)])


def up_near(columns, py):
    low = 128 * py
    two, three, four = (np.zeros((128, 128)) for _ in range(3))
    for u in range(3):
        for c in range(34):
            two[42 * u + c] = pick(columns[1], 32 * py - 1 + c, low, 128)
    for s in range(4):
        for c in range(18):
            three[32 * s + c] = pick(columns[2], 16 * py - 1 + c, low, 128)
        for c in range(10):
            four[10 * s + c] = four[64 + 10 * s + c] = pick(columns[3], 8 * py - 1 + c, low, 128)
    return np.concatenate([two, three, four])


def up_rows(rows, px):
    z, low = px // 4, 16 * px
    w = np.zeros((32, 16))
    firsts = ((0, 10, 8 * px - 1), (10, 6, 4 * px - 1), (16, 4, 2 * px - 1), (20, 8, 4 * z - 2), (28, 4, 2 * z - 1))
    for level, (at, count, first) in enumerate(firsts):
        for i in range(count):
            w[at + i] = pick(rows[level], first + i, low, 16) / 20.0 ** (level + 1)
    return w


def split(matrix):
    high = matrix.astype(BF)
    return high, (matrix - high.astype(np.float64)).astype(BF)


@functools.cache
def tables():
    rows, columns = composites(512), composites(1024)
    some = (12, 13, 14, 15, 0, 31)
    down_w = np.stack([down_rows(rows, px) for px in some])
    up_w = np.stack([up_rows(rows, px) for px in some])
    down_b, near = [], []
    for py in (0, 3, 7):
        high, low = split(down_columns(columns, py))
        down_b.append(np.concatenate([high, low[:, :128]], axis=1))
        near.append(up_near(columns, py).astype(BF))
    up = []
    for py in range(8):
        one, five = up_one(columns, py)
        high, low = split(five)
        up.append(np.concatenate([one.astype(BF), high, low]))
    weights = [down_w.reshape(6, 144, 128), np.pad(up_w.reshape(6, 4, 128), ((0, 0), (0, 4), (0, 0)))]
    return (
        np.concatenate(weights, axis=1).astype(np.float32),
        np.stack(down_b),
        np.stack(up),
        np.stack(near),
        (down_w != 0).any(axis=(0, 3)).tolist(),
        (up_w != 0).any(axis=0).tolist(),
    )


def kernel(
    down_used, up_used,
    res_hbm, ff_hbm, f1_hbm, f2_hbm, f3_hbm, f4_hbm, ci_hbm, w_hbm, db_hbm, up_hbm, near_hbm,
    out_ref,
    res, ff, f1, f2, f3, f4, ci, dw, uw, db, db5, up, near,
    xt, yy, own, sb, pb, eb, xm, hs, hb, cs, cb, p0, acc,
    abuf, a5, a3, yb5, yb4, zb5, f4own, zb4, gs, gb, hs2, hb2, rs, rb, rb5, p5,
    lsem, a5send, a5recv, a3send, a3recv, bsend, brecv, dsend, drecv, msend, mrecv, y5send, y5recv, y4send, y4recv,
    z5send, z5recv, z4send, z4recv, hsend, hrecv, esend, erecv, gsend, grecv, h2send, h2recv, rsend, rrecv, r5send, r5recv, zs,
):
    px, py = lax.axis_index("px"), lax.axis_index("py")
    z, y = px // 4, px % 4
    x, core = py // 2, py % 2
    has_left, has_right = px > 0, px < 31
    step = 2 * core - 1
    has_beside = jnp.logical_and(py + step >= 0, py + step < 8)
    beside = jnp.clip(py + step, 0, 7)
    beyond = jnp.clip(py + 2 * step, 0, 7)
    has_behind = jnp.logical_and(py - 2 * step >= 0, py - 2 * step < 8)
    behind = jnp.clip(py - 2 * step, 0, 7)
    partner = py + 1 - 2 * core
    variant = jnp.where(px == 0, 4, jnp.where(px == 31, 5, y))
    place = jnp.where(py == 0, 0, jnp.where(py == 7, 2, 1))
    lane = lax.broadcasted_iota(jnp.int32, (32, 128), 1)
    lane8 = lax.broadcasted_iota(jnp.int32, (8, 128), 1)

    def roll(tile, shift):
        if isinstance(shift, int):
            shift %= 128
            return tile if shift == 0 else pltpu.roll(tile, shift, 1)
        return pltpu.roll(tile, shift, 1)

    def only(mask, tile):
        return jnp.where(mask, tile, 0.0)

    barrier = pltpu.get_barrier_semaphore()

    def greet(**where):
        pl.semaphore_signal(barrier, inc=1, device_id=where, device_id_type=MESH)

    for d in (1, 7):
        greet(px=((z + d) % 8) * 4 + y, py=py)

    local = [
        (res_hbm, res),
        (db_hbm.at[place, :, pl.ds(0, 512)], db.at[pl.ds(0, 128)]),
        (db_hbm.at[place, :, pl.ds(0, 512)], db.at[pl.ds(128, 128)]),
        (db_hbm.at[place, :, pl.ds(512, 128)], db5),
        (w_hbm.at[variant, pl.ds(0, 144)], dw),
        (w_hbm.at[variant, pl.ds(144, 8)], uw),
        (up_hbm.at[py], up),
        (f3_hbm.at[0, 0], f3),
        (f2_hbm, f2),
        (ci_hbm, ci),
        (ff_hbm, ff),
        (near_hbm.at[place], near),
    ]
    local += [(f1_hbm.at[b, x], f1.at[b]) for b in range(4)]
    local += [(f4_hbm.at[jnp.clip(2 * z - 1 + b, 0, 15), 0], f4.at[b]) for b in range(4)]
    local = [pltpu.make_async_copy(s, d, lsem.at[i]) for i, (s, d) in enumerate(local)]
    for copy in local[:5]:
        copy.start()

    for d in (4, 3, 5, 2, 6, 1, 7):
        greet(px=px, py=(py + d) % 8)
    for d in range(1, 4):
        greet(px=z * 4 + (y + d) % 4, py=py)
    left_diagonal = jnp.logical_and(has_left, has_beside)
    right_diagonal = jnp.logical_and(has_right, has_beside)

    @pl.when(has_left)
    def _():
        greet(px=px - 1, py=py)

    @pl.when(has_right)
    def _():
        greet(px=px + 1, py=py)

    def send(src, dst, ssem, rsem, **where):
        return pltpu.make_async_remote_copy(
            src_ref=src, dst_ref=dst, send_sem=ssem, recv_sem=rsem, device_id=where, device_id_type=MESH
        )

    nothing = jnp.zeros((32, 128), F32)
    nothing8 = jnp.zeros((8, 128), F32)
    for end in (0, 9):
        zb5[end] = nothing8
        for i in range(2):
            eb[end, i] = nothing

    for side, missing in ((0, px == 0), (1, px == 31)):

        @pl.when(missing)
        def _(side=side):
            for i in range(3):
                pb[side, i] = nothing
                hb2[side, i] = nothing8
            hb[side] = nothing
            for i in range(6):
                gb[side, i] = nothing8

    for side, missing in ((0, z == 0), (1, z == 7)):

        @pl.when(missing)
        def _(side=side):
            for i in range(3):
                zb4[side, i] = nothing8

    diag = (left_diagonal, has_beside, right_diagonal)
    for i in range(3):

        @pl.when(jnp.logical_not(diag[i]))
        def _(i=i):
            cb[i] = nothing

    local[0].wait()
    for f in range(16):
        xt[f] = res[pl.ds(f, 32, stride=16), :]
    rows = xt[...].reshape(512, 128)
    high = rows.astype(BF)
    low = (rows - high.astype(F32)).astype(BF)
    both = jnp.concatenate([high, low], axis=1)
    for i in range(1, 5):
        local[i].wait()
    yy[:, :256] = jnp.dot(both, db[:, :256], preferred_element_type=F32)
    yy[:, :128] += jnp.dot(high, db5[...], preferred_element_type=F32)

    def packed(t):
        at = 128 * GROUP_OF[t]
        total = None
        for f in range(16):
            if down_used[t][f]:
                term = yy[32 * f : 32 * f + 32, at : at + 128] * dw[16 * t + f : 16 * t + f + 1, :]
                total = term if total is None else total + term
        return total

    eb[py + 1, 0] = packed(0)
    a5[py] = eb[py + 1, 0, pl.ds(pl.multiple_of(8 * x, 8), 8), :]
    pl.semaphore_wait(
        barrier,
        12 + jnp.where(has_left, 1, 0) + jnp.where(has_right, 1, 0),
    )

    def pass_on(i):
        for d in (1, 7):
            peer = {"px": ((z + d) % 8) * 4 + y, "py": py}
            pl.semaphore_signal(zs.at[i], inc=1, device_id=peer, device_id_type=MESH)

    sent = []

    def begin(copy):
        copy.start()
        sent.append(copy)

    FAR = (4, 3, 5, 2, 6, 1, 7)

    def to_five(d, me):
        peer = (me + d) % 8
        group = pl.multiple_of(8 * (peer // 2), 8)
        return send(eb.at[py + 1, 0, pl.ds(group, 8)], a5.at[me], a5send.at[d - 1], a5recv.at[me], px=px, py=peer)

    def to_three(d, me):
        peer = (me + d) % 8
        return send(abuf.at[peer // 2], a3.at[me], a3send.at[d - 1], a3recv.at[me], px=px, py=peer)

    for d in FAR:
        begin(to_five(d, py))
    pass_on(0)
    for copy in local[5:]:
        copy.start()

    yy[:, 256:] = jnp.dot(both, db[:, 256:], preferred_element_type=F32)
    for t in range(1, 4):
        tile = packed(t)
        own[t - 1] = tile
        for c in range(4):
            abuf[c, t - 1] = tile[8 * c : 8 * c + 8]
    a3[py] = abuf[x]
    for d in FAR:
        begin(to_three(d, py))
    pl.semaphore_wait(zs.at[0], 2)
    pass_on(1)
    for t in range(4, 9):
        own[t - 1] = packed(t)
    sb[0, 0] = own[0]
    sb[1, 0] = own[0]
    sb[0, 1] = own[3]
    sb[1, 1] = own[7]
    sb[0, 2] = xt[0]
    sb[1, 2] = xt[15]

    def left_copy(src, dst, ssem, rsem):
        return send(src.at[0], dst.at[1], ssem.at[0], rsem.at[1], px=px - 1, py=py)

    def right_copy(src, dst, ssem, rsem):
        return send(src.at[1], dst.at[0], ssem.at[1], rsem.at[0], px=px + 1, py=py)

    def start_rows(*refs):
        @pl.when(has_left)
        def _():
            left_copy(*refs).start()

        @pl.when(has_right)
        def _():
            right_copy(*refs).start()

    def got_rows(src, dst, ssem, rsem):
        @pl.when(has_left)
        def _():
            send(src.at[1], dst.at[0], ssem.at[1], rsem.at[0], px=px - 1, py=py).wait_recv()

        @pl.when(has_right)
        def _():
            send(src.at[0], dst.at[1], ssem.at[0], rsem.at[1], px=px + 1, py=py).wait_recv()

    def sent_rows(*refs):
        @pl.when(has_left)
        def _():
            left_copy(*refs).wait_send()

        @pl.when(has_right)
        def _():
            right_copy(*refs).wait_send()

    b_refs = (sb, pb, bsend, brecv)
    start_rows(*b_refs)
    pl.semaphore_wait(zs.at[1], 2)
    pass_on(2)

    for d in range(1, 8):
        to_five(d, (py + 8 - d) % 8).wait_recv()
    five, fours = None, [None] * 3
    for p in range(8):
        tile = a5[p]
        term = only(((lane8 - 4 * p + 1) & 31) < 6, roll(tile, 4 * p - 1))
        five = term if five is None else five + term
        close = ((lane8 - 8 * p + 1) & 63) < 10
        for m in range(3):
            term = only(close, roll(tile, 8 * p - 1 - LANES_FOUR[m]))
            fours[m] = term if fours[m] is None else fours[m] + term
    yb5[y] = five
    for m in range(3):
        yb4[y, m] = fours[m]

    def to_y(buffer, ssem, rsem, d, slot):
        return send(buffer.at[slot], buffer.at[slot], ssem.at[d - 1], rsem.at[slot], px=z * 4 + (y + d) % 4, py=py)

    for d in (2, 1, 3):
        begin(to_y(yb5, y5send, y5recv, d, y))
    for d in (2, 1, 3):
        begin(to_y(yb4, y4send, y4recv, d, y))

    for d in range(1, 8):
        to_three(d, (py + 8 - d) % 8).wait_recv()
    rows_three = []
    for s in range(4):
        total = None
        for p in range(8):
            close = jnp.logical_and(lane8 >= 16 * p - 1, lane8 <= 16 * p + 16)
            term = only(close, roll(a3[p, 0], 16 * p - 1 - 32 * s))
            total = term if total is None else total + term
        rows_three.append(total)
    rows_two = []
    for r in range(6):
        half, u = next((h, ROWS_TWO[h].index(r)) for h in range(2) if r in ROWS_TWO[h])
        pair = [None, None]
        for p in range(8):
            turned = roll(a3[p, 1 + half], 32 * p - 1 - 42 * u)
            first = 32 * (p % 4) - 1
            close = jnp.logical_and(lane8 >= first, lane8 <= first + 33)
            term = only(close, turned)
            pair[p // 4] = term if pair[p // 4] is None else pair[p // 4] + term
            if p == 3:
                pair[1] = only(lane8 == 0, turned)
            if p == 4:
                pair[0] = pair[0] + only(lane8 == 127, turned)
        rows_two.append(pair)
    for side in range(2):
        for i in range(2):
            gs[side, i] = rows_three[2 * side + i]
            for t in range(2):
                gs[side, 2 + 2 * i + t] = rows_two[4 * side + i][t]
    g_refs = (gs, gb, gsend, grecv)
    start_rows(*g_refs)

    got_rows(*b_refs)
    mine = own[0]
    across = jnp.where(lane < 64, roll(pb[0, 0], 64), roll(pb[1, 0], 64))
    inside = jnp.logical_or((lane & 63) < 50, (lane & 63) > 61)
    mine = mine + only(inside, across)
    corner = jnp.where(lane < 28, roll(pb[0, 2], 27), roll(pb[1, 2], 29))
    eb[py + 1, 1] = jnp.where(jnp.logical_and(lane >= 26, lane < 30), corner, mine)
    xm[core, 0] = own[3] + pb[0, 1]
    for m in range(1, 4):
        xm[core, m] = own[3 + m]
    xm[core, 4] = own[7] + pb[1, 1]

    def to_partner(slot):
        return send(xm.at[slot], xm.at[slot], msend, mrecv, px=px, py=partner)

    def edge_copy(i, slot, peer):
        return send(eb.at[slot + 1], eb.at[slot + 1], dsend.at[i], drecv.at[slot], px=px, py=peer)

    @pl.when(has_beside)
    def _():
        edge_copy(0, py, beside).start()
        edge_copy(1, py, beyond).start()

    begin(edge_copy(2, py, partner))
    begin(to_partner(core))

    for d in range(1, 4):
        to_y(yb5, y5send, y5recv, d, (y + 4 - d) % 4).wait_recv()
    zb5[z + 1] = (yb5[0] + yb5[1]) + (yb5[2] + yb5[3])

    def to_z(d, slot):
        return send(zb5.at[slot + 1], zb5.at[slot + 1], z5send.at[d - 1], z5recv.at[slot], px=((z + d) % 8) * 4 + y, py=py)

    pl.semaphore_wait(zs.at[2], 2)
    for d in FAR:
        begin(to_z(d, z))
    for d in range(1, 4):
        to_y(yb4, y4send, y4recv, d, (y + 4 - d) % 4).wait_recv()
    for m in range(3):
        f4own[m] = (yb4[0, m] + yb4[1, m]) + (yb4[2, m] + yb4[3, m])

    def z4_down():
        return send(f4own, zb4.at[1], z4send.at[0], z4recv.at[1], px=px - 4, py=py)

    def z4_up():
        return send(f4own, zb4.at[0], z4send.at[1], z4recv.at[0], px=px + 4, py=py)

    @pl.when(z > 0)
    def _():
        z4_down().start()

    @pl.when(z < 7)
    def _():
        z4_up().start()

    def solve(windows, factor):
        return jnp.dot(windows.astype(BF), factor, preferred_element_type=F32)

    def window(at, shifted, halo):
        parts = [jnp.where(at == 0, halo(0), shifted[0])]
        for j in range(1, 4):
            parts.append(jnp.where(at <= 2 * j - 2, shifted[j - 1], jnp.where(at <= 2 * j, halo(j), shifted[j])))
        last = jnp.where(at <= 6, shifted[3], halo(4))
        return jnp.concatenate(parts + [last[:, :8]], axis=1)

    def lifted(tiles, table):
        count = 32 * len(tiles)
        fine = jnp.concatenate(tiles, axis=0)
        top = fine.astype(BF)
        rest = (fine - top.astype(F32)).astype(BF)
        product = jnp.dot(jnp.concatenate([top, rest], axis=0), table, preferred_element_type=F32)
        product = product[:count] + product[count:]
        return [product[32 * i : 32 * i + 32] for i in range(len(tiles))]

    got_rows(*g_refs)
    for side in range(2):
        for i in range(2):
            rows_three[2 * side + i] = rows_three[2 * side + i] + gb[side, i]
            rows_two[4 * side + i] = [rows_two[4 * side + i][t] + gb[side, 2 + 2 * i + t] for t in range(2)]
    local[7].wait()
    shifted = [roll(rows_three[k], 2 * k + 1) for k in range(4)]
    solved = solve(window(lane8, shifted, lambda j: nothing8), f3[...])
    three = [solved[:, :128], solved[:, 128:]]
    local[8].wait()
    two = []
    for b in range(2):
        turned = [[roll(rows_two[2 * b + k][t], 2 * k + 1) for k in range(4)] for t in range(2)]

        def right_of(j, turned=turned):
            return only(lane8 == 2 * j - 1, turned[1][j - 1]) if j > 0 else nothing8

        def left_of(j, turned=turned):
            return only(lane8 == 2 * j, turned[0][j]) if j < 4 else nothing8

        left_tile = solve(window(lane8, turned[0], right_of), f2[b, 0])
        right_tile = solve(window(lane8, turned[1], left_of), f2[b, 1])
        for h in range(2):
            at = slice(128 * h, 128 * h + 128)
            two.append((left_tile[:, at], right_tile[:, at]))
    for side in range(2):
        hs2[side, 0] = three[side]
        for t in range(2):
            hs2[side, 1 + t] = two[3 * side][t]
    h2_refs = (hs2, hb2, h2send, h2recv)
    start_rows(*h2_refs)

    edge_copy(2, partner, partner).wait_recv()

    @pl.when(has_beside)
    def _():
        edge_copy(0, beside, beside).wait_recv()

    @pl.when(has_behind)
    def _():
        edge_copy(1, behind, behind).wait_recv()

    to_partner(1 - core).wait_recv()
    left_edge, first_edge, second_edge, right_edge = (eb[2 * x + i, 1] for i in range(4))
    even = (lane & 1) == 0

    def edges(n):
        mid = jnp.where(even, second_edge, roll(first_edge, -n))
        outer = jnp.where(even, right_edge, roll(left_edge, -n))
        halo = jnp.where(even, first_edge + roll(left_edge, -n), right_edge + roll(second_edge, -n))
        return mid, outer, halo

    edges_of = {2: edges(4), 3: edges(6)}
    rows_one = []
    for r in range(10):
        m, h = divmod(r, 2)
        if h == 0:
            main = jnp.where(lane < 64, xm[0, m], roll(xm[1, m], 64))
        else:
            main = jnp.where(lane < 64, roll(xm[0, m], 64), xm[1, m])
        at, last = edge_lanes(r)
        mid, outer, _ = edges_of[(last - at) // 2]
        main = main + only(jnp.logical_or(lane == 63, lane == 64), roll(mid, 63 - at))
        main = main + only(jnp.logical_or(lane == 127, lane == 0), roll(outer, 127 - at))
        rows_one.append(main)
    halo_two, halo_three = edges_of[2][2], edges_of[3][2]
    halos = jnp.where(
        lane < 4,
        roll(halo_two, -18),
        jnp.where(lane < 10, roll(halo_three, -46), jnp.where(lane < 16, roll(halo_three, -104), roll(halo_two, -66))),
    )
    one = []
    for b in range(4):
        local[12 + b].wait()
        turned = [roll(rows_one[2 * b + k], 2 * k + 1) for k in range(4)]
        side = roll(halos, -4 * b)
        solved = solve(window(lane, turned, lambda j, side=side: side), f1[b])
        one += [solved[:, :128], solved[:, 128:]]
    hs[0] = one[0]
    hs[1] = one[7]
    h_refs = (hs, hb, hsend, hrecv)
    start_rows(*h_refs)
    column = nothing
    for r in range(8):
        column = jnp.where(lane == r, roll(one[r], r + core), column)
    cs[...] = column

    def to_side(d):
        return send(cs, cb.at[1 - d], esend.at[1 - d], erecv.at[1 - d], px=px + d, py=beside)

    for d in (-1, 1, 0):

        @pl.when(diag[1 + d])
        def _(d=d):
            to_side(d).start()

    @pl.when(z > 0)
    def _():
        send(f4own, zb4.at[0], z4send.at[1], z4recv.at[0], px=px - 4, py=py).wait_recv()

    @pl.when(z < 7)
    def _():
        send(f4own, zb4.at[1], z4send.at[0], z4recv.at[1], px=px + 4, py=py).wait_recv()

    quads = (zb4[0, 1], zb4[0, 2] + f4own[0], f4own[1], f4own[2] + zb4[1, 0], zb4[1, 1])
    four = []
    for b in range(4):
        local[16 + b].wait()
        first, second = quads[b], quads[b + 1]
        v0 = jnp.where(
            lane8 <= 64,
            only(lane8 >= 1, roll(first, 1)),
            only(lane8 >= 67, roll(first, 3)),
        )
        v1 = jnp.where(
            lane8 <= 2,
            roll(first, 3),
            jnp.where(lane8 <= 68, only(lane8 >= 5, roll(second, 5)), only(lane8 >= 71, roll(second, 7))),
        )
        v2 = only(lane8 <= 6, roll(second, 7))
        four.append(solve(jnp.concatenate([v0, v1, v2[:, :8]], axis=1), f4[b]))

    got_rows(*h2_refs)
    three = [hb2[0, 0]] + three + [hb2[1, 0]]
    two = [(hb2[0, 1], hb2[0, 2])] + two + [(hb2[1, 1], hb2[1, 2])]
    for c in range(4):

        def moved(tile, shift, width, c=c):
            return roll(tile, (shift + 1 - width * 2 * c + 512 - width * core) % 128)

        for half in range(2):
            pieces = []
            for u in range(3):
                row = two[3 * half + u]
                tile = row[c // 2]
                if c == 1:
                    tile = jnp.where(lane8 == 0, row[1], row[0])
                if c == 2:
                    tile = jnp.where(lane8 == 127, row[0], row[1])
                pieces.append(moved(tile, 42 * u, 32))
            rs[c, half] = jnp.where(lane8 < 42, pieces[0], jnp.where(lane8 < 84, pieces[1], pieces[2]))
        pieces = [moved(three[s], 32 * s, 16) for s in range(4)]
        rs[c, 2] = jnp.where(
            lane8 < 64, jnp.where(lane8 < 32, pieces[0], pieces[1]), jnp.where(lane8 < 96, pieces[2], pieces[3])
        )
        pieces = [moved(four[b], 10 * b, 8) for b in range(4)]
        low_lane = lane8 & 63
        rs[c, 3] = jnp.where(
            low_lane < 20,
            jnp.where(low_lane < 10, pieces[0], pieces[1]),
            jnp.where(low_lane < 30, pieces[2], pieces[3]),
        )
    rb[x] = rs[x]

    def to_chip(d, me):
        peer = (me + d) % 4
        return send(rs.at[peer], rb.at[me], rsend.at[d - 1], rrecv.at[me], px=px, py=2 * peer + core)

    for d in (2, 1, 3):
        begin(to_chip(d, x))

    before, after = eb[py, 0], eb[py + 2, 0]
    corner_before, corner_after = eb[py, 1], eb[py + 2, 1]
    facing = jnp.where(even, before, after)
    corners = jnp.where(even, corner_before, corner_after)
    halos = jnp.where(
        lane < 2,
        roll(corners, -26),
        jnp.where(lane < 18, roll(facing, -46), jnp.where(lane < 34, roll(facing, -94), roll(corners, 6))),
    )
    local[10].wait()
    for b in range(8):
        tiles = []
        for k in range(4):
            at = 2 * b + k
            tile = pb[0, 2] if at == 0 else pb[1, 2] if at == 17 else xt[at - 1]
            tiles.append(roll(tile, 2 * k + 1))
        side = roll(halos, -4 * b)
        solved = solve(window(lane, tiles, lambda j, side=side: side), ff[b, 0])
        p0[2 * b] = solved[:, :128]
        p0[2 * b + 1] = solved[:, 128:]

    for d in range(1, 8):
        to_z(d, (z + 8 - d) % 8).wait_recv()
    local[9].wait()
    down = [roll(zb5[i + 1], -32) if i < 8 else nothing8 for i in range(0, 10, 2)]
    rise = [nothing8] + [roll(zb5[i + 1], 32) for i in range(1, 8, 2)]
    flat = [
        jnp.where(lane8 < 96, down[j], down[j + 1]) + jnp.where(lane8 >= 32, rise[j + 1], rise[j]) for j in range(4)
    ]
    solved = solve(jnp.concatenate(flat, axis=1), ci[...])
    p5[0] = nothing8
    p5[5] = nothing8
    for j in range(4):
        p5[j + 1] = solved[:, 128 * j : 128 * j + 128]
    odd = z % 2
    lead = (z + odd) // 2
    edge = 32 + 64 * odd
    rb5[x] = jnp.where(lane8 < edge, roll(p5[lead], edge), roll(p5[lead + 1], edge))

    def to_chip5(d, me):
        peer = (me + d) % 4
        return send(rb5.at[me], rb5.at[me], r5send.at[d - 1], r5recv.at[me], px=px, py=2 * peer + core)

    for d in (2, 1, 3):
        begin(to_chip5(d, x))

    got_rows(*h_refs)
    for d in (-1, 0, 1):

        @pl.when(diag[1 + d])
        def _(d=d):
            send(cs, cb.at[1 + d], esend.at[1 + d], erecv.at[1 + d], px=px + d, py=beside).wait_recv()

    local[6].wait()
    local[11].wait()
    one = [hb[0]] + one + [hb[1]]
    at_lane = 127 * (1 - core)
    for r in range(10):
        source, from_lane = (0, 7) if r == 0 else (2, 0) if r == 9 else (1, r - 1)
        one[r] = jnp.where(lane == at_lane, roll(cb[source], (at_lane - from_lane + 128) % 128), one[r])
    one = lifted(one, up[0:128, :])
    for d in range(1, 4):
        to_chip(d, (x + 4 - d) % 4).wait_recv()
    back = [rb[:, t].reshape(32, 128) for t in range(4)]
    two = [only(jnp.logical_and(lane >= 42 * u, lane < 42 * u + 34), back[h]) for h in range(2) for u in range(3)]
    three = [only((lane // 32) == s, back[2]) for s in range(4)]
    four = [
        only(jnp.logical_and(lane >= 64 * h + 10 * b, lane < 64 * h + 10 * b + 10), back[3])
        for b in range(4)
        for h in range(2)
    ]
    two = lifted(two, near[0:128, :])
    three = lifted(three, near[128:256, :])
    four = lifted(four, near[256:384, :])
    local[5].wait()
    terms = one + two + three + four
    for f in range(16):
        total = p0[f]
        for r in range(28):
            if up_used[r][f]:
                total = total + uw[r // 8, 16 * (r % 8) + f] * terms[r]
        acc[f] = total

    for d in range(1, 4):
        to_chip5(d, (x + 4 - d) % 4).wait_recv()
    five = rb5[...].reshape(32, 128)
    full = jnp.concatenate([only((lane // 32) == s, five) for s in range(4)], axis=0)
    top = full.astype(BF)
    rest = (full - top.astype(F32)).astype(BF)
    product = jnp.dot(jnp.concatenate([top, rest], axis=0), up[128:256, :], preferred_element_type=F32)
    product = product[:128] + product[128:] + jnp.dot(top, up[256:384, :], preferred_element_type=F32)
    for f in range(16):
        total = acc[f]
        for s in range(4):
            if up_used[28 + s][f]:
                total = total + uw[3, 16 * (4 + s) + f] * product[32 * s : 32 * s + 32]
        out_ref[pl.ds(f, 32, stride=16), :] = total

    for copy in sent:
        copy.wait_send()
    for refs in (b_refs, g_refs, h2_refs, h_refs):
        sent_rows(*refs)

    @pl.when(has_beside)
    def _():
        edge_copy(0, py, beside).wait_send()
        edge_copy(1, py, beyond).wait_send()

    @pl.when(z > 0)
    def _():
        z4_down().wait_send()

    @pl.when(z < 7)
    def _():
        z4_up().wait_send()

    for d in (-1, 0, 1):

        @pl.when(diag[1 + d])
        def _(d=d):
            to_side(d).wait_send()


def per_device(residual, fine, one, two, three, four, inverse):
    weights, down_b, up, near, down_used, up_used = tables()

    def tiles(*lead):
        return pltpu.VMEM(lead + (32, 128), F32)

    def small(*lead):
        return pltpu.VMEM(lead + (8, 128), F32)

    dma = pltpu.SemaphoreType.DMA
    out = pl.pallas_call(
        functools.partial(kernel, down_used, up_used),
        out_shape=jax.ShapeDtypeStruct((512, 128), F32),
        in_specs=[pl.BlockSpec(memory_space=pltpu.HBM)] * 11,
        out_specs=pl.BlockSpec(memory_space=pltpu.VMEM),
        scratch_shapes=[
            pltpu.VMEM((512, 128), F32),
            pltpu.VMEM((8, 1, 520, 256), BF),
            pltpu.VMEM((4, 520, 256), BF),
            pltpu.VMEM((2, 2, 520, 256), BF),
            pltpu.VMEM((520, 256), BF),
            pltpu.VMEM((4, 264, 128), BF),
            pltpu.VMEM((512, 512), BF),
            pltpu.VMEM((144, 128), F32),
            pltpu.SMEM((8, 128), F32),
            pltpu.VMEM((256, 512), BF),
            pltpu.VMEM((128, 128), BF),
            pltpu.VMEM((384, 128), BF),
            pltpu.VMEM((384, 128), BF),
            tiles(16),
            pltpu.VMEM((512, 512), F32),
            tiles(8),
            tiles(2, 3),
            tiles(2, 3),
            tiles(10, 2),
            tiles(2, 5),
            tiles(2),
            tiles(2),
            tiles(),
            tiles(3),
            tiles(16),
            tiles(16),
            small(4, 3),
            small(8),
            small(8, 3),
            small(4),
            small(4, 3),
            small(10),
            small(3),
            small(2, 3),
            small(2, 6),
            small(2, 6),
            small(2, 3),
            small(2, 3),
            small(4, 4),
            small(4, 4),
            small(4),
            small(6),
            dma((20,)),
        ]
        + [
            dma if n == 0 else dma((n,))
            for n in (7, 8, 7, 8, 2, 2, 3, 8, 0, 0, 3, 4, 3, 4, 7, 8, 2, 2, 2, 2, 3, 3, 2, 2, 2, 2, 3, 4, 3, 4)
        ]
        + [pltpu.SemaphoreType.REGULAR((3,))],
        compiler_params=pltpu.CompilerParams(
            collective_id=0, has_side_effects=True, vmem_limit_bytes=56147968
        ),
    )(
        residual.reshape(512, 128), fine, one, two, three, four, inverse,
        jnp.asarray(weights), jnp.asarray(down_b), jnp.asarray(up), jnp.asarray(near),
    )
    return out.reshape(32, 16, 128)


def solution(mesh):
    placed = (
        P(None, "px", "py"),
        P("px", "py", None, None),
        P("px", None, None, None),
        P("px", None, None, None),
        P("px", None, None, None),
        P(),
        P(),
    )
    return jax.shard_map(
        per_device, mesh=mesh, in_specs=placed, out_specs=P(None, "px", "py"), check_vma=False
    )
```

```python
import functools

import jax
import jax.numpy as jnp
import numpy as np
from jax import lax
from jax.experimental import pallas as pl
from jax.experimental.pallas import tpu as pltpu
from jax.sharding import PartitionSpec as P

F32 = jnp.float32
BF = jnp.bfloat16
MESH = pl.DeviceIdType.MESH
LANES_FOUR = (6, 16, 38)
ROWS_TWO = ((0, 1, 2), (4, 5, 3))
GROUP_OF = (0, 1, 2, 2, 3, 3, 3, 3, 3)


def composites(count):
    found, now = [], np.eye(count)
    for _ in range(5):
        fine = now.shape[0]
        step = np.zeros((fine // 2, fine))
        for i in range(fine // 2):
            for shift, tap in ((-1, 1), (0, 3), (1, 3), (2, 1)):
                if 0 <= 2 * i + shift < fine:
                    step[i, 2 * i + shift] = tap
        now = step @ now
        found.append(now)
    return found


def pick(matrix, row, low, count):
    if 0 <= row < matrix.shape[0]:
        return matrix[row, low : low + count]
    return np.zeros(count)


def edge_lanes(row):
    slot, first, count = ((0, 0, 2), (1, 2, 3), (3, 5, 3), (2, 8, 2))[(row >= 2) + (row >= 5) + (row >= 8)]
    base = 32 * slot + 18 + 2 * (row - first)
    return base, base + 2 * count


def down_rows(rows, px):
    z, low = px // 4, 16 * px
    a1, a2, a3, a4, a5 = (m / 20.0 ** (i + 1) for i, m in enumerate(rows))
    w = np.zeros((9, 16, 128))
    for s in range(4):
        w[0, :, 32 * s : 32 * s + 6] = pick(a5, 2 * z - 1 + s, low, 16)[:, None]
        w[1, :, 32 * s : 32 * s + 18] = pick(a3, 2 * px - 1 + s, low, 16)[:, None]
    for m, at in enumerate(LANES_FOUR):
        for h in range(2):
            w[0, :, at + 64 * h : at + 64 * h + 10] = pick(a4, 4 * z - 1 + 2 * m + h, low, 16)[:, None]
    for e in range(16):
        w[0, e // 2, 48 + e] = 1.0
        w[0, 8 + e // 2, 112 + e] = 1.0
    for r in range(10):
        for at in edge_lanes(r):
            w[1, :, at : at + 2] = pick(a1, 8 * px - 1 + r, low, 16)[:, None]
    for half in range(2):
        for u in range(3):
            w[2 + half, :, 42 * u : 42 * u + 34] = pick(a2, 4 * px - 1 + ROWS_TWO[half][u], low, 16)[:, None]
    for m in range(5):
        for h in range(2):
            w[4 + m, :, 64 * h : 64 * h + 64] = pick(a1, 8 * px - 1 + 2 * m + h, low, 16)[:, None]
    return w


def down_columns(columns, py):
    b1, b2, b3, b4, b5 = columns
    low = 128 * py
    b = np.zeros((128, 512))
    for s in range(4):
        for c in range(6):
            b[:, 32 * s + c] = pick(b5, 4 * py - 1 + c, low, 128)
        for c in range(18):
            b[:, 128 + 32 * s + c] = pick(b3, 16 * py - 1 + c, low, 128)
    for at in LANES_FOUR:
        for c in range(10):
            b[:, at + c] = b[:, at + 64 + c] = pick(b4, 8 * py - 1 + c, low, 128)
    for e in range(16):
        b[0 if e % 2 else 127, 48 + e] = 1.0
        b[0 if e % 2 else 127, 112 + e] = 1.0
    for r in range(10):
        p, q = edge_lanes(r)
        for at, col in ((p, -1), (p + 1, 0), (q, 63), (q + 1, 64)):
            b[:, 128 + at] = pick(b1, 64 * py + col, low, 128)
    for u in range(3):
        for c in range(34):
            b[:, 256 + 42 * u + c] = pick(b2, 32 * py - 1 + c, low, 128)
    for c in range(64):
        b[:, 384 + c] = b[:, 448 + c] = pick(b1, 64 * py + c, low, 128)
    return b


def up_one(columns, py):
    low, tile = 128 * py, 128 * (py // 2)
    one = np.stack([pick(columns[0], tile + c, low, 128) for c in range(128)])
    if py % 2 == 0:
        one[127] = pick(columns[0], tile - 1, low, 128)
    else:
        one[0] = pick(columns[0], tile + 128, low, 128)
    return one, np.stack([pick(columns[4], c % 32, low, 128) for c in range(128)])


def up_near(columns, py):
    low = 128 * py
    two, three, four = (np.zeros((128, 128)) for _ in range(3))
    for u in range(3):
        for c in range(34):
            two[42 * u + c] = pick(columns[1], 32 * py - 1 + c, low, 128)
    for s in range(4):
        for c in range(18):
            three[32 * s + c] = pick(columns[2], 16 * py - 1 + c, low, 128)
        for c in range(10):
            four[10 * s + c] = four[64 + 10 * s + c] = pick(columns[3], 8 * py - 1 + c, low, 128)
    return np.concatenate([two, three, four])


def up_rows(rows, px):
    z, low = px // 4, 16 * px
    w = np.zeros((32, 16))
    firsts = ((0, 10, 8 * px - 1), (10, 6, 4 * px - 1), (16, 4, 2 * px - 1), (20, 8, 4 * z - 2), (28, 4, 2 * z - 1))
    for level, (at, count, first) in enumerate(firsts):
        for i in range(count):
            w[at + i] = pick(rows[level], first + i, low, 16) / 20.0 ** (level + 1)
    return w


def split(matrix):
    high = matrix.astype(BF)
    return high, (matrix - high.astype(np.float64)).astype(BF)


@functools.cache
def tables():
    rows, columns = composites(512), composites(1024)
    some = (12, 13, 14, 15, 0, 31)
    down_w = np.stack([down_rows(rows, px) for px in some])
    up_w = np.stack([up_rows(rows, px) for px in some])
    down_b, near = [], []
    for py in (0, 3, 7):
        high, low = split(down_columns(columns, py))
        down_b.append(np.concatenate([high, low[:, :128]], axis=1))
        near.append(up_near(columns, py).astype(BF))
    up = []
    for py in range(8):
        one, five = up_one(columns, py)
        high, low = split(five)
        up.append(np.concatenate([one.astype(BF), high, low]))
    weights = [down_w.reshape(6, 144, 128), np.pad(up_w.reshape(6, 4, 128), ((0, 0), (0, 4), (0, 0)))]
    return (
        np.concatenate(weights, axis=1).astype(np.float32),
        np.stack(down_b),
        np.stack(up),
        np.stack(near),
        (down_w != 0).any(axis=(0, 3)).tolist(),
        (up_w != 0).any(axis=0).tolist(),
    )


def kernel(
    down_used, up_used,
    res_hbm, ff_hbm, f1_hbm, f2_hbm, f3_hbm, f4_hbm, ci_hbm, w_hbm, db_hbm, up_hbm, near_hbm,
    out_ref,
    res, ff, f1, f2, f3, f4, ci, dw, uw, db, db5, up, near,
    xt, yy, own, sb, pb, eb, xm, hs, hb, cs, cb, p0, acc,
    abuf, a5, a3, yb5, yb4, zb5, f4own, zb4, gs, gb, ns, nb, rs, rb, rb5, p5,
    lsem, a5send, a5recv, a3send, a3recv, bsend, brecv, dsend, drecv, msend, mrecv, y5send, y5recv, y4send, y4recv,
    z5send, z5recv, z4send, z4recv, hsend, hrecv, esend, erecv, gsend, grecv, nsend, nrecv, rsend, rrecv, r5send, r5recv, zs,
):
    px, py = lax.axis_index("px"), lax.axis_index("py")
    z, y = px // 4, px % 4
    x, core = py // 2, py % 2
    has_left, has_right = px > 0, px < 31
    step = 2 * core - 1
    has_beside = jnp.logical_and(py + step >= 0, py + step < 8)
    beside = jnp.clip(py + step, 0, 7)
    beyond = jnp.clip(py + 2 * step, 0, 7)
    has_behind = jnp.logical_and(py - 2 * step >= 0, py - 2 * step < 8)
    behind = jnp.clip(py - 2 * step, 0, 7)
    partner = py + 1 - 2 * core
    variant = jnp.where(px == 0, 4, jnp.where(px == 31, 5, y))
    place = jnp.where(py == 0, 0, jnp.where(py == 7, 2, 1))
    lane = lax.broadcasted_iota(jnp.int32, (32, 128), 1)
    lane8 = lax.broadcasted_iota(jnp.int32, (8, 128), 1)

    def roll(tile, shift):
        if isinstance(shift, int):
            shift %= 128
            return tile if shift == 0 else pltpu.roll(tile, shift, 1)
        return pltpu.roll(tile, shift, 1)

    def only(mask, tile):
        return jnp.where(mask, tile, 0.0)

    barrier = pltpu.get_barrier_semaphore()

    def greet(**where):
        pl.semaphore_signal(barrier, inc=1, device_id=where, device_id_type=MESH)

    for d in (1, 7):
        greet(px=((z + d) % 8) * 4 + y, py=py)

    local = [
        (res_hbm, res),
        (db_hbm.at[place, :, pl.ds(0, 512)], db.at[pl.ds(0, 128)]),
        (db_hbm.at[place, :, pl.ds(0, 512)], db.at[pl.ds(128, 128)]),
        (db_hbm.at[place, :, pl.ds(512, 128)], db5),
        (w_hbm.at[variant, pl.ds(0, 144)], dw),
        (w_hbm.at[variant, pl.ds(144, 8)], uw),
        (up_hbm.at[py], up),
        (f3_hbm.at[0, 0], f3),
        (f2_hbm, f2),
        (ci_hbm, ci),
        (ff_hbm, ff),
        (near_hbm.at[place], near),
    ]
    local += [(f1_hbm.at[b, x], f1.at[b]) for b in range(4)]
    local += [(f4_hbm.at[jnp.clip(2 * z - 1 + b, 0, 15), 0], f4.at[b]) for b in range(4)]
    local = [pltpu.make_async_copy(s, d, lsem.at[i]) for i, (s, d) in enumerate(local)]
    for copy in local[:5]:
        copy.start()

    for d in (4, 3, 5, 2, 6, 1, 7):
        greet(px=px, py=(py + d) % 8)
    for d in range(1, 4):
        greet(px=z * 4 + (y + d) % 4, py=py)
    left_diagonal = jnp.logical_and(has_left, has_beside)
    right_diagonal = jnp.logical_and(has_right, has_beside)

    @pl.when(has_left)
    def _():
        greet(px=px - 1, py=py)

    @pl.when(has_right)
    def _():
        greet(px=px + 1, py=py)

    def send(src, dst, ssem, rsem, **where):
        return pltpu.make_async_remote_copy(
            src_ref=src, dst_ref=dst, send_sem=ssem, recv_sem=rsem, device_id=where, device_id_type=MESH
        )

    nothing = jnp.zeros((32, 128), F32)
    nothing8 = jnp.zeros((8, 128), F32)
    for end in (0, 9):
        zb5[end] = nothing8
        for i in range(2):
            eb[end, i] = nothing

    for side, missing in ((0, px == 0), (1, px == 31)):

        @pl.when(missing)
        def _(side=side):
            for i in range(3):
                pb[side, i] = nothing
            for i in range(4):
                nb[side, i] = nothing8
            hb[side] = nothing
            for i in range(6):
                gb[side, i] = nothing8

    for side, missing in ((0, z == 0), (1, z == 7)):

        @pl.when(missing)
        def _(side=side):
            for i in range(3):
                zb4[side, i] = nothing8

    diag = (left_diagonal, has_beside, right_diagonal)
    for i in range(3):

        @pl.when(jnp.logical_not(diag[i]))
        def _(i=i):
            cb[i] = nothing

    local[0].wait()
    for f in range(16):
        xt[f] = res[pl.ds(f, 32, stride=16), :]
    rows = xt[...].reshape(512, 128)
    high = rows.astype(BF)
    low = (rows - high.astype(F32)).astype(BF)
    both = jnp.concatenate([high, low], axis=1)
    for i in range(1, 5):
        local[i].wait()
    yy[:, :256] = jnp.dot(both, db[:, :256], preferred_element_type=F32)
    yy[:, :128] += jnp.dot(high, db5[...], preferred_element_type=F32)

    def packed(t):
        at = 128 * GROUP_OF[t]
        total = None
        for f in range(16):
            if down_used[t][f]:
                term = yy[32 * f : 32 * f + 32, at : at + 128] * dw[16 * t + f : 16 * t + f + 1, :]
                total = term if total is None else total + term
        return total

    eb[py + 1, 0] = packed(0)
    a5[py] = eb[py + 1, 0, pl.ds(pl.multiple_of(8 * x, 8), 8), :]
    pl.semaphore_wait(
        barrier,
        12 + jnp.where(has_left, 1, 0) + jnp.where(has_right, 1, 0),
    )

    def pass_on(i):
        for d in (1, 7):
            peer = {"px": ((z + d) % 8) * 4 + y, "py": py}
            pl.semaphore_signal(zs.at[i], inc=1, device_id=peer, device_id_type=MESH)

    sent = []

    def begin(copy):
        copy.start()
        sent.append(copy)

    FAR = (4, 3, 5, 2, 6, 1, 7)

    def to_five(d, me):
        peer = (me + d) % 8
        group = pl.multiple_of(8 * (peer // 2), 8)
        return send(eb.at[py + 1, 0, pl.ds(group, 8)], a5.at[me], a5send.at[d - 1], a5recv.at[me], px=px, py=peer)

    def to_three(d, me):
        peer = (me + d) % 8
        return send(abuf.at[peer // 2], a3.at[me], a3send.at[d - 1], a3recv.at[me], px=px, py=peer)

    for d in FAR:
        begin(to_five(d, py))
    pass_on(0)
    for copy in local[5:]:
        copy.start()

    yy[:, 256:] = jnp.dot(both, db[:, 256:], preferred_element_type=F32)
    for t in range(1, 4):
        tile = packed(t)
        own[t - 1] = tile
        for c in range(4):
            abuf[c, t - 1] = tile[8 * c : 8 * c + 8]
    a3[py] = abuf[x]
    for d in FAR:
        begin(to_three(d, py))
    pl.semaphore_wait(zs.at[0], 2)
    pass_on(1)
    for t in range(4, 9):
        own[t - 1] = packed(t)
    sb[0, 0] = own[0]
    sb[1, 0] = own[0]
    sb[0, 1] = own[3]
    sb[1, 1] = own[7]
    sb[0, 2] = xt[0]
    sb[1, 2] = xt[15]

    def left_copy(src, dst, ssem, rsem):
        return send(src.at[0], dst.at[1], ssem.at[0], rsem.at[1], px=px - 1, py=py)

    def right_copy(src, dst, ssem, rsem):
        return send(src.at[1], dst.at[0], ssem.at[1], rsem.at[0], px=px + 1, py=py)

    def start_rows(*refs):
        @pl.when(has_left)
        def _():
            left_copy(*refs).start()

        @pl.when(has_right)
        def _():
            right_copy(*refs).start()

    def got_rows(src, dst, ssem, rsem):
        @pl.when(has_left)
        def _():
            send(src.at[1], dst.at[0], ssem.at[1], rsem.at[0], px=px - 1, py=py).wait_recv()

        @pl.when(has_right)
        def _():
            send(src.at[0], dst.at[1], ssem.at[0], rsem.at[1], px=px + 1, py=py).wait_recv()

    def sent_rows(*refs):
        @pl.when(has_left)
        def _():
            left_copy(*refs).wait_send()

        @pl.when(has_right)
        def _():
            right_copy(*refs).wait_send()

    b_refs = (sb, pb, bsend, brecv)
    start_rows(*b_refs)
    pl.semaphore_wait(zs.at[1], 2)
    pass_on(2)

    for d in range(1, 8):
        to_five(d, (py + 8 - d) % 8).wait_recv()
    five, fours = None, [None] * 3
    for p in range(8):
        tile = a5[p]
        term = only(((lane8 - 4 * p + 1) & 31) < 6, roll(tile, 4 * p - 1))
        five = term if five is None else five + term
        close = ((lane8 - 8 * p + 1) & 63) < 10
        for m in range(3):
            term = only(close, roll(tile, 8 * p - 1 - LANES_FOUR[m]))
            fours[m] = term if fours[m] is None else fours[m] + term
    yb5[y] = five
    for m in range(3):
        yb4[y, m] = fours[m]

    def to_y(buffer, ssem, rsem, d, slot):
        return send(buffer.at[slot], buffer.at[slot], ssem.at[d - 1], rsem.at[slot], px=z * 4 + (y + d) % 4, py=py)

    for d in (2, 1, 3):
        begin(to_y(yb5, y5send, y5recv, d, y))
    for d in (2, 1, 3):
        begin(to_y(yb4, y4send, y4recv, d, y))

    for d in range(1, 8):
        to_three(d, (py + 8 - d) % 8).wait_recv()
    rows_three = []
    for s in range(4):
        total = None
        for p in range(8):
            close = jnp.logical_and(lane8 >= 16 * p - 1, lane8 <= 16 * p + 16)
            term = only(close, roll(a3[p, 0], 16 * p - 1 - 32 * s))
            total = term if total is None else total + term
        rows_three.append(total)
    rows_two = []
    for r in range(6):
        half, u = next((h, ROWS_TWO[h].index(r)) for h in range(2) if r in ROWS_TWO[h])
        pair = [None, None]
        for p in range(8):
            turned = roll(a3[p, 1 + half], 32 * p - 1 - 42 * u)
            first = 32 * (p % 4) - 1
            close = jnp.logical_and(lane8 >= first, lane8 <= first + 33)
            term = only(close, turned)
            pair[p // 4] = term if pair[p // 4] is None else pair[p // 4] + term
            if p == 3:
                pair[1] = only(lane8 == 0, turned)
            if p == 4:
                pair[0] = pair[0] + only(lane8 == 127, turned)
        rows_two.append(pair)
    for side in range(2):
        for i in range(2):
            gs[side, i] = rows_three[2 * side + i]
            for t in range(2):
                gs[side, 2 + 2 * i + t] = rows_two[4 * side + i][t]
    g_refs = (gs, gb, gsend, grecv)
    start_rows(*g_refs)

    got_rows(*b_refs)
    mine = own[0]
    across = jnp.where(lane < 64, roll(pb[0, 0], 64), roll(pb[1, 0], 64))
    inside = jnp.logical_or((lane & 63) < 50, (lane & 63) > 61)
    mine = mine + only(inside, across)
    corner = jnp.where(lane < 28, roll(pb[0, 2], 27), roll(pb[1, 2], 29))
    eb[py + 1, 1] = jnp.where(jnp.logical_and(lane >= 26, lane < 30), corner, mine)
    xm[core, 0] = own[3] + pb[0, 1]
    for m in range(1, 4):
        xm[core, m] = own[3 + m]
    xm[core, 4] = own[7] + pb[1, 1]

    def to_partner(slot):
        return send(xm.at[slot], xm.at[slot], msend, mrecv, px=px, py=partner)

    def edge_copy(i, slot, peer):
        return send(eb.at[slot + 1], eb.at[slot + 1], dsend.at[i], drecv.at[slot], px=px, py=peer)

    @pl.when(has_beside)
    def _():
        edge_copy(0, py, beside).start()
        edge_copy(1, py, beyond).start()

    begin(edge_copy(2, py, partner))
    begin(to_partner(core))

    for d in range(1, 4):
        to_y(yb5, y5send, y5recv, d, (y + 4 - d) % 4).wait_recv()
    zb5[z + 1] = (yb5[0] + yb5[1]) + (yb5[2] + yb5[3])

    def to_z(d, slot):
        return send(zb5.at[slot + 1], zb5.at[slot + 1], z5send.at[d - 1], z5recv.at[slot], px=((z + d) % 8) * 4 + y, py=py)

    pl.semaphore_wait(zs.at[2], 2)
    for d in FAR:
        begin(to_z(d, z))
    for d in range(1, 4):
        to_y(yb4, y4send, y4recv, d, (y + 4 - d) % 4).wait_recv()
    for m in range(3):
        f4own[m] = (yb4[0, m] + yb4[1, m]) + (yb4[2, m] + yb4[3, m])

    def z4_down():
        return send(f4own, zb4.at[1], z4send.at[0], z4recv.at[1], px=px - 4, py=py)

    def z4_up():
        return send(f4own, zb4.at[0], z4send.at[1], z4recv.at[0], px=px + 4, py=py)

    @pl.when(z > 0)
    def _():
        z4_down().start()

    @pl.when(z < 7)
    def _():
        z4_up().start()

    def solve(windows, factor):
        return jnp.dot(windows.astype(BF), factor, preferred_element_type=F32)

    def window(at, shifted, halo):
        parts = [jnp.where(at == 0, halo(0), shifted[0])]
        for j in range(1, 4):
            parts.append(jnp.where(at <= 2 * j - 2, shifted[j - 1], jnp.where(at <= 2 * j, halo(j), shifted[j])))
        last = jnp.where(at <= 6, shifted[3], halo(4))
        return jnp.concatenate(parts + [last[:, :8]], axis=1)

    def lifted(tiles, table):
        count = 32 * len(tiles)
        fine = jnp.concatenate(tiles, axis=0)
        top = fine.astype(BF)
        rest = (fine - top.astype(F32)).astype(BF)
        product = jnp.dot(jnp.concatenate([top, rest], axis=0), table, preferred_element_type=F32)
        product = product[:count] + product[count:]
        return [product[32 * i : 32 * i + 32] for i in range(len(tiles))]

    got_rows(*g_refs)
    for side in range(2):
        for i in range(2):
            rows_three[2 * side + i] = rows_three[2 * side + i] + gb[side, i]
            rows_two[4 * side + i] = [rows_two[4 * side + i][t] + gb[side, 2 + 2 * i + t] for t in range(2)]
    local[7].wait()
    shifted = [roll(rows_three[k], 2 * k + 1) for k in range(4)]
    solved = solve(window(lane8, shifted, lambda j: nothing8), f3[...])
    three = [solved[:, :128], solved[:, 128:]]
    local[8].wait()
    two = []
    for b in range(2):
        turned = [[roll(rows_two[2 * b + k][t], 2 * k + 1) for k in range(4)] for t in range(2)]

        def right_of(j, turned=turned):
            return only(lane8 == 2 * j - 1, turned[1][j - 1]) if j > 0 else nothing8

        def left_of(j, turned=turned):
            return only(lane8 == 2 * j, turned[0][j]) if j < 4 else nothing8

        left_tile = solve(window(lane8, turned[0], right_of), f2[b, 0])
        right_tile = solve(window(lane8, turned[1], left_of), f2[b, 1])
        for h in range(2):
            at = slice(128 * h, 128 * h + 128)
            two.append((left_tile[:, at], right_tile[:, at]))

    def moved(tile, c, shift, width):
        return roll(tile, (shift + 1 - width * 2 * c + 512 - width * core) % 128)

    def moved_two(row, c, shift):
        tile = row[c // 2]
        if c == 1:
            tile = jnp.where(lane8 == 0, row[1], row[0])
        if c == 2:
            tile = jnp.where(lane8 == 127, row[0], row[1])
        return moved(tile, c, shift, 32)

    for side in range(2):
        for c in range(4):
            ns[side, c] = jnp.where(lane8 < 64, moved_two(two[3 * side], c, 0), moved(three[side], c, 64, 16))

    def to_near(side, c, me):
        return send(
            ns.at[side, c], nb.at[1 - side, me], nsend.at[side, c], nrecv.at[1 - side, me],
            px=px + 2 * side - 1, py=2 * c + core,
        )

    for side, there in ((0, has_left), (1, has_right)):

        @pl.when(there)
        def _(side=side):
            for c in range(4):
                to_near(side, c, x).start()

    edge_copy(2, partner, partner).wait_recv()

    @pl.when(has_beside)
    def _():
        edge_copy(0, beside, beside).wait_recv()

    @pl.when(has_behind)
    def _():
        edge_copy(1, behind, behind).wait_recv()

    to_partner(1 - core).wait_recv()
    left_edge, first_edge, second_edge, right_edge = (eb[2 * x + i, 1] for i in range(4))
    even = (lane & 1) == 0

    def edges(n):
        mid = jnp.where(even, second_edge, roll(first_edge, -n))
        outer = jnp.where(even, right_edge, roll(left_edge, -n))
        halo = jnp.where(even, first_edge + roll(left_edge, -n), right_edge + roll(second_edge, -n))
        return mid, outer, halo

    edges_of = {2: edges(4), 3: edges(6)}
    rows_one = []
    for r in range(10):
        m, h = divmod(r, 2)
        if h == 0:
            main = jnp.where(lane < 64, xm[0, m], roll(xm[1, m], 64))
        else:
            main = jnp.where(lane < 64, roll(xm[0, m], 64), xm[1, m])
        at, last = edge_lanes(r)
        mid, outer, _ = edges_of[(last - at) // 2]
        main = main + only(jnp.logical_or(lane == 63, lane == 64), roll(mid, 63 - at))
        main = main + only(jnp.logical_or(lane == 127, lane == 0), roll(outer, 127 - at))
        rows_one.append(main)
    halo_two, halo_three = edges_of[2][2], edges_of[3][2]
    halos = jnp.where(
        lane < 4,
        roll(halo_two, -18),
        jnp.where(lane < 10, roll(halo_three, -46), jnp.where(lane < 16, roll(halo_three, -104), roll(halo_two, -66))),
    )
    one = []
    for b in range(4):
        local[12 + b].wait()
        turned = [roll(rows_one[2 * b + k], 2 * k + 1) for k in range(4)]
        side = roll(halos, -4 * b)
        solved = solve(window(lane, turned, lambda j, side=side: side), f1[b])
        one += [solved[:, :128], solved[:, 128:]]
    hs[0] = one[0]
    hs[1] = one[7]
    h_refs = (hs, hb, hsend, hrecv)
    start_rows(*h_refs)
    column = nothing
    for r in range(8):
        column = jnp.where(lane == r, roll(one[r], r + core), column)
    cs[...] = column

    def to_side(d):
        return send(cs, cb.at[1 - d], esend.at[1 - d], erecv.at[1 - d], px=px + d, py=beside)

    for d in (-1, 1, 0):

        @pl.when(diag[1 + d])
        def _(d=d):
            to_side(d).start()

    @pl.when(z > 0)
    def _():
        send(f4own, zb4.at[0], z4send.at[1], z4recv.at[0], px=px - 4, py=py).wait_recv()

    @pl.when(z < 7)
    def _():
        send(f4own, zb4.at[1], z4send.at[0], z4recv.at[1], px=px + 4, py=py).wait_recv()

    quads = (zb4[0, 1], zb4[0, 2] + f4own[0], f4own[1], f4own[2] + zb4[1, 0], zb4[1, 1])
    four = []
    for b in range(4):
        local[16 + b].wait()
        first, second = quads[b], quads[b + 1]
        v0 = jnp.where(
            lane8 <= 64,
            only(lane8 >= 1, roll(first, 1)),
            only(lane8 >= 67, roll(first, 3)),
        )
        v1 = jnp.where(
            lane8 <= 2,
            roll(first, 3),
            jnp.where(lane8 <= 68, only(lane8 >= 5, roll(second, 5)), only(lane8 >= 71, roll(second, 7))),
        )
        v2 = only(lane8 <= 6, roll(second, 7))
        four.append(solve(jnp.concatenate([v0, v1, v2[:, :8]], axis=1), f4[b]))

    for c in range(4):
        pieces = [moved_two(two[u], c, 42 * u) for u in range(3)]
        rs[c, 0] = jnp.where(lane8 < 42, pieces[0], jnp.where(lane8 < 84, pieces[1], pieces[2]))
        pieces = [moved(three[s], c, 32 * s + 32, 16) for s in range(2)]
        rs[c, 1] = jnp.where(lane8 < 84, jnp.where(lane8 < 64, pieces[0], pieces[1]), moved_two(two[3], c, 84))
        pieces = [moved(four[b], c, 10 * b, 8) for b in range(4)]
        low_lane = lane8 & 63
        rs[c, 2] = jnp.where(
            low_lane < 20,
            jnp.where(low_lane < 10, pieces[0], pieces[1]),
            jnp.where(low_lane < 30, pieces[2], pieces[3]),
        )
    rb[x] = rs[x]

    def to_chip(d, me):
        peer = (me + d) % 4
        return send(rs.at[peer], rb.at[me], rsend.at[d - 1], rrecv.at[me], px=px, py=2 * peer + core)

    for d in (2, 1, 3):
        begin(to_chip(d, x))

    for d in range(1, 8):
        to_z(d, (z + 8 - d) % 8).wait_recv()
    local[9].wait()
    down = [roll(zb5[i + 1], -32) if i < 8 else nothing8 for i in range(0, 10, 2)]
    rise = [nothing8] + [roll(zb5[i + 1], 32) for i in range(1, 8, 2)]
    flat = [
        jnp.where(lane8 < 96, down[j], down[j + 1]) + jnp.where(lane8 >= 32, rise[j + 1], rise[j]) for j in range(4)
    ]
    solved = solve(jnp.concatenate(flat, axis=1), ci[...])
    p5[0] = nothing8
    p5[5] = nothing8
    for j in range(4):
        p5[j + 1] = solved[:, 128 * j : 128 * j + 128]
    odd = z % 2
    lead = (z + odd) // 2
    edge = 32 + 64 * odd
    rb5[x] = jnp.where(lane8 < edge, roll(p5[lead], edge), roll(p5[lead + 1], edge))

    def to_chip5(d, me):
        peer = (me + d) % 4
        return send(rb5.at[me], rb5.at[me], r5send.at[d - 1], r5recv.at[me], px=px, py=2 * peer + core)

    for d in (2, 1, 3):
        begin(to_chip5(d, x))

    before, after = eb[py, 0], eb[py + 2, 0]
    corner_before, corner_after = eb[py, 1], eb[py + 2, 1]
    facing = jnp.where(even, before, after)
    corners = jnp.where(even, corner_before, corner_after)
    halos = jnp.where(
        lane < 2,
        roll(corners, -26),
        jnp.where(lane < 18, roll(facing, -46), jnp.where(lane < 34, roll(facing, -94), roll(corners, 6))),
    )
    local[10].wait()
    for b in range(8):
        tiles = []
        for k in range(4):
            at = 2 * b + k
            tile = pb[0, 2] if at == 0 else pb[1, 2] if at == 17 else xt[at - 1]
            tiles.append(roll(tile, 2 * k + 1))
        side = roll(halos, -4 * b)
        solved = solve(window(lane, tiles, lambda j, side=side: side), ff[b, 0])
        p0[2 * b] = solved[:, :128]
        p0[2 * b + 1] = solved[:, 128:]

    got_rows(*h_refs)
    for d in (-1, 0, 1):

        @pl.when(diag[1 + d])
        def _(d=d):
            send(cs, cb.at[1 + d], esend.at[1 + d], erecv.at[1 + d], px=px + d, py=beside).wait_recv()

    local[6].wait()
    local[11].wait()
    one = [hb[0]] + one + [hb[1]]
    at_lane = 127 * (1 - core)
    for r in range(10):
        source, from_lane = (0, 7) if r == 0 else (2, 0) if r == 9 else (1, r - 1)
        one[r] = jnp.where(lane == at_lane, roll(cb[source], (at_lane - from_lane + 128) % 128), one[r])
    one = lifted(one, up[0:128, :])
    for d in range(1, 4):
        to_chip(d, (x + 4 - d) % 4).wait_recv()
    for side, there in ((0, has_left), (1, has_right)):

        @pl.when(there)
        def _(side=side):
            for c in range(4):
                to_near(1 - side, x, c).wait_recv()

    back = [rb[:, t].reshape(32, 128) for t in range(3)]
    outer = [nb[side].reshape(32, 128) for side in range(2)]

    def slot(tile, first, count):
        return only(jnp.logical_and(lane >= first, lane < first + count), tile)

    two = [slot(outer[0], 0, 34)] + [slot(back[0], 42 * u, 34) for u in range(3)]
    two += [slot(back[1], 84, 34), slot(outer[1], 0, 34)]
    three = [slot(outer[0], 64, 18), slot(back[1], 32, 18), slot(back[1], 64, 18), slot(outer[1], 64, 18)]
    four = [
        only(jnp.logical_and(lane >= 64 * h + 10 * b, lane < 64 * h + 10 * b + 10), back[2])
        for b in range(4)
        for h in range(2)
    ]
    two = lifted(two, near[0:128, :])
    three = lifted(three, near[128:256, :])
    four = lifted(four, near[256:384, :])
    local[5].wait()
    terms = one + two + three + four
    for f in range(16):
        total = p0[f]
        for r in range(28):
            if up_used[r][f]:
                total = total + uw[r // 8, 16 * (r % 8) + f] * terms[r]
        acc[f] = total

    for d in range(1, 4):
        to_chip5(d, (x + 4 - d) % 4).wait_recv()
    five = rb5[...].reshape(32, 128)
    full = jnp.concatenate([only((lane // 32) == s, five) for s in range(4)], axis=0)
    top = full.astype(BF)
    rest = (full - top.astype(F32)).astype(BF)
    product = jnp.dot(jnp.concatenate([top, rest], axis=0), up[128:256, :], preferred_element_type=F32)
    product = product[:128] + product[128:] + jnp.dot(top, up[256:384, :], preferred_element_type=F32)
    for f in range(16):
        total = acc[f]
        for s in range(4):
            if up_used[28 + s][f]:
                total = total + uw[3, 16 * (4 + s) + f] * product[32 * s : 32 * s + 32]
        out_ref[pl.ds(f, 32, stride=16), :] = total

    for copy in sent:
        copy.wait_send()
    for refs in (b_refs, g_refs, h_refs):
        sent_rows(*refs)

    for side, there in ((0, has_left), (1, has_right)):

        @pl.when(there)
        def _(side=side):
            for c in range(4):
                to_near(side, c, x).wait_send()

    @pl.when(has_beside)
    def _():
        edge_copy(0, py, beside).wait_send()
        edge_copy(1, py, beyond).wait_send()

    @pl.when(z > 0)
    def _():
        z4_down().wait_send()

    @pl.when(z < 7)
    def _():
        z4_up().wait_send()

    for d in (-1, 0, 1):

        @pl.when(diag[1 + d])
        def _(d=d):
            to_side(d).wait_send()


def per_device(residual, fine, one, two, three, four, inverse):
    weights, down_b, up, near, down_used, up_used = tables()

    def tiles(*lead):
        return pltpu.VMEM(lead + (32, 128), F32)

    def small(*lead):
        return pltpu.VMEM(lead + (8, 128), F32)

    dma = pltpu.SemaphoreType.DMA
    out = pl.pallas_call(
        functools.partial(kernel, down_used, up_used),
        out_shape=jax.ShapeDtypeStruct((512, 128), F32),
        in_specs=[pl.BlockSpec(memory_space=pltpu.HBM)] * 11,
        out_specs=pl.BlockSpec(memory_space=pltpu.VMEM),
        scratch_shapes=[
            pltpu.VMEM((512, 128), F32),
            pltpu.VMEM((8, 1, 520, 256), BF),
            pltpu.VMEM((4, 520, 256), BF),
            pltpu.VMEM((2, 2, 520, 256), BF),
            pltpu.VMEM((520, 256), BF),
            pltpu.VMEM((4, 264, 128), BF),
            pltpu.VMEM((512, 512), BF),
            pltpu.VMEM((144, 128), F32),
            pltpu.SMEM((8, 128), F32),
            pltpu.VMEM((256, 512), BF),
            pltpu.VMEM((128, 128), BF),
            pltpu.VMEM((384, 128), BF),
            pltpu.VMEM((384, 128), BF),
            tiles(16),
            pltpu.VMEM((512, 512), F32),
            tiles(8),
            tiles(2, 3),
            tiles(2, 3),
            tiles(10, 2),
            tiles(2, 5),
            tiles(2),
            tiles(2),
            tiles(),
            tiles(3),
            tiles(16),
            tiles(16),
            small(4, 3),
            small(8),
            small(8, 3),
            small(4),
            small(4, 3),
            small(10),
            small(3),
            small(2, 3),
            small(2, 6),
            small(2, 6),
            small(2, 4),
            small(2, 4),
            small(4, 3),
            small(4, 3),
            small(4),
            small(6),
            dma((20,)),
        ]
        + [
            dma if n == 0 else dma(n if isinstance(n, tuple) else (n,))
            for n in (7, 8, 7, 8, 2, 2, 3, 8, 0, 0, 3, 4, 3, 4, 7, 8, 2, 2, 2, 2, 3, 3, 2, 2, (2, 4), (2, 4), 3, 4, 3, 4)
        ]
        + [pltpu.SemaphoreType.REGULAR((3,))],
        compiler_params=pltpu.CompilerParams(
            collective_id=0, has_side_effects=True, vmem_limit_bytes=56147968
        ),
    )(
        residual.reshape(512, 128), fine, one, two, three, four, inverse,
        jnp.asarray(weights), jnp.asarray(down_b), jnp.asarray(up), jnp.asarray(near),
    )
    return out.reshape(32, 16, 128)


def solution(mesh):
    placed = (
        P(None, "px", "py"),
        P("px", "py", None, None),
        P("px", None, None, None),
        P("px", None, None, None),
        P("px", None, None, None),
        P(),
        P(),
    )
    return jax.shard_map(
        per_device, mesh=mesh, in_specs=placed, out_specs=P(None, "px", "py"), check_vma=False
    )
```

```python
import functools

import jax
import jax.numpy as jnp
import numpy as np
from jax import lax
from jax.experimental import pallas as pl
from jax.experimental.pallas import tpu as pltpu
from jax.sharding import PartitionSpec as P

F32 = jnp.float32
BF = jnp.bfloat16
MESH = pl.DeviceIdType.MESH
LANES_FOUR = (6, 16, 38)
ROWS_TWO = ((0, 1, 2), (4, 5, 3))
GROUP_OF = (0, 1, 2, 2, 3, 3, 3, 3, 3)


def composites(count):
    found, now = [], np.eye(count)
    for _ in range(5):
        fine = now.shape[0]
        step = np.zeros((fine // 2, fine))
        for i in range(fine // 2):
            for shift, tap in ((-1, 1), (0, 3), (1, 3), (2, 1)):
                if 0 <= 2 * i + shift < fine:
                    step[i, 2 * i + shift] = tap
        now = step @ now
        found.append(now)
    return found


def pick(matrix, row, low, count):
    if 0 <= row < matrix.shape[0]:
        return matrix[row, low : low + count]
    return np.zeros(count)


def edge_lanes(row):
    slot, first, count = ((0, 0, 2), (1, 2, 3), (3, 5, 3), (2, 8, 2))[(row >= 2) + (row >= 5) + (row >= 8)]
    base = 32 * slot + 18 + 2 * (row - first)
    return base, base + 2 * count


def down_rows(rows, px):
    z, low = px // 4, 16 * px
    a1, a2, a3, a4, a5 = (m / 20.0 ** (i + 1) for i, m in enumerate(rows))
    w = np.zeros((9, 16, 128))
    for s in range(4):
        w[0, :, 32 * s : 32 * s + 6] = pick(a5, 2 * z - 1 + s, low, 16)[:, None]
        w[1, :, 32 * s : 32 * s + 18] = pick(a3, 2 * px - 1 + s, low, 16)[:, None]
    for m, at in enumerate(LANES_FOUR):
        for h in range(2):
            w[0, :, at + 64 * h : at + 64 * h + 10] = pick(a4, 4 * z - 1 + 2 * m + h, low, 16)[:, None]
    for e in range(16):
        w[0, e // 2, 48 + e] = 1.0
        w[0, 8 + e // 2, 112 + e] = 1.0
    for r in range(10):
        for at in edge_lanes(r):
            w[1, :, at : at + 2] = pick(a1, 8 * px - 1 + r, low, 16)[:, None]
    for half in range(2):
        for u in range(3):
            w[2 + half, :, 42 * u : 42 * u + 34] = pick(a2, 4 * px - 1 + ROWS_TWO[half][u], low, 16)[:, None]
    for m in range(5):
        for h in range(2):
            w[4 + m, :, 64 * h : 64 * h + 64] = pick(a1, 8 * px - 1 + 2 * m + h, low, 16)[:, None]
    return w


def down_columns(columns, py):
    b1, b2, b3, b4, b5 = columns
    low = 128 * py
    b = np.zeros((128, 512))
    for s in range(4):
        for c in range(6):
            b[:, 32 * s + c] = pick(b5, 4 * py - 1 + c, low, 128)
        for c in range(18):
            b[:, 128 + 32 * s + c] = pick(b3, 16 * py - 1 + c, low, 128)
    for at in LANES_FOUR:
        for c in range(10):
            b[:, at + c] = b[:, at + 64 + c] = pick(b4, 8 * py - 1 + c, low, 128)
    for e in range(16):
        b[0 if e % 2 else 127, 48 + e] = 1.0
        b[0 if e % 2 else 127, 112 + e] = 1.0
    for r in range(10):
        p, q = edge_lanes(r)
        for at, col in ((p, -1), (p + 1, 0), (q, 63), (q + 1, 64)):
            b[:, 128 + at] = pick(b1, 64 * py + col, low, 128)
    for u in range(3):
        for c in range(34):
            b[:, 256 + 42 * u + c] = pick(b2, 32 * py - 1 + c, low, 128)
    for c in range(64):
        b[:, 384 + c] = b[:, 448 + c] = pick(b1, 64 * py + c, low, 128)
    return b


def up_one(columns, py):
    low, tile = 128 * py, 128 * (py // 2)
    one = np.stack([pick(columns[0], tile + c, low, 128) for c in range(128)])
    if py % 2 == 0:
        one[127] = pick(columns[0], tile - 1, low, 128)
    else:
        one[0] = pick(columns[0], tile + 128, low, 128)
    return one, np.stack([pick(columns[4], c % 32, low, 128) for c in range(128)])


def up_near(columns, py):
    low = 128 * py
    two, three, four = (np.zeros((128, 128)) for _ in range(3))
    for u in range(3):
        for c in range(34):
            two[42 * u + c] = pick(columns[1], 32 * py - 1 + c, low, 128)
    for s in range(4):
        for c in range(18):
            three[32 * s + c] = pick(columns[2], 16 * py - 1 + c, low, 128)
        for c in range(10):
            four[10 * s + c] = four[64 + 10 * s + c] = pick(columns[3], 8 * py - 1 + c, low, 128)
    return np.concatenate([two, three, four])


def up_rows(rows, px):
    z, low = px // 4, 16 * px
    w = np.zeros((32, 16))
    firsts = ((0, 10, 8 * px - 1), (10, 6, 4 * px - 1), (16, 4, 2 * px - 1), (20, 8, 4 * z - 2), (28, 4, 2 * z - 1))
    for level, (at, count, first) in enumerate(firsts):
        for i in range(count):
            w[at + i] = pick(rows[level], first + i, low, 16) / 20.0 ** (level + 1)
    return w


def split(matrix):
    high = matrix.astype(BF)
    return high, (matrix - high.astype(np.float64)).astype(BF)


@functools.cache
def tables():
    rows, columns = composites(512), composites(1024)
    some = (12, 13, 14, 15, 0, 31)
    down_w = np.stack([down_rows(rows, px) for px in some])
    up_w = np.stack([up_rows(rows, px) for px in some])
    down_b, near = [], []
    for py in (0, 3, 7):
        high, low = split(down_columns(columns, py))
        down_b.append(np.concatenate([high, low[:, :128]], axis=1))
        near.append(up_near(columns, py).astype(BF))
    up = []
    for py in range(8):
        one, five = up_one(columns, py)
        high, low = split(five)
        up.append(np.concatenate([one.astype(BF), high, low]))
    weights = [down_w.reshape(6, 144, 128), np.pad(up_w.reshape(6, 4, 128), ((0, 0), (0, 4), (0, 0)))]
    return (
        np.concatenate(weights, axis=1).astype(np.float32),
        np.stack(down_b),
        np.stack(up),
        np.stack(near),
        (down_w != 0).any(axis=(0, 3)).tolist(),
        (up_w != 0).any(axis=0).tolist(),
    )


def kernel(
    down_used, up_used,
    res_hbm, ff_hbm, f1_hbm, f2_hbm, f3_hbm, f4_hbm, ci_hbm, w_hbm, db_hbm, up_hbm, near_hbm,
    out_ref,
    res, ff, f1, f2, f3, f4, ci, dw, uw, db, db5, up, near,
    xt, yy, own, sb, pb, eb, xm, hs, hb, cs, cb, p0, acc,
    abuf, a5, a3, yb5, yb4, zb5, f4own, zb4, gs, gb, ns, nb, rs, rb, rb5, p5,
    lsem, a5send, a5recv, a3send, a3recv, bsend, brecv, dsend, drecv, msend, mrecv, y5send, y5recv, y4send, y4recv,
    z5send, z5recv, z4send, z4recv, hsend, hrecv, esend, erecv, gsend, grecv, nsend, nrecv, rsend, rrecv, r5send, r5recv, zs,
):
    px, py = lax.axis_index("px"), lax.axis_index("py")
    z, y = px // 4, px % 4
    x, core = py // 2, py % 2
    has_left, has_right = px > 0, px < 31
    step = 2 * core - 1
    has_beside = jnp.logical_and(py + step >= 0, py + step < 8)
    beside = jnp.clip(py + step, 0, 7)
    beyond = jnp.clip(py + 2 * step, 0, 7)
    has_behind = jnp.logical_and(py - 2 * step >= 0, py - 2 * step < 8)
    behind = jnp.clip(py - 2 * step, 0, 7)
    partner = py + 1 - 2 * core
    variant = jnp.where(px == 0, 4, jnp.where(px == 31, 5, y))
    place = jnp.where(py == 0, 0, jnp.where(py == 7, 2, 1))
    lane = lax.broadcasted_iota(jnp.int32, (32, 128), 1)
    lane8 = lax.broadcasted_iota(jnp.int32, (8, 128), 1)

    def roll(tile, shift):
        if isinstance(shift, int):
            shift %= 128
            return tile if shift == 0 else pltpu.roll(tile, shift, 1)
        return pltpu.roll(tile, shift, 1)

    def only(mask, tile):
        return jnp.where(mask, tile, 0.0)

    barrier = pltpu.get_barrier_semaphore()

    def greet(**where):
        pl.semaphore_signal(barrier, inc=1, device_id=where, device_id_type=MESH)

    for d in (1, 7):
        greet(px=((z + d) % 8) * 4 + y, py=py)

    local = [
        (res_hbm, res),
        (db_hbm.at[place, :, pl.ds(0, 512)], db.at[pl.ds(0, 128)]),
        (db_hbm.at[place, :, pl.ds(0, 512)], db.at[pl.ds(128, 128)]),
        (db_hbm.at[place, :, pl.ds(512, 128)], db5),
        (w_hbm.at[variant, pl.ds(0, 144)], dw),
        (w_hbm.at[variant, pl.ds(144, 8)], uw),
        (up_hbm.at[py], up),
        (f3_hbm.at[0, 0], f3),
        (f2_hbm, f2),
        (ci_hbm, ci),
        (ff_hbm, ff),
        (near_hbm.at[place], near),
    ]
    local += [(f1_hbm.at[b, x], f1.at[b]) for b in range(4)]
    local += [(f4_hbm.at[jnp.clip(2 * z - 1 + b, 0, 15), 0], f4.at[b]) for b in range(4)]
    local = [pltpu.make_async_copy(s, d, lsem.at[i]) for i, (s, d) in enumerate(local)]
    for copy in local[:5]:
        copy.start()

    for d in (4, 3, 5, 2, 6, 1, 7):
        greet(px=px, py=(py + d) % 8)
    for d in range(1, 4):
        greet(px=z * 4 + (y + d) % 4, py=py)
    left_diagonal = jnp.logical_and(has_left, has_beside)
    right_diagonal = jnp.logical_and(has_right, has_beside)

    @pl.when(has_left)
    def _():
        greet(px=px - 1, py=py)

    @pl.when(has_right)
    def _():
        greet(px=px + 1, py=py)

    def send(src, dst, ssem, rsem, **where):
        return pltpu.make_async_remote_copy(
            src_ref=src, dst_ref=dst, send_sem=ssem, recv_sem=rsem, device_id=where, device_id_type=MESH
        )

    nothing = jnp.zeros((32, 128), F32)
    nothing8 = jnp.zeros((8, 128), F32)
    for end in (0, 9):
        zb5[end] = nothing8
        for i in range(2):
            eb[end, i] = nothing

    for side, missing in ((0, px == 0), (1, px == 31)):

        @pl.when(missing)
        def _(side=side):
            for i in range(3):
                pb[side, i] = nothing
            for i in range(4):
                nb[side, i] = nothing8
            hb[side] = nothing
            for i in range(6):
                gb[side, i] = nothing8

    for side, missing in ((0, z == 0), (1, z == 7)):

        @pl.when(missing)
        def _(side=side):
            for i in range(3):
                zb4[side, i] = nothing8

    diag = (left_diagonal, has_beside, right_diagonal)
    for i in range(3):

        @pl.when(jnp.logical_not(diag[i]))
        def _(i=i):
            cb[i] = nothing

    local[0].wait()
    for f in range(16):
        xt[f] = res[pl.ds(f, 32, stride=16), :]
    rows = xt[...].reshape(512, 128)
    high = rows.astype(BF)
    low = (rows - high.astype(F32)).astype(BF)
    both = jnp.concatenate([high, low], axis=1)
    for i in range(1, 5):
        local[i].wait()
    yy[:, :256] = jnp.dot(both, db[:, :256], preferred_element_type=F32)
    yy[:, :128] += jnp.dot(high, db5[...], preferred_element_type=F32)

    def packed(t):
        at = 128 * GROUP_OF[t]
        total = None
        for f in range(16):
            if down_used[t][f]:
                term = yy[32 * f : 32 * f + 32, at : at + 128] * dw[16 * t + f : 16 * t + f + 1, :]
                total = term if total is None else total + term
        return total

    eb[py + 1, 0] = packed(0)
    a5[py] = eb[py + 1, 0, pl.ds(pl.multiple_of(8 * x, 8), 8), :]
    pl.semaphore_wait(
        barrier,
        12 + jnp.where(has_left, 1, 0) + jnp.where(has_right, 1, 0),
    )

    def pass_on(i):
        for d in (1, 7):
            peer = {"px": ((z + d) % 8) * 4 + y, "py": py}
            pl.semaphore_signal(zs.at[i], inc=1, device_id=peer, device_id_type=MESH)

    sent = []

    def begin(copy):
        copy.start()
        sent.append(copy)

    FAR = (4, 3, 5, 2, 6, 1, 7)

    def to_five(d, me):
        peer = (me + d) % 8
        group = pl.multiple_of(8 * (peer // 2), 8)
        return send(eb.at[py + 1, 0, pl.ds(group, 8)], a5.at[me], a5send.at[d - 1], a5recv.at[me], px=px, py=peer)

    def to_three(d, me):
        peer = (me + d) % 8
        return send(abuf.at[peer // 2], a3.at[me], a3send.at[d - 1], a3recv.at[me], px=px, py=peer)

    for d in FAR:
        begin(to_five(d, py))
    pass_on(0)
    for copy in local[5:]:
        copy.start()

    yy[:, 256:] = jnp.dot(both, db[:, 256:], preferred_element_type=F32)
    for t in range(1, 4):
        tile = packed(t)
        own[t - 1] = tile
        for c in range(4):
            abuf[c, t - 1] = tile[8 * c : 8 * c + 8]
    a3[py] = abuf[x]
    for t in range(4, 9):
        own[t - 1] = packed(t)
    sb[0, 0] = own[0]
    sb[1, 0] = own[0]
    sb[0, 1] = own[3]
    sb[1, 1] = own[7]
    sb[0, 2] = xt[0]
    sb[1, 2] = xt[15]

    def left_copy(src, dst, ssem, rsem):
        return send(src.at[0], dst.at[1], ssem.at[0], rsem.at[1], px=px - 1, py=py)

    def right_copy(src, dst, ssem, rsem):
        return send(src.at[1], dst.at[0], ssem.at[1], rsem.at[0], px=px + 1, py=py)

    def start_rows(*refs):
        @pl.when(has_left)
        def _():
            left_copy(*refs).start()

        @pl.when(has_right)
        def _():
            right_copy(*refs).start()

    def got_rows(src, dst, ssem, rsem):
        @pl.when(has_left)
        def _():
            send(src.at[1], dst.at[0], ssem.at[1], rsem.at[0], px=px - 1, py=py).wait_recv()

        @pl.when(has_right)
        def _():
            send(src.at[0], dst.at[1], ssem.at[0], rsem.at[1], px=px + 1, py=py).wait_recv()

    def sent_rows(*refs):
        @pl.when(has_left)
        def _():
            left_copy(*refs).wait_send()

        @pl.when(has_right)
        def _():
            right_copy(*refs).wait_send()

    b_refs = (sb, pb, bsend, brecv)
    start_rows(*b_refs)
    for d in FAR:
        begin(to_three(d, py))
    pl.semaphore_wait(zs.at[0], 2)
    pass_on(1)
    pl.semaphore_wait(zs.at[1], 2)
    pass_on(2)

    for d in range(1, 8):
        to_five(d, (py + 8 - d) % 8).wait_recv()
    five, fours = None, [None] * 3
    for p in range(8):
        tile = a5[p]
        term = only(((lane8 - 4 * p + 1) & 31) < 6, roll(tile, 4 * p - 1))
        five = term if five is None else five + term
        close = ((lane8 - 8 * p + 1) & 63) < 10
        for m in range(3):
            term = only(close, roll(tile, 8 * p - 1 - LANES_FOUR[m]))
            fours[m] = term if fours[m] is None else fours[m] + term
    yb5[y] = five
    for m in range(3):
        yb4[y, m] = fours[m]

    def to_y(buffer, ssem, rsem, d, slot):
        return send(buffer.at[slot], buffer.at[slot], ssem.at[d - 1], rsem.at[slot], px=z * 4 + (y + d) % 4, py=py)

    for d in (2, 1, 3):
        begin(to_y(yb5, y5send, y5recv, d, y))
    for d in (2, 1, 3):
        begin(to_y(yb4, y4send, y4recv, d, y))

    for d in range(1, 8):
        to_three(d, (py + 8 - d) % 8).wait_recv()
    rows_three = []
    for s in range(4):
        total = None
        for p in range(8):
            close = jnp.logical_and(lane8 >= 16 * p - 1, lane8 <= 16 * p + 16)
            term = only(close, roll(a3[p, 0], 16 * p - 1 - 32 * s))
            total = term if total is None else total + term
        rows_three.append(total)
    rows_two = []
    for r in range(6):
        half, u = next((h, ROWS_TWO[h].index(r)) for h in range(2) if r in ROWS_TWO[h])
        pair = [None, None]
        for p in range(8):
            turned = roll(a3[p, 1 + half], 32 * p - 1 - 42 * u)
            first = 32 * (p % 4) - 1
            close = jnp.logical_and(lane8 >= first, lane8 <= first + 33)
            term = only(close, turned)
            pair[p // 4] = term if pair[p // 4] is None else pair[p // 4] + term
            if p == 3:
                pair[1] = only(lane8 == 0, turned)
            if p == 4:
                pair[0] = pair[0] + only(lane8 == 127, turned)
        rows_two.append(pair)
    for side in range(2):
        for i in range(2):
            gs[side, i] = rows_three[2 * side + i]
            for t in range(2):
                gs[side, 2 + 2 * i + t] = rows_two[4 * side + i][t]
    g_refs = (gs, gb, gsend, grecv)
    start_rows(*g_refs)

    got_rows(*b_refs)
    mine = own[0]
    across = jnp.where(lane < 64, roll(pb[0, 0], 64), roll(pb[1, 0], 64))
    inside = jnp.logical_or((lane & 63) < 50, (lane & 63) > 61)
    mine = mine + only(inside, across)
    corner = jnp.where(lane < 28, roll(pb[0, 2], 27), roll(pb[1, 2], 29))
    eb[py + 1, 1] = jnp.where(jnp.logical_and(lane >= 26, lane < 30), corner, mine)
    xm[core, 0] = own[3] + pb[0, 1]
    for m in range(1, 4):
        xm[core, m] = own[3 + m]
    xm[core, 4] = own[7] + pb[1, 1]

    def to_partner(slot):
        return send(xm.at[slot], xm.at[slot], msend, mrecv, px=px, py=partner)

    def edge_copy(i, slot, peer):
        return send(eb.at[slot + 1], eb.at[slot + 1], dsend.at[i], drecv.at[slot], px=px, py=peer)

    @pl.when(has_beside)
    def _():
        edge_copy(0, py, beside).start()
        edge_copy(1, py, beyond).start()

    begin(edge_copy(2, py, partner))
    begin(to_partner(core))

    for d in range(1, 4):
        to_y(yb5, y5send, y5recv, d, (y + 4 - d) % 4).wait_recv()
    zb5[z + 1] = (yb5[0] + yb5[1]) + (yb5[2] + yb5[3])

    def to_z(d, slot):
        return send(zb5.at[slot + 1], zb5.at[slot + 1], z5send.at[d - 1], z5recv.at[slot], px=((z + d) % 8) * 4 + y, py=py)

    pl.semaphore_wait(zs.at[2], 2)
    for d in FAR:
        begin(to_z(d, z))
    for d in range(1, 4):
        to_y(yb4, y4send, y4recv, d, (y + 4 - d) % 4).wait_recv()
    for m in range(3):
        f4own[m] = (yb4[0, m] + yb4[1, m]) + (yb4[2, m] + yb4[3, m])

    def z4_down():
        return send(f4own, zb4.at[1], z4send.at[0], z4recv.at[1], px=px - 4, py=py)

    def z4_up():
        return send(f4own, zb4.at[0], z4send.at[1], z4recv.at[0], px=px + 4, py=py)

    @pl.when(z > 0)
    def _():
        z4_down().start()

    @pl.when(z < 7)
    def _():
        z4_up().start()

    def solve(windows, factor):
        return jnp.dot(windows.astype(BF), factor, preferred_element_type=F32)

    def window(at, shifted, halo):
        parts = [jnp.where(at == 0, halo(0), shifted[0])]
        for j in range(1, 4):
            parts.append(jnp.where(at <= 2 * j - 2, shifted[j - 1], jnp.where(at <= 2 * j, halo(j), shifted[j])))
        last = jnp.where(at <= 6, shifted[3], halo(4))
        return jnp.concatenate(parts + [last[:, :8]], axis=1)

    def lifted(tiles, table):
        count = 32 * len(tiles)
        fine = jnp.concatenate(tiles, axis=0)
        top = fine.astype(BF)
        rest = (fine - top.astype(F32)).astype(BF)
        product = jnp.dot(jnp.concatenate([top, rest], axis=0), table, preferred_element_type=F32)
        product = product[:count] + product[count:]
        return [product[32 * i : 32 * i + 32] for i in range(len(tiles))]

    got_rows(*g_refs)
    for side in range(2):
        for i in range(2):
            rows_three[2 * side + i] = rows_three[2 * side + i] + gb[side, i]
            rows_two[4 * side + i] = [rows_two[4 * side + i][t] + gb[side, 2 + 2 * i + t] for t in range(2)]
    local[7].wait()
    shifted = [roll(rows_three[k], 2 * k + 1) for k in range(4)]
    solved = solve(window(lane8, shifted, lambda j: nothing8), f3[...])
    three = [solved[:, :128], solved[:, 128:]]
    local[8].wait()
    two = []
    for b in range(2):
        turned = [[roll(rows_two[2 * b + k][t], 2 * k + 1) for k in range(4)] for t in range(2)]

        def right_of(j, turned=turned):
            return only(lane8 == 2 * j - 1, turned[1][j - 1]) if j > 0 else nothing8

        def left_of(j, turned=turned):
            return only(lane8 == 2 * j, turned[0][j]) if j < 4 else nothing8

        left_tile = solve(window(lane8, turned[0], right_of), f2[b, 0])
        right_tile = solve(window(lane8, turned[1], left_of), f2[b, 1])
        for h in range(2):
            at = slice(128 * h, 128 * h + 128)
            two.append((left_tile[:, at], right_tile[:, at]))

    def moved(tile, c, shift, width):
        return roll(tile, (shift + 1 - width * 2 * c + 512 - width * core) % 128)

    def moved_two(row, c, shift):
        tile = row[c // 2]
        if c == 1:
            tile = jnp.where(lane8 == 0, row[1], row[0])
        if c == 2:
            tile = jnp.where(lane8 == 127, row[0], row[1])
        return moved(tile, c, shift, 32)

    for side in range(2):
        for c in range(4):
            ns[side, c] = jnp.where(lane8 < 64, moved_two(two[3 * side], c, 0), moved(three[side], c, 64, 16))

    def to_near(side, c, me):
        return send(
            ns.at[side, c], nb.at[1 - side, me], nsend.at[side, c], nrecv.at[1 - side, me],
            px=px + 2 * side - 1, py=2 * c + core,
        )

    for side, there in ((0, has_left), (1, has_right)):

        @pl.when(there)
        def _(side=side):
            for c in range(4):
                to_near(side, c, x).start()

    edge_copy(2, partner, partner).wait_recv()

    @pl.when(has_beside)
    def _():
        edge_copy(0, beside, beside).wait_recv()

    @pl.when(has_behind)
    def _():
        edge_copy(1, behind, behind).wait_recv()

    to_partner(1 - core).wait_recv()
    left_edge, first_edge, second_edge, right_edge = (eb[2 * x + i, 1] for i in range(4))
    even = (lane & 1) == 0

    def edges(n):
        mid = jnp.where(even, second_edge, roll(first_edge, -n))
        outer = jnp.where(even, right_edge, roll(left_edge, -n))
        halo = jnp.where(even, first_edge + roll(left_edge, -n), right_edge + roll(second_edge, -n))
        return mid, outer, halo

    edges_of = {2: edges(4), 3: edges(6)}
    rows_one = []
    for r in range(10):
        m, h = divmod(r, 2)
        if h == 0:
            main = jnp.where(lane < 64, xm[0, m], roll(xm[1, m], 64))
        else:
            main = jnp.where(lane < 64, roll(xm[0, m], 64), xm[1, m])
        at, last = edge_lanes(r)
        mid, outer, _ = edges_of[(last - at) // 2]
        main = main + only(jnp.logical_or(lane == 63, lane == 64), roll(mid, 63 - at))
        main = main + only(jnp.logical_or(lane == 127, lane == 0), roll(outer, 127 - at))
        rows_one.append(main)
    halo_two, halo_three = edges_of[2][2], edges_of[3][2]
    halos = jnp.where(
        lane < 4,
        roll(halo_two, -18),
        jnp.where(lane < 10, roll(halo_three, -46), jnp.where(lane < 16, roll(halo_three, -104), roll(halo_two, -66))),
    )
    one = []
    for b in range(4):
        local[12 + b].wait()
        turned = [roll(rows_one[2 * b + k], 2 * k + 1) for k in range(4)]
        side = roll(halos, -4 * b)
        solved = solve(window(lane, turned, lambda j, side=side: side), f1[b])
        one += [solved[:, :128], solved[:, 128:]]
    hs[0] = one[0]
    hs[1] = one[7]
    h_refs = (hs, hb, hsend, hrecv)
    start_rows(*h_refs)
    column = nothing
    for r in range(8):
        column = jnp.where(lane == r, roll(one[r], r + core), column)
    cs[...] = column

    def to_side(d):
        return send(cs, cb.at[1 - d], esend.at[1 - d], erecv.at[1 - d], px=px + d, py=beside)

    for d in (-1, 1, 0):

        @pl.when(diag[1 + d])
        def _(d=d):
            to_side(d).start()

    @pl.when(z > 0)
    def _():
        send(f4own, zb4.at[0], z4send.at[1], z4recv.at[0], px=px - 4, py=py).wait_recv()

    @pl.when(z < 7)
    def _():
        send(f4own, zb4.at[1], z4send.at[0], z4recv.at[1], px=px + 4, py=py).wait_recv()

    quads = (zb4[0, 1], zb4[0, 2] + f4own[0], f4own[1], f4own[2] + zb4[1, 0], zb4[1, 1])
    four = []
    for b in range(4):
        local[16 + b].wait()
        first, second = quads[b], quads[b + 1]
        v0 = jnp.where(
            lane8 <= 64,
            only(lane8 >= 1, roll(first, 1)),
            only(lane8 >= 67, roll(first, 3)),
        )
        v1 = jnp.where(
            lane8 <= 2,
            roll(first, 3),
            jnp.where(lane8 <= 68, only(lane8 >= 5, roll(second, 5)), only(lane8 >= 71, roll(second, 7))),
        )
        v2 = only(lane8 <= 6, roll(second, 7))
        four.append(solve(jnp.concatenate([v0, v1, v2[:, :8]], axis=1), f4[b]))

    for c in range(4):
        pieces = [moved_two(two[u], c, 42 * u) for u in range(3)]
        rs[c, 0] = jnp.where(lane8 < 42, pieces[0], jnp.where(lane8 < 84, pieces[1], pieces[2]))
        pieces = [moved(three[s], c, 32 * s + 32, 16) for s in range(2)]
        rs[c, 1] = jnp.where(lane8 < 84, jnp.where(lane8 < 64, pieces[0], pieces[1]), moved_two(two[3], c, 84))
        pieces = [moved(four[b], c, 10 * b, 8) for b in range(4)]
        low_lane = lane8 & 63
        rs[c, 2] = jnp.where(
            low_lane < 20,
            jnp.where(low_lane < 10, pieces[0], pieces[1]),
            jnp.where(low_lane < 30, pieces[2], pieces[3]),
        )
    rb[x] = rs[x]

    def to_chip(d, me):
        peer = (me + d) % 4
        return send(rs.at[peer], rb.at[me], rsend.at[d - 1], rrecv.at[me], px=px, py=2 * peer + core)

    for d in (2, 1, 3):
        begin(to_chip(d, x))

    for d in range(1, 8):
        to_z(d, (z + 8 - d) % 8).wait_recv()
    local[9].wait()
    down = [roll(zb5[i + 1], -32) if i < 8 else nothing8 for i in range(0, 10, 2)]
    rise = [nothing8] + [roll(zb5[i + 1], 32) for i in range(1, 8, 2)]
    flat = [
        jnp.where(lane8 < 96, down[j], down[j + 1]) + jnp.where(lane8 >= 32, rise[j + 1], rise[j]) for j in range(4)
    ]
    solved = solve(jnp.concatenate(flat, axis=1), ci[...])
    p5[0] = nothing8
    p5[5] = nothing8
    for j in range(4):
        p5[j + 1] = solved[:, 128 * j : 128 * j + 128]
    odd = z % 2
    lead = (z + odd) // 2
    edge = 32 + 64 * odd
    rb5[x] = jnp.where(lane8 < edge, roll(p5[lead], edge), roll(p5[lead + 1], edge))

    def to_chip5(d, me):
        peer = (me + d) % 4
        return send(rb5.at[me], rb5.at[me], r5send.at[d - 1], r5recv.at[me], px=px, py=2 * peer + core)

    for d in (2, 1, 3):
        begin(to_chip5(d, x))

    before, after = eb[py, 0], eb[py + 2, 0]
    corner_before, corner_after = eb[py, 1], eb[py + 2, 1]
    facing = jnp.where(even, before, after)
    corners = jnp.where(even, corner_before, corner_after)
    halos = jnp.where(
        lane < 2,
        roll(corners, -26),
        jnp.where(lane < 18, roll(facing, -46), jnp.where(lane < 34, roll(facing, -94), roll(corners, 6))),
    )
    local[10].wait()
    for b in range(8):
        tiles = []
        for k in range(4):
            at = 2 * b + k
            tile = pb[0, 2] if at == 0 else pb[1, 2] if at == 17 else xt[at - 1]
            tiles.append(roll(tile, 2 * k + 1))
        side = roll(halos, -4 * b)
        solved = solve(window(lane, tiles, lambda j, side=side: side), ff[b, 0])
        p0[2 * b] = solved[:, :128]
        p0[2 * b + 1] = solved[:, 128:]

    got_rows(*h_refs)
    for d in (-1, 0, 1):

        @pl.when(diag[1 + d])
        def _(d=d):
            send(cs, cb.at[1 + d], esend.at[1 + d], erecv.at[1 + d], px=px + d, py=beside).wait_recv()

    local[6].wait()
    local[11].wait()
    one = [hb[0]] + one + [hb[1]]
    at_lane = 127 * (1 - core)
    for r in range(10):
        source, from_lane = (0, 7) if r == 0 else (2, 0) if r == 9 else (1, r - 1)
        one[r] = jnp.where(lane == at_lane, roll(cb[source], (at_lane - from_lane + 128) % 128), one[r])
    one = lifted(one, up[0:128, :])
    for d in range(1, 4):
        to_chip(d, (x + 4 - d) % 4).wait_recv()
    for side, there in ((0, has_left), (1, has_right)):

        @pl.when(there)
        def _(side=side):
            for c in range(4):
                to_near(1 - side, x, c).wait_recv()

    back = [rb[:, t].reshape(32, 128) for t in range(3)]
    outer = [nb[side].reshape(32, 128) for side in range(2)]

    def slot(tile, first, count):
        return only(jnp.logical_and(lane >= first, lane < first + count), tile)

    two = [slot(outer[0], 0, 34)] + [slot(back[0], 42 * u, 34) for u in range(3)]
    two += [slot(back[1], 84, 34), slot(outer[1], 0, 34)]
    three = [slot(outer[0], 64, 18), slot(back[1], 32, 18), slot(back[1], 64, 18), slot(outer[1], 64, 18)]
    four = [
        only(jnp.logical_and(lane >= 64 * h + 10 * b, lane < 64 * h + 10 * b + 10), back[2])
        for b in range(4)
        for h in range(2)
    ]
    two = lifted(two, near[0:128, :])
    three = lifted(three, near[128:256, :])
    four = lifted(four, near[256:384, :])
    local[5].wait()
    terms = one + two + three + four
    for f in range(16):
        total = p0[f]
        for r in range(28):
            if up_used[r][f]:
                total = total + uw[r // 8, 16 * (r % 8) + f] * terms[r]
        acc[f] = total

    for d in range(1, 4):
        to_chip5(d, (x + 4 - d) % 4).wait_recv()
    five = rb5[...].reshape(32, 128)
    full = jnp.concatenate([only((lane // 32) == s, five) for s in range(4)], axis=0)
    top = full.astype(BF)
    rest = (full - top.astype(F32)).astype(BF)
    product = jnp.dot(jnp.concatenate([top, rest], axis=0), up[128:256, :], preferred_element_type=F32)
    product = product[:128] + product[128:] + jnp.dot(top, up[256:384, :], preferred_element_type=F32)
    for f in range(16):
        total = acc[f]
        for s in range(4):
            if up_used[28 + s][f]:
                total = total + uw[3, 16 * (4 + s) + f] * product[32 * s : 32 * s + 32]
        out_ref[pl.ds(f, 32, stride=16), :] = total

    for copy in sent:
        copy.wait_send()
    for refs in (b_refs, g_refs, h_refs):
        sent_rows(*refs)

    for side, there in ((0, has_left), (1, has_right)):

        @pl.when(there)
        def _(side=side):
            for c in range(4):
                to_near(side, c, x).wait_send()

    @pl.when(has_beside)
    def _():
        edge_copy(0, py, beside).wait_send()
        edge_copy(1, py, beyond).wait_send()

    @pl.when(z > 0)
    def _():
        z4_down().wait_send()

    @pl.when(z < 7)
    def _():
        z4_up().wait_send()

    for d in (-1, 0, 1):

        @pl.when(diag[1 + d])
        def _(d=d):
            to_side(d).wait_send()


def per_device(residual, fine, one, two, three, four, inverse):
    weights, down_b, up, near, down_used, up_used = tables()

    def tiles(*lead):
        return pltpu.VMEM(lead + (32, 128), F32)

    def small(*lead):
        return pltpu.VMEM(lead + (8, 128), F32)

    dma = pltpu.SemaphoreType.DMA
    out = pl.pallas_call(
        functools.partial(kernel, down_used, up_used),
        out_shape=jax.ShapeDtypeStruct((512, 128), F32),
        in_specs=[pl.BlockSpec(memory_space=pltpu.HBM)] * 11,
        out_specs=pl.BlockSpec(memory_space=pltpu.VMEM),
        scratch_shapes=[
            pltpu.VMEM((512, 128), F32),
            pltpu.VMEM((8, 1, 520, 256), BF),
            pltpu.VMEM((4, 520, 256), BF),
            pltpu.VMEM((2, 2, 520, 256), BF),
            pltpu.VMEM((520, 256), BF),
            pltpu.VMEM((4, 264, 128), BF),
            pltpu.VMEM((512, 512), BF),
            pltpu.VMEM((144, 128), F32),
            pltpu.SMEM((8, 128), F32),
            pltpu.VMEM((256, 512), BF),
            pltpu.VMEM((128, 128), BF),
            pltpu.VMEM((384, 128), BF),
            pltpu.VMEM((384, 128), BF),
            tiles(16),
            pltpu.VMEM((512, 512), F32),
            tiles(8),
            tiles(2, 3),
            tiles(2, 3),
            tiles(10, 2),
            tiles(2, 5),
            tiles(2),
            tiles(2),
            tiles(),
            tiles(3),
            tiles(16),
            tiles(16),
            small(4, 3),
            small(8),
            small(8, 3),
            small(4),
            small(4, 3),
            small(10),
            small(3),
            small(2, 3),
            small(2, 6),
            small(2, 6),
            small(2, 4),
            small(2, 4),
            small(4, 3),
            small(4, 3),
            small(4),
            small(6),
            dma((20,)),
        ]
        + [
            dma if n == 0 else dma(n if isinstance(n, tuple) else (n,))
            for n in (7, 8, 7, 8, 2, 2, 3, 8, 0, 0, 3, 4, 3, 4, 7, 8, 2, 2, 2, 2, 3, 3, 2, 2, (2, 4), (2, 4), 3, 4, 3, 4)
        ]
        + [pltpu.SemaphoreType.REGULAR((3,))],
        compiler_params=pltpu.CompilerParams(
            collective_id=0, has_side_effects=True, vmem_limit_bytes=56147968
        ),
    )(
        residual.reshape(512, 128), fine, one, two, three, four, inverse,
        jnp.asarray(weights), jnp.asarray(down_b), jnp.asarray(up), jnp.asarray(near),
    )
    return out.reshape(32, 16, 128)


def solution(mesh):
    placed = (
        P(None, "px", "py"),
        P("px", "py", None, None),
        P("px", None, None, None),
        P("px", None, None, None),
        P("px", None, None, None),
        P(),
        P(),
    )
    return jax.shard_map(
        per_device, mesh=mesh, in_specs=placed, out_specs=P(None, "px", "py"), check_vma=False
    )
```
